32 devices in a mesh: row: 8 (over z, core), col: 4 (over y, x).
Axes of the slice: x: 2, y: 2, z: 4, core: 2. Of those that a mesh axis runs over, the one named last changes fastest.
Arguments:
- running_cost: float32 [2048, 2048], P('row', 'col'), may hold values from 0.5 to 7.5, as said below
- control_x: float32 [2048, 2048], P('row', 'col'), may hold values from -6 to 6
- control_y: float32 [2048, 2048], P('row', 'col'), may hold values from -6 to 6
- prior_density: float32 [2048, 2048], P('row', 'col'), may hold values from 0.5 to 2
Outputs:
- value_field: float32 [2048, 2048], P('row', 'col')
- density: float32 [2048, 2048], P('row', 'col')
- ergodic: float32 [], replicated
The draws below stay inside these ranges and needn't reach their ends.
Inputs may be any that keep to these rules, and one draw needn't show every extreme that they name: `running_cost`: strictly positive.
All inputs are finite; a program needn't handle non-finite values.
Results may differ from the reference program's by a relative error of at most 0.0003.
Values sent between devices are 32-bit elements; how exact they have to be, the bound alone decides.
No kernel may reach another device: no remote copies, remote signals or barrier semaphores. Data moves between devices by JAX's collectives and lax.ppermute only.
A program may use at most 64 MiB of HBM per device.

```python
import jax
import jax.numpy as jnp

ITERS = 3
NX = 2048
NY = 2048


def draw_running_cost(key, part):
    rows = jnp.arange(NX, dtype=jnp.float32)
    ramp = 1.0 + 2.0 * rows / (NX - 1.0)
    rough = jax.random.uniform(key, (NX, NY), jnp.float32, 0.5, 1.5)
    return (ramp[:, None] * rough).astype(jnp.float32)


def shard_levels(key, shape, split, smallest, largest):
    gain, own = 1.0, jax.random.fold_in(key, 6)
    for position, blocks in split:
        draws = jnp.exp(jax.random.uniform(jax.random.fold_in(own, position), (blocks,), jnp.float32, smallest / len(split), largest / len(split)))
        gain = gain * jnp.repeat(draws, shape[position] // blocks).reshape([-1 if axis == position else 1 for axis in range(len(shape))])
    return gain


def scatter_about(stream_key, extent, spread, reach, cuts=(), held_as=jnp.bfloat16):
    entries = jax.random.normal(stream_key, extent, jnp.float32) * spread
    if len(cuts) > 0:
        entries = shard_levels(stream_key, extent, cuts, -0.22, 0.18) * entries
    return jnp.clip(entries, min=-reach, max=reach).astype(held_as)


def setup_inputs(seed: int = 0) -> dict:
    key_list = jax.random.split(jax.random.key(seed), 5)
    running_cost = draw_running_cost(jax.random.fold_in(key_list[4], 71), 0)
    control_x = scatter_about(key_list[1], (NX, NY), 1.0, 6.0, ((0, 8), (1, 4)), jnp.float32)
    control_y = scatter_about(key_list[2], (NX, NY), 1.0, 6.0, ((0, 8), (1, 4)), jnp.float32)
    prior_density = jnp.clip(0.5 + 1.5 * jax.random.uniform(key_list[3], (NX, NY), jnp.float32) ** shard_levels(key_list[3], (NX, NY), ((0, 8), (1, 4)), -0.2, 0.2), 0.5, 2.0)
    return dict(running_cost=running_cost, control_x=control_x, control_y=control_y, prior_density=prior_density)


discount_rate = 0.05
diffusion = 0.25


def interior(padded):
    return padded[1:-1, 1:-1]


def neighbours(padded):
    return (padded[2:, 1:-1], padded[:-2, 1:-1], padded[1:-1, 2:], padded[1:-1, :-2])


def coefficients(conduct, padded_conduct, zeroth):
    weights = tuple(diffusion * 0.5 * (conduct + outside) for outside in neighbours(padded_conduct))
    center = zeroth + ((weights[0] + weights[1]) + (weights[2] + weights[3]))
    return (center,) + weights


def operator_apply(padded, coeffs):
    beside = neighbours(padded)
    inflow = (coeffs[1] * beside[0] + coeffs[2] * beside[1]) + (coeffs[3] * beside[2] + coeffs[4] * beside[3])
    return coeffs[0] * interior(padded) - inflow


def conjugate(coeffs, forcing):
    solution = jnp.zeros_like(forcing)
    residual = forcing
    direction = forcing
    norm_now = jnp.sum(residual * residual)
    for iteration in range(ITERS):
        applied = operator_apply(jnp.pad(direction, 1), coeffs)
        step_size = norm_now / jnp.sum(direction * applied)
        solution = solution + step_size * direction
        residual = residual - step_size * applied
        norm_next = jnp.sum(residual * residual)
        direction = residual + (norm_next / norm_now) * direction
        norm_now = norm_next
    return solution


def reference(running_cost, control_x, control_y, prior_density):
    control_cost = 0.5 * (control_x * control_x + control_y * control_y)
    conduct = 1.0 + control_cost
    padded_conduct = jnp.pad(conduct, 1)
    bellman = coefficients(conduct, padded_conduct, discount_rate)
    value_field = conjugate(bellman, running_cost + control_cost)
    padded_value = jnp.pad(value_field, 1)
    beside = neighbours(padded_value)
    slope_row = 0.5 * (beside[0] - beside[1])
    slope_col = 0.5 * (beside[2] - beside[3])
    congestion = (slope_row * slope_row + slope_col * slope_col) / (2.0 * diffusion)
    planck = coefficients(conduct, padded_conduct, discount_rate + congestion)
    density = conjugate(planck, prior_density)
    weighted = jnp.sum(prior_density * (running_cost + control_cost - discount_rate * value_field))
    ergodic = weighted / jnp.sum(prior_density)
    return value_field, density, ergodic
```

```python
import functools

import jax
import jax.numpy as jnp
from jax import lax
from jax.experimental import pallas as pl
from jax.experimental.pallas import tpu as pltpu
from jax.sharding import PartitionSpec as P

discount_rate = 0.05
diffusion = 0.25
SCALE = 0.0625
FACE = diffusion * 0.5 * SCALE
LANES = 128
SUB = 8
WIDE = 7
PAD = 2 * SUB
VMEM_BYTES = 16 * 2**20
VM = pl.BlockSpec(memory_space=pltpu.VMEM)
BOTH = ("row", "col")


def two_sum(a, b):
    s = a + b
    t = s - a
    return s, (a - (s - t)) + (b - t)


def fast_sum(a, b):
    s = a + b
    return s, b - (s - a)


def halves(a):
    t = a * 4097.0
    hi = t - (t - a)
    return hi, a - hi


def two_prod(a, b):
    p = a * b
    ah, al = halves(a)
    bh, bl = halves(b)
    return p, ((ah * bh - p) + ah * bl + al * bh) + al * bl


def dmul(a, b):
    p, e = two_prod(a[0], b[0])
    return fast_sum(p, e + (a[0] * b[1] + a[1] * b[0]))


def dsub(a, b):
    s, e = two_sum(a[0], -b[0])
    return fast_sum(s, e + (a[1] - b[1]))


def ddiv(a, b):
    q = a[0] / b[0]
    r = dsub(a, dmul((q, jnp.zeros_like(q)), b))
    return fast_sum(q, r[0] / b[0])


def galerkin(dots):
    d00, d01, d02, d03, d11, d12, d13, d22, d23 = dots
    zero = jnp.zeros_like(d00[0])
    l1 = ddiv(d11, d01)
    l2 = ddiv(d12, d01)
    s11 = dsub(d12, dmul(l1, d02))
    s12 = dsub(d13, dmul(l1, d03))
    s21 = dsub(d22, dmul(l2, d02))
    s22 = dsub(d23, dmul(l2, d03))
    g0 = (d00[0] * SCALE, d00[1] * SCALE)
    g1 = dsub((d01[0] * SCALE, d01[1] * SCALE), dmul(l1, g0))
    g2 = dsub((d02[0] * SCALE, d02[1] * SCALE), dmul(l2, g0))
    l3 = ddiv(s21, s11)
    t22 = dsub(s22, dmul(l3, s12))
    g2 = dsub(g2, dmul(l3, g1))
    full1 = s11[0] > 1e-12 * d12[0]
    full2 = full1 & (t22[0] > 1e-12 * d23[0])
    c2 = jnp.where(full2, ddiv(g2, t22)[0], zero)
    c1 = ddiv(dsub(g1, dmul(s12, (c2, zero))), s11)[0]
    c1 = jnp.where(full1, c1, zero)
    r0 = dsub(dsub(g0, dmul(d02, (c1, zero))), dmul(d03, (c2, zero)))
    return ddiv(r0, d01)[0], c1, c2


PAIRS = ((0, 0), (0, 1), (0, 2), (0, 3), (1, 1), (1, 2), (1, 3), (2, 2), (2, 3))


def split_short(a):
    t = a * 65537.0
    hi = t - (t - a)
    return hi, a - hi


def dot_step(groups, sums):
    parts = [[split_short(v) for v in vs] for vs in groups]
    out = []
    for k, (i, j) in enumerate(PAIRS):
        main = None
        rest = None
        for vs, ps in zip(groups, parts):
            m = ps[i][0] * ps[j][0]
            if i == j:
                r = ps[i][1] * (vs[i] + ps[i][0])
            else:
                r = ps[i][0] * ps[j][1] + ps[i][1] * vs[j]
            main = m if main is None else main + m
            rest = r if rest is None else rest + r
        s, e = two_sum(sums[2 * k], main)
        out += [s, sums[2 * k + 1] + (e + rest)]
    return tuple(out)


def pack_sums(sums, extra=()):
    lane = lax.broadcasted_iota(jnp.int32, (1, LANES), 1)
    row = jnp.zeros((1, LANES), jnp.float32)
    total = lambda a: jnp.sum(jnp.sum(a, axis=0, keepdims=True), axis=1, keepdims=True)
    for k in range(len(PAIRS)):
        s, e = sums[2 * k], sums[2 * k + 1]
        peak = jnp.max(jnp.max(jnp.abs(s), axis=0, keepdims=True), axis=1, keepdims=True)
        lift = jnp.broadcast_to(peak * 2048.0, s.shape)
        main = (s + lift) - lift
        row = jnp.where(lane == k, total(main), row)
        row = jnp.where(lane == 64 + k, total((s - main) + e), row)
    for k, a in enumerate(extra):
        row = jnp.where(lane == len(PAIRS) + k, total(a), row)
    return row


def gathered_sums(ref, extra=0):
    rows = [(ref[d], None) for d in range(ref.shape[0])]
    while len(rows) > 1:
        merged = []
        for k in range(0, len(rows) - 1, 2):
            (a, ea), (b, eb) = rows[k], rows[k + 1]
            s, e = two_sum(a, b)
            e = e if ea is None else e + (ea + eb)
            merged.append((s, e))
        if len(rows) % 2:
            a, ea = rows[-1]
            merged.append((a, jnp.zeros_like(a) if ea is None else ea))
        rows = merged
    s, e = rows[0]
    lane = lax.broadcasted_iota(jnp.int32, s.shape, 1)
    pick = lambda a, k: jnp.sum(jnp.where(lane == k, a, 0.0), axis=1, keepdims=True)
    dots = []
    for k in range(len(PAIRS)):
        hi = pick(s, k)
        lo = pick(e, k) + pick(s, 64 + k)
        dots.append(fast_sum(hi, lo))
    return dots, [pick(s, len(PAIRS) + k) for k in range(extra)]


def fields_of(rc, cx, cy):
    control_cost = 0.5 * (cx * cx + cy * cy)
    return rc + control_cost, 1.0 + control_cost


def edge_rows_kernel(*refs):
    first, last, (up_ref, down_ref) = refs[:4], refs[4:8], refs[8:]
    for (rc, cx, cy, pd), out in ((first, up_ref), (last, down_ref)):
        forcing, conduct = fields_of(rc[...], cx[...], cy[...])
        out[0:SUB] = forcing
        out[SUB : 2 * SUB] = conduct
        out[2 * SUB :] = pd[...]


def fields_kernel(rc_ref, cx_ref, cy_ref, pd_ref, f_ref, c_ref, p_ref):
    i = pl.program_id(0)
    rows = rc_ref.shape[0]
    base = pl.multiple_of(i * rows, SUB)
    for j in range(f_ref.shape[0]):
        cols = slice(j * LANES, (j + 1) * LANES)
        forcing, conduct = fields_of(rc_ref[:, cols], cx_ref[:, cols], cy_ref[:, cols])
        f_ref[j, pl.ds(base, rows), :] = forcing
        c_ref[j, pl.ds(base, rows), :] = conduct
        p_ref[j, pl.ds(base, rows), :] = pd_ref[:, cols]


def row_tile(own_ref, north_ref, south_ref, field, j, t):
    tiles = own_ref.shape[1] // SUB + 2
    cols = slice(j * LANES, (j + 1) * LANES)
    if t == 0:
        return north_ref[field * SUB : (field + 1) * SUB, cols]
    if t == tiles - 1:
        return south_ref[field * SUB : (field + 1) * SUB, cols]
    return own_ref[j, (t - 1) * SUB : t * SUB, :]


def packing(tiles):
    per = LANES // WIDE
    return per, -(-tiles // per)


def pack_columns_kernel(f_ref, c_ref, p_ref, north_ref, south_ref, west_ref, east_ref):
    tiles = f_ref.shape[1] // SUB + 2
    per, groups = packing(tiles)
    lane = lax.broadcasted_iota(jnp.int32, (SUB, LANES), 1)
    last = f_ref.shape[0] - 1
    for field, own in enumerate((f_ref, c_ref, p_ref)):
        for v in range(groups):
            west = jnp.zeros((SUB, LANES), jnp.float32)
            east = west
            for g in range(min(per, tiles - v * per)):
                here = (lane >= WIDE * g) & (lane < WIDE * (g + 1))
                a = row_tile(own, north_ref, south_ref, field, 0, v * per + g)
                b = row_tile(own, north_ref, south_ref, field, last, v * per + g)
                west = jnp.where(here, pltpu.roll(a, (WIDE * g) % LANES, 1), west)
                east = jnp.where(here, pltpu.roll(b, (WIDE * (g + 1)) % LANES, 1), east)
            at = (field * groups + v) * SUB
            west_ref[at : at + SUB] = west
            east_ref[at : at + SUB] = east


def fill(refs, owns, north_ref, south_ref, west_ref, east_ref):
    last = refs[0].shape[0] - 1
    rows = refs[0].shape[1]
    tiles = (rows - 2 * PAD) // SUB + 2
    per, groups = packing(tiles)
    lane = lax.broadcasted_iota(jnp.int32, (SUB, LANES), 1)
    zero = jnp.zeros((SUB, LANES), jnp.float32)
    for field, ref in enumerate(refs):
        mine = slice(field * SUB, (field + 1) * SUB)
        for j in range(last + 1):
            ref[j, 0:SUB] = zero
            ref[j, rows - SUB : rows] = zero
        for j in range(last):
            cols = slice(j * LANES, (j + 1) * LANES)
            ref[j, SUB : 2 * SUB] = north_ref[mine, cols]
            ref[j, rows - 2 * SUB : rows - SUB] = south_ref[mine, cols]
            ref[j, PAD : rows - PAD] = owns[field][j]
        for t in range(tiles):
            v, g = divmod(t, per)
            at = (field * groups + v) * SUB
            west = pltpu.roll(west_ref[at : at + SUB], (-WIDE * (g + 1)) % LANES, 1)
            east = pltpu.roll(east_ref[at : at + SUB], (-WIDE * g) % LANES, 1)
            tile = jnp.where(lane < WIDE, east, jnp.where(lane >= LANES - WIDE, west, 0.0))
            ref[last, SUB + t * SUB : 2 * SUB + t * SUB] = tile


def beside(ref, r, count):
    lane = lax.broadcasted_iota(jnp.int32, (SUB, LANES), 1)
    here = [ref[j, pl.ds(r, SUB), :] for j in range(count)]
    south = [ref[j, pl.ds(r + 1, SUB), :] for j in range(count)]
    north = [ref[j, pl.ds(r - 1, SUB), :] for j in range(count)]
    left = [pltpu.roll(a, LANES - 1, 1) for a in here]
    right = [pltpu.roll(a, 1, 1) for a in here]
    east = [jnp.where(lane == LANES - 1, left[(j + 1) % count], left[j]) for j in range(count)]
    west = [jnp.where(lane == 0, right[(j - 1) % count], right[j]) for j in range(count)]
    return here, south, north, east, west


def weighted_apply(center, w, cells):
    here, south, north, east, west = cells
    return center * here - ((w[0] * south + w[1] * north) + (w[2] * east + w[3] * west))


def apply_tiles(ref, w_ref, center_ref, r, count):
    cells = beside(ref, r, count)
    at = pl.ds(r, SUB)
    out = []
    for j in range(count):
        w = [w_ref[k, j, at, :] for k in range(4)]
        out.append(weighted_apply(center_ref[j, at, :], w, [c[j] for c in cells]))
    return out, cells[0]


def clear_pads(refs):
    zero = jnp.zeros((SUB, LANES), jnp.float32)
    for ref in refs:
        rows = ref.shape[1]
        for j in range(ref.shape[0]):
            ref[j, 0:SUB] = zero
            ref[j, rows - SUB : rows] = zero


def row_tiles(ref):
    return (ref.shape[1] - 2 * SUB) // SUB


def krylov(v0_ref, v1_ref, v2_ref, w_ref, center_ref):
    count, tiles = v0_ref.shape[0], row_tiles(v0_ref)
    own = count - 1

    def second(t, _):
        r = pl.multiple_of(SUB + t * SUB, SUB)
        out, _h = apply_tiles(v1_ref, w_ref, center_ref, r, count)
        for j in range(count):
            v2_ref[j, pl.ds(r, SUB), :] = out[j]
        return 0

    lax.fori_loop(0, tiles, second, 0)

    def third(t, sums):
        groups = []
        for u in range(2):
            r = pl.multiple_of(PAD + (2 * t + u) * SUB, SUB)
            out, here = apply_tiles(v2_ref, w_ref, center_ref, r, count)
            at = pl.ds(r, SUB)
            for j in range(own):
                groups.append((v0_ref[j, at, :], v1_ref[j, at, :], here[j], out[j]))
        return dot_step(groups, sums)

    zero = jnp.zeros((SUB, LANES), jnp.float32)
    return lax.fori_loop(0, (tiles - 2) // 2, third, (zero,) * (2 * len(PAIRS)))


def value_kernel(f_in, c_in, p_in, north_ref, south_ref, west_ref, east_ref,
                 f_ref, c_ref, p_ref, v1_ref, v2_ref, w_ref, faces_ref, row_ref, center_ref):
    fill((f_ref, c_ref, p_ref), (f_in, c_in, p_in), north_ref, south_ref, west_ref, east_ref)
    clear_pads((v1_ref, v2_ref))
    count, tiles = f_ref.shape[0], row_tiles(f_ref)

    def first(t, _):
        r = pl.multiple_of(SUB + t * SUB, SUB)
        at = pl.ds(r, SUB)
        cond = beside(c_ref, r, count)
        cells = beside(f_ref, r, count)
        for j in range(count):
            c = cond[0][j]
            inside = jnp.minimum(c, 1.0)
            face = inside * FACE
            w = [face * (c + cond[k][j]) for k in (1, 2, 3, 4)]
            faces = (w[0] + w[1]) + (w[2] + w[3])
            center = inside * (discount_rate * SCALE) + faces
            for k in range(4):
                w_ref[k, j, at, :] = w[k]
            faces_ref[j, at, :] = faces
            center_ref[j, at, :] = center
            v1_ref[j, at, :] = weighted_apply(center, w, [x[j] for x in cells])
        return 0

    lax.fori_loop(0, tiles, first, 0)
    sums = krylov(f_ref, v1_ref, v2_ref, w_ref, center_ref)
    row_ref[...] = jnp.broadcast_to(pack_sums(sums)[None], row_ref.shape)


def density_kernel(rows_ref, f_ref, c_ref, p_ref, v1_ref, v2_ref, w_ref, faces_ref,
                   value_ref, u1_ref, u2_ref, row_ref, vx_ref, center_ref):
    dots, _unused = gathered_sums(rows_ref)
    c0, c1, c2 = [jnp.broadcast_to(c, (SUB, LANES)) for c in galerkin(dots)]
    count, tiles = f_ref.shape[0], row_tiles(f_ref)
    own = count - 1
    clear_pads((vx_ref, u1_ref, u2_ref))

    def value(t, _):
        at = pl.ds(pl.multiple_of(SUB + t * SUB, SUB), SUB)
        for j in range(count):
            vx_ref[j, at, :] = (c0 * f_ref[j, at, :] + c1 * v1_ref[j, at, :]) + c2 * v2_ref[j, at, :]
        return 0

    lax.fori_loop(0, tiles, value, 0)

    def first(t, _):
        r = pl.multiple_of(SUB + t * SUB, SUB)
        at = pl.ds(r, SUB)
        val = beside(vx_ref, r, count)
        cells = beside(p_ref, r, count)
        for j in range(count):
            inside = jnp.minimum(c_ref[j, at, :], 1.0)
            slope_row = 0.5 * (val[1][j] - val[2][j])
            slope_col = 0.5 * (val[3][j] - val[4][j])
            congestion = (slope_row * slope_row + slope_col * slope_col) * (0.5 / diffusion)
            zeroth = (discount_rate + congestion) * SCALE
            center = inside * zeroth + faces_ref[j, at, :]
            center_ref[j, at, :] = center
            w = [w_ref[k, j, at, :] for k in range(4)]
            u1_ref[j, at, :] = weighted_apply(center, w, [x[j] for x in cells])
        return 0

    lax.fori_loop(0, tiles, first, 0)

    def outer(t, sums):
        r = pl.multiple_of(PAD + t * SUB, SUB)
        at = pl.ds(r, SUB)
        to = pl.ds(pl.multiple_of(t * SUB, SUB), SUB)
        cost, weight = sums
        for j in range(own):
            v = vx_ref[j, at, :]
            p = p_ref[j, at, :]
            value_ref[to, j * LANES : (j + 1) * LANES] = v
            cost = cost + p * (f_ref[j, at, :] - discount_rate * v)
            weight = weight + p
        return cost, weight

    zero = jnp.zeros((SUB, LANES), jnp.float32)
    extra = lax.fori_loop(0, tiles - 2, outer, (zero, zero))
    sums = krylov(p_ref, u1_ref, u2_ref, w_ref, center_ref)
    row_ref[...] = jnp.broadcast_to(pack_sums(sums, extra)[None], row_ref.shape)


def finish_kernel(rows_ref, p_ref, u1_ref, u2_ref, density_ref, ergodic_ref):
    dots, (cost, weight) = gathered_sums(rows_ref, 2)
    ergodic_ref[...] = cost / weight
    c0, c1, c2 = [jnp.broadcast_to(c, (SUB, LANES)) for c in galerkin(dots)]
    own = p_ref.shape[0] - 1

    def tile(t, _):
        at = pl.ds(pl.multiple_of(PAD + t * SUB, SUB), SUB)
        to = pl.ds(pl.multiple_of(t * SUB, SUB), SUB)
        for j in range(own):
            density_ref[to, j * LANES : (j + 1) * LANES] = (
                c0 * p_ref[j, at, :] + c1 * u1_ref[j, at, :]
            ) + c2 * u2_ref[j, at, :]
        return 0

    lax.fori_loop(0, density_ref.shape[0] // SUB, tile, 0)


def f32(*shape):
    return jax.ShapeDtypeStruct(shape, jnp.float32)


def exchange(back, ahead, axis):
    count = lax.axis_size(axis)
    ends = count - 1
    after = lax.ppermute(back, axis, [(i + 1, i) for i in range(ends)])
    before = lax.ppermute(ahead, axis, [(i, i + 1) for i in range(ends)])
    return before, after


def everyone(row):
    return lax.all_to_all(row, BOTH, 0, 0, tiled=True)


def body(*args):
    rows, cols = args[0].shape
    devices = lax.axis_size("row") * lax.axis_size("col")
    count = cols // LANES + 1
    ext = (count, rows + 2 * PAD, LANES)
    tiles = rows // SUB + 2
    _per, groups = packing(tiles)
    top = pl.BlockSpec((SUB, cols), lambda i: (0, 0))
    end = pl.BlockSpec((SUB, cols), lambda i: (rows // SUB - 1, 0))
    small = pltpu.CompilerParams(vmem_limit_bytes=VMEM_BYTES)
    up, down = pl.pallas_call(
        edge_rows_kernel,
        grid=(1,),
        in_specs=[top] * 4 + [end] * 4,
        out_specs=[pl.BlockSpec((3 * SUB, cols), lambda i: (0, 0))] * 2,
        out_shape=[f32(3 * SUB, cols)] * 2,
        compiler_params=small,
    )(*args, *args)
    north, south = exchange(up, down, "row")
    step = min(rows, 64)
    fields = pl.pallas_call(
        fields_kernel,
        grid=(rows // step,),
        in_specs=[pl.BlockSpec((step, cols), lambda i: (i, 0))] * 4,
        out_specs=[VM] * 3,
        out_shape=[f32(count - 1, rows, LANES)] * 3,
        cost_estimate=pl.CostEstimate(flops=10**6, bytes_accessed=4 * 10**6, transcendentals=0),
        compiler_params=small,
    )(*args)
    west, east = pl.pallas_call(
        pack_columns_kernel,
        in_specs=[VM] * 5,
        out_specs=[VM] * 2,
        out_shape=[f32(3 * groups * SUB, LANES)] * 2,
        compiler_params=small,
    )(*fields, north, south)
    west, east = exchange(west, east, "col")
    f, c, p, v1, v2, w, faces, row = pl.pallas_call(
        value_kernel,
        in_specs=[VM] * 7,
        out_specs=[VM] * 8,
        out_shape=[f32(*ext)] * 5 + [f32(4, *ext), f32(*ext), f32(devices, 1, LANES)],
        scratch_shapes=[pltpu.VMEM(ext, jnp.float32)],
        compiler_params=small,
    )(*fields, north, south, west, east)
    value, u1, u2, row = pl.pallas_call(
        density_kernel,
        in_specs=[VM] * 8,
        out_specs=[VM] * 4,
        out_shape=[f32(rows, cols), f32(*ext), f32(*ext), f32(devices, 1, LANES)],
        scratch_shapes=[pltpu.VMEM(ext, jnp.float32)] * 2,
        compiler_params=small,
    )(everyone(row), f, c, p, v1, v2, w, faces)
    density, ergodic = pl.pallas_call(
        finish_kernel,
        in_specs=[VM] * 4,
        out_specs=[VM] * 2,
        out_shape=[f32(rows, cols), f32(1, 1)],
        compiler_params=small,
    )(everyone(row), p, u1, u2)
    return value, density, ergodic[0, 0]


def solution(mesh):
    spec = P("row", "col")
    return jax.shard_map(body, mesh=mesh, in_specs=(spec,) * 4, out_specs=(spec, spec, P()), check_vma=False)
```

```python
import functools

import jax
import jax.numpy as jnp
from jax import lax
from jax.experimental import pallas as pl
from jax.experimental.pallas import tpu as pltpu
from jax.sharding import PartitionSpec as P

discount_rate = 0.05
diffusion = 0.25
SCALE = 0.0625
FACE = diffusion * 0.5 * SCALE
LANES = 128
SUB = 8
WIDE = 7
DEEP = 3
PAD = 2 * SUB
VMEM_BYTES = 16 * 2**20
VM = pl.BlockSpec(memory_space=pltpu.VMEM)
BOTH = ("row", "col")


def two_sum(a, b):
    s = a + b
    t = s - a
    return s, (a - (s - t)) + (b - t)


def fast_sum(a, b):
    s = a + b
    return s, b - (s - a)


def halves(a):
    t = a * 4097.0
    hi = t - (t - a)
    return hi, a - hi


def two_prod(a, b):
    p = a * b
    ah, al = halves(a)
    bh, bl = halves(b)
    return p, ((ah * bh - p) + ah * bl + al * bh) + al * bl


def dmul(a, b):
    p, e = two_prod(a[0], b[0])
    return fast_sum(p, e + (a[0] * b[1] + a[1] * b[0]))


def dsub(a, b):
    s, e = two_sum(a[0], -b[0])
    return fast_sum(s, e + (a[1] - b[1]))


def ddiv(a, b):
    q = a[0] / b[0]
    r = dsub(a, dmul((q, jnp.zeros_like(q)), b))
    return fast_sum(q, r[0] / b[0])


def galerkin(dots):
    d00, d01, d02, d03, d11, d12, d13, d22, d23 = dots
    zero = jnp.zeros_like(d00[0])
    l1 = ddiv(d11, d01)
    l2 = ddiv(d12, d01)
    s11 = dsub(d12, dmul(l1, d02))
    s12 = dsub(d13, dmul(l1, d03))
    s21 = dsub(d22, dmul(l2, d02))
    s22 = dsub(d23, dmul(l2, d03))
    g0 = (d00[0] * SCALE, d00[1] * SCALE)
    g1 = dsub((d01[0] * SCALE, d01[1] * SCALE), dmul(l1, g0))
    g2 = dsub((d02[0] * SCALE, d02[1] * SCALE), dmul(l2, g0))
    l3 = ddiv(s21, s11)
    t22 = dsub(s22, dmul(l3, s12))
    g2 = dsub(g2, dmul(l3, g1))
    full1 = s11[0] > 1e-12 * d12[0]
    full2 = full1 & (t22[0] > 1e-12 * d23[0])
    c2 = jnp.where(full2, ddiv(g2, t22)[0], zero)
    c1 = ddiv(dsub(g1, dmul(s12, (c2, zero))), s11)[0]
    c1 = jnp.where(full1, c1, zero)
    r0 = dsub(dsub(g0, dmul(d02, (c1, zero))), dmul(d03, (c2, zero)))
    return ddiv(r0, d01)[0], c1, c2


PAIRS = ((0, 0), (0, 1), (0, 2), (0, 3), (1, 1), (1, 2), (1, 3), (2, 2), (2, 3))


def split_short(a):
    t = a * 65537.0
    hi = t - (t - a)
    return hi, a - hi


def dot_step(groups, sums):
    parts = [[split_short(v) for v in vs] for vs in groups]
    out = []
    for k, (i, j) in enumerate(PAIRS):
        main = None
        rest = None
        for vs, ps in zip(groups, parts):
            m = ps[i][0] * ps[j][0]
            if i == j:
                r = ps[i][1] * (vs[i] + ps[i][0])
            else:
                r = ps[i][0] * ps[j][1] + ps[i][1] * vs[j]
            main = m if main is None else main + m
            rest = r if rest is None else rest + r
        s, e = two_sum(sums[2 * k], main)
        out += [s, sums[2 * k + 1] + (e + rest)]
    return tuple(out)


def pack_sums(sums, extra=()):
    lane = lax.broadcasted_iota(jnp.int32, (1, LANES), 1)
    row = jnp.zeros((1, LANES), jnp.float32)
    total = lambda a: jnp.sum(jnp.sum(a, axis=0, keepdims=True), axis=1, keepdims=True)
    for k in range(len(PAIRS)):
        s, e = sums[2 * k], sums[2 * k + 1]
        peak = jnp.max(jnp.max(jnp.abs(s), axis=0, keepdims=True), axis=1, keepdims=True)
        lift = jnp.broadcast_to(peak * 2048.0, s.shape)
        main = (s + lift) - lift
        row = jnp.where(lane == k, total(main), row)
        row = jnp.where(lane == 64 + k, total((s - main) + e), row)
    for k, a in enumerate(extra):
        row = jnp.where(lane == len(PAIRS) + k, total(a), row)
    return row


def gathered_sums(ref, extra=0):
    rows = [(ref[d], None) for d in range(ref.shape[0])]
    while len(rows) > 1:
        merged = []
        for k in range(0, len(rows) - 1, 2):
            (a, ea), (b, eb) = rows[k], rows[k + 1]
            s, e = two_sum(a, b)
            e = e if ea is None else e + (ea + eb)
            merged.append((s, e))
        if len(rows) % 2:
            a, ea = rows[-1]
            merged.append((a, jnp.zeros_like(a) if ea is None else ea))
        rows = merged
    s, e = rows[0]
    lane = lax.broadcasted_iota(jnp.int32, s.shape, 1)
    pick = lambda a, k: jnp.sum(jnp.where(lane == k, a, 0.0), axis=1, keepdims=True)
    dots = []
    for k in range(len(PAIRS)):
        hi = pick(s, k)
        lo = pick(e, k) + pick(s, 64 + k)
        dots.append(fast_sum(hi, lo))
    return dots, [pick(s, len(PAIRS) + k) for k in range(extra)]


def fields_of(rc, cx, cy):
    control_cost = 0.5 * (cx * cx + cy * cy)
    return rc + control_cost, 1.0 + control_cost


def edge_rows(rc, cx, cy, pd):
    return jnp.concatenate([*fields_of(rc, cx, cy), pd])


def neighbours_along(axis):
    i = lax.axis_index(axis)
    return i > 0, i < lax.axis_size(axis) - 1


def lanes():
    return lax.broadcasted_iota(jnp.int32, (SUB, LANES), 1)


def tile_cols(j):
    return slice(j * LANES, (j + 1) * LANES)


def halo_tile(ref, field, j, present):
    return jnp.where(present, ref[field * SUB : (field + 1) * SUB, tile_cols(j)], 0.0)


def packing(tiles):
    per = LANES // WIDE
    return per, -(-tiles // per)


def pack_columns_kernel(f_ref, c_ref, p_ref, north_ref, south_ref, west_ref, east_ref):
    tiles = f_ref.shape[0] // SUB + 2
    per, groups = packing(tiles)
    lane = lanes()
    has_north, has_south = neighbours_along("row")
    for field, own in enumerate((f_ref, c_ref, p_ref)):

        def tile(j, t):
            if t == 0:
                return halo_tile(north_ref, field, j, has_north)
            if t == tiles - 1:
                return halo_tile(south_ref, field, j, has_south)
            return own[(t - 1) * SUB : t * SUB, tile_cols(j)]

        for v in range(groups):
            west = jnp.zeros((SUB, LANES), jnp.float32)
            east = west
            for g in range(min(per, tiles - v * per)):
                here = (lane >= WIDE * g) & (lane < WIDE * (g + 1))
                a = tile(0, v * per + g)
                b = tile(f_ref.shape[1] // LANES - 1, v * per + g)
                west = jnp.where(here, pltpu.roll(a, (WIDE * g) % LANES, 1), west)
                east = jnp.where(here, pltpu.roll(b, (WIDE * (g + 1)) % LANES, 1), east)
            at = (field * groups + v) * SUB
            west_ref[at : at + SUB] = west
            east_ref[at : at + SUB] = east


def beside(ref, r, which, margin=False):
    lane = lanes()
    here = [ref[j, pl.ds(r, SUB), :] for j in which]
    south = [ref[j, pl.ds(r + 1, SUB), :] for j in which]
    north = [ref[j, pl.ds(r - 1, SUB), :] for j in which]
    left = [pltpu.roll(a, LANES - 1, 1) for a in here]
    right = [pltpu.roll(a, 1, 1) for a in here]
    n = len(which) - 1 if margin else len(which)
    over, under = left[:n], right[:n]
    past, before = left[0], right[n - 1]
    if margin:
        past = pltpu.roll(here[n], LANES - 1 - SUB, 1)
        before = pltpu.roll(here[n], 1 + SUB, 1)
    if n > 1 or margin:
        over = [jnp.where(lane == LANES - 1, left[k + 1] if k < n - 1 else past, left[k]) for k in range(n)]
        under = [jnp.where(lane == 0, right[k - 1] if k > 0 else before, right[k]) for k in range(n)]
    return here, south, north, over + left[n:], under + right[n:]


def weighted_apply(center, w, cells):
    here, south, north, east, west = cells
    return center * here - ((w[0] * south + w[1] * north) + (w[2] * east + w[3] * west))


def apply_tiles(ref, w_ref, center_ref, r, which, margin=False, center_at=None):
    cells = beside(ref, r, which, margin)
    at = pl.ds(r, SUB)
    out = []
    for i, j in enumerate(which):
        w = [w_ref[k, j, at, :] for k in range(4)]
        center = center_ref[j if center_at is None else center_at, at, :]
        out.append(weighted_apply(center, w, [c[i] for c in cells]))
    return out, cells[0]


def first_vector(f_ref, c_ref, v1_ref, w_ref, faces_ref, center_ref, r, which, center_at=None):
    at = pl.ds(r, SUB)
    cond = beside(c_ref, r, which)
    cells = beside(f_ref, r, which)
    for i, j in enumerate(which):
        c = cond[0][i]
        inside = jnp.minimum(c, 1.0)
        face = inside * FACE
        w = [face * (c + cond[k][i]) for k in (1, 2, 3, 4)]
        faces = (w[0] + w[1]) + (w[2] + w[3])
        center = inside * (discount_rate * SCALE) + faces
        for k in range(4):
            w_ref[k, j, at, :] = w[k]
        faces_ref[j, at, :] = faces
        center_ref[j if center_at is None else center_at, at, :] = center
        v1_ref[j, at, :] = weighted_apply(center, w, [x[i] for x in cells])


def clear_pads(refs, which):
    zero = jnp.zeros((SUB, LANES), jnp.float32)
    for ref in refs:
        rows = ref.shape[1]
        for j in which:
            ref[j, 0:SUB] = zero
            ref[j, rows - SUB : rows] = zero


def row_tiles(ref):
    return (ref.shape[1] - 2 * SUB) // SUB


def sweep(start, stop, step, unroll=2):
    def some(t, _):
        for u in range(unroll):
            step(pl.multiple_of(SUB + (start + t * unroll + u) * SUB, SUB))
        return 0

    whole = (stop - start) // unroll
    lax.fori_loop(0, whole, some, 0)
    for t in range(start + whole * unroll, stop):
        step(SUB + t * SUB)


def second_vector(v1_ref, v2_ref, w_ref, center_ref, which, margin=False, center_at=None, unroll=2):
    def step(r):
        out, _here = apply_tiles(v1_ref, w_ref, center_ref, r, which, margin, center_at)
        for i, j in enumerate(which):
            v2_ref[j, pl.ds(r, SUB), :] = out[i]

    sweep(0, row_tiles(v1_ref), step, unroll)


def products(v_refs, w_ref, center_ref, which, take, margin=False, center_at=None, unroll=2):
    v0_ref, v1_ref, v2_ref = v_refs
    own = which[:-1] if margin else which

    def step(t, sums):
        groups = []
        for u in range(unroll):
            r = pl.multiple_of(PAD + (t * unroll + u) * SUB, SUB)
            out, here = apply_tiles(v2_ref, w_ref, center_ref, r, which if margin else own, margin, center_at)
            at = pl.ds(r, SUB)
            for i, j in enumerate(own):
                vs = [v0_ref[j, at, :], v1_ref[j, at, :], here[i]]
                mask = take(j)
                if mask is not None:
                    vs = [jnp.where(mask, v, 0.0) for v in vs]
                groups.append((*vs, out[i]))
        return dot_step(groups, sums)

    zero = jnp.zeros((SUB, LANES), jnp.float32)
    return lax.fori_loop(0, (row_tiles(v0_ref) - 2) // unroll, step, (zero,) * (2 * len(PAIRS)))


def inner_first_kernel(f_in, c_in, f_ref, c_ref, v1_ref, w_ref, faces_ref, center_ref):
    own = list(range(f_ref.shape[0] - 1))
    rows = f_in.shape[0]
    clear_pads((f_ref, c_ref, v1_ref), own)
    for j in own:
        f_ref[j, PAD : PAD + rows] = f_in[:, tile_cols(j)]
        c_ref[j, PAD : PAD + rows] = c_in[:, tile_cols(j)]
    sweep(2, row_tiles(f_ref) - 2,
          lambda r: first_vector(f_ref, c_ref, v1_ref, w_ref, faces_ref, center_ref, r, own))


def inner_rest_kernel(after, p_in, north_ref, south_ref, f_in, c_in, v1_in, w_in, faces_in, center_in,
                      f_ref, c_ref, v1_ref, w_ref, faces_ref, center_ref, p_ref, v2_ref, sums_ref):
    count = f_ref.shape[0] - 1
    own = list(range(count))
    rows = f_ref.shape[1]
    tiles = row_tiles(f_ref)
    has_north, has_south = neighbours_along("row")
    clear_pads((p_ref, v2_ref), own)
    lane = lanes()
    for j in own:
        p_ref[j, PAD : rows - PAD] = p_in[:, tile_cols(j)]
    for field, ref in enumerate((f_ref, c_ref, p_ref)):
        for j in own:
            ref[j, SUB : 2 * SUB] = halo_tile(north_ref, field, j, has_north)
            ref[j, rows - 2 * SUB : rows - SUB] = halo_tile(south_ref, field, j, has_south)
        for t in range(1, tiles + 1):
            at = slice(t * SUB, (t + 1) * SUB)
            last = pltpu.roll(ref[count - 1, at], SUB, 1)
            first = pltpu.roll(ref[0, at], LANES - SUB, 1)
            ref[count, at] = jnp.where(lane < SUB, last, jnp.where(lane >= LANES - SUB, first, 0.0))
    for t in (0, 1, tiles - 2, tiles - 1):
        first_vector(f_ref, c_ref, v1_ref, w_ref, faces_ref, center_ref, SUB + t * SUB, own)
    second_vector(v1_ref, v2_ref, w_ref, center_ref, own)

    def take(j):
        mask = lane >= DEEP if j == 0 else None
        if j == count - 1:
            far = lane < LANES - DEEP
            mask = far if mask is None else mask & far
        return mask

    sums = products((f_ref, v1_ref, v2_ref), w_ref, center_ref, own, take)
    for k, a in enumerate(sums):
        sums_ref[k] = a


def margin_kernel(west_ref, east_ref, sums_in, f_in, c_in, p_in, v1_in, v2_in, w_in, faces_in,
                  f_ref, c_ref, p_ref, v1_ref, v2_ref, w_ref, faces_ref, row_ref, center_ref):
    count = f_ref.shape[0] - 1
    margin = [count]
    tiles = row_tiles(f_ref)
    per, groups = packing(tiles)
    lane = lanes()
    has_west, has_east = neighbours_along("col")
    take_east = (lane >= SUB) & (lane < SUB + WIDE) & has_east
    take_west = (lane >= LANES - SUB - WIDE) & (lane < LANES - SUB) & has_west
    clear_pads((f_ref, c_ref, p_ref, v1_ref, v2_ref), margin)
    for field, ref in enumerate((f_ref, c_ref, p_ref)):
        for t in range(tiles):
            v, g = divmod(t, per)
            src = slice((field * groups + v) * SUB, (field * groups + v + 1) * SUB)
            at = slice(SUB + t * SUB, 2 * SUB + t * SUB)
            west = pltpu.roll(west_ref[src], (LANES - SUB - WIDE * (g + 1)) % LANES, 1)
            east = pltpu.roll(east_ref[src], (SUB - WIDE * g) % LANES, 1)
            ref[count, at] = jnp.where(take_east, east, jnp.where(take_west, west, ref[count, at]))
    sweep(0, tiles, lambda r: first_vector(
        f_ref, c_ref, v1_ref, w_ref, faces_ref, center_ref, r, margin, 0), 4)
    second_vector(v1_ref, v2_ref, w_ref, center_ref, margin, center_at=0, unroll=4)
    mask = ((lane >= SUB - DEEP) & (lane < SUB)) | ((lane >= LANES - SUB) & (lane < LANES - SUB + DEEP))
    sums = products((f_ref, v1_ref, v2_ref), w_ref, center_ref, margin, lambda j: mask,
                    center_at=0, unroll=4)

    def patch(r):
        at = pl.ds(r, SUB)
        first, last = lane < DEEP, lane >= LANES - DEEP
        for ref in (v1_ref, v2_ref, faces_ref, w_ref.at[3]):
            ref[0, at, :] = jnp.where(first, pltpu.roll(ref[count, at, :], SUB, 1), ref[0, at, :])
        for ref in (v1_ref, v2_ref, faces_ref, w_ref.at[2]):
            tile = jnp.where(last, pltpu.roll(ref[count, at, :], LANES - SUB, 1), ref[count - 1, at, :])
            ref[count - 1, at, :] = tile

    sweep(0, tiles, patch)
    total = []
    for k in range(len(PAIRS)):
        s, e = two_sum(sums[2 * k], sums_in[2 * k])
        total += [s, e + (sums[2 * k + 1] + sums_in[2 * k + 1])]
    row_ref[...] = jnp.broadcast_to(pack_sums(total)[None], row_ref.shape)


def density_kernel(rows_ref, f_ref, c_ref, p_ref, v1_ref, v2_ref, w_ref, faces_ref,
                   value_ref, u1_ref, u2_ref, row_ref, vx_ref, center_ref):
    dots, _unused = gathered_sums(rows_ref)
    c0, c1, c2 = [jnp.broadcast_to(c, (SUB, LANES)) for c in galerkin(dots)]
    which = list(range(f_ref.shape[0]))
    own = which[:-1]
    tiles = row_tiles(f_ref)
    clear_pads((vx_ref, u1_ref, u2_ref), which)

    def value(r):
        at = pl.ds(r, SUB)
        for j in which:
            vx_ref[j, at, :] = (c0 * f_ref[j, at, :] + c1 * v1_ref[j, at, :]) + c2 * v2_ref[j, at, :]

    sweep(0, tiles, value)

    def first(r):
        at = pl.ds(r, SUB)
        val = beside(vx_ref, r, which, True)
        cells = beside(p_ref, r, which, True)
        for j in which:
            inside = jnp.minimum(c_ref[j, at, :], 1.0)
            slope_row = 0.5 * (val[1][j] - val[2][j])
            slope_col = 0.5 * (val[3][j] - val[4][j])
            congestion = (slope_row * slope_row + slope_col * slope_col) * (0.5 / diffusion)
            zeroth = (discount_rate + congestion) * SCALE
            center = inside * zeroth + faces_ref[j, at, :]
            center_ref[j, at, :] = center
            w = [w_ref[k, j, at, :] for k in range(4)]
            u1_ref[j, at, :] = weighted_apply(center, w, [x[j] for x in cells])

    sweep(0, tiles, first)

    def outer(t, sums):
        r = pl.multiple_of(PAD + t * SUB, SUB)
        at = pl.ds(r, SUB)
        to = pl.ds(pl.multiple_of(t * SUB, SUB), SUB)
        cost, weight = sums
        for j in own:
            v = vx_ref[j, at, :]
            p = p_ref[j, at, :]
            value_ref[to, tile_cols(j)] = v
            cost = cost + p * (f_ref[j, at, :] - discount_rate * v)
            weight = weight + p
        return cost, weight

    zero = jnp.zeros((SUB, LANES), jnp.float32)
    extra = lax.fori_loop(0, tiles - 2, outer, (zero, zero))
    second_vector(u1_ref, u2_ref, w_ref, center_ref, which, True)
    sums = products((p_ref, u1_ref, u2_ref), w_ref, center_ref, which, lambda j: None, True)
    row_ref[...] = jnp.broadcast_to(pack_sums(sums, extra)[None], row_ref.shape)


def finish_kernel(rows_ref, p_ref, u1_ref, u2_ref, density_ref, ergodic_ref):
    dots, (cost, weight) = gathered_sums(rows_ref, 2)
    ergodic_ref[...] = cost / weight
    c0, c1, c2 = [jnp.broadcast_to(c, (SUB, LANES)) for c in galerkin(dots)]
    own = p_ref.shape[0] - 1

    def tile(t, _):
        at = pl.ds(pl.multiple_of(PAD + t * SUB, SUB), SUB)
        to = pl.ds(pl.multiple_of(t * SUB, SUB), SUB)
        for j in range(own):
            density_ref[to, j * LANES : (j + 1) * LANES] = (
                c0 * p_ref[j, at, :] + c1 * u1_ref[j, at, :]
            ) + c2 * u2_ref[j, at, :]
        return 0

    lax.fori_loop(0, density_ref.shape[0] // SUB, tile, 0)


def f32(*shape):
    return jax.ShapeDtypeStruct(shape, jnp.float32)


def exchange(back, ahead, axis):
    count = lax.axis_size(axis)
    after = lax.ppermute(back, axis, [((i + 1) % count, i) for i in range(count)])
    before = lax.ppermute(ahead, axis, [(i, (i + 1) % count) for i in range(count)])
    return before, after


def everyone(row):
    return lax.all_to_all(row, BOTH, 0, 0, tiled=True)


def body(*args):
    rows, cols = args[0].shape
    devices = lax.axis_size("row") * lax.axis_size("col")
    count = cols // LANES
    ext = f32(count + 1, rows + 2 * PAD, LANES)
    ext4 = f32(4, *ext.shape)
    everyones = f32(devices, 1, LANES)
    _per, groups = packing(rows // SUB + 2)
    small = pltpu.CompilerParams(vmem_limit_bytes=VMEM_BYTES)

    def call(kernel, ins, outs, scratch=0, **more):
        return pl.pallas_call(
            kernel,
            in_specs=[VM] * len(ins),
            out_specs=[VM] * len(outs),
            out_shape=outs,
            scratch_shapes=[pltpu.VMEM(ext.shape if scratch > 1 else (1, *ext.shape[1:]), jnp.float32)] * scratch,
            compiler_params=small,
            **more,
        )(*ins)

    cost = lambda us: pl.CostEstimate(flops=0, bytes_accessed=int(us * 2e6), transcendentals=0)
    up, down = [edge_rows(*[x[at] for x in args]) for at in (slice(0, SUB), slice(rows - SUB, rows))]
    north, south = exchange(up, down, "row")
    forcing, conduct = fields_of(*args[:3])
    prior = args[3]
    f, c, v1, w, faces, center = call(
        inner_first_kernel, (forcing, conduct), [ext] * 3 + [ext4, ext, ext], cost_estimate=cost(1.5))
    packs = call(
        pack_columns_kernel, (forcing, conduct, prior, north, south), [f32(3 * groups * SUB, LANES)] * 2)
    west, east = exchange(*packs, "col")
    f, c, v1, w, faces, _center, p, v2, sums = call(
        inner_rest_kernel, (packs[0], prior, north, south, f, c, v1, w, faces, center),
        [ext] * 3 + [ext4] + [ext] * 4 + [f32(2 * len(PAIRS), SUB, LANES)],
        input_output_aliases={4 + k: k for k in range(6)}, cost_estimate=cost(4))
    f, c, p, v1, v2, w, faces, row = call(
        margin_kernel, (west, east, sums, f, c, p, v1, v2, w, faces),
        [ext] * 5 + [ext4, ext, everyones], 1, input_output_aliases={3 + k: k for k in range(7)})
    value, u1, u2, row = call(
        density_kernel, (everyone(row), f, c, p, v1, v2, w, faces),
        [f32(rows, cols), ext, ext, everyones], 2)
    density, ergodic = call(finish_kernel, (everyone(row), p, u1, u2), [f32(rows, cols), f32(1, 1)])
    return value, density, ergodic[0, 0]


def solution(mesh):
    spec = P("row", "col")
    return jax.shard_map(body, mesh=mesh, in_specs=(spec,) * 4, out_specs=(spec, spec, P()), check_vma=False)
```

```python
import functools

import jax
import jax.numpy as jnp
from jax import lax
from jax.experimental import pallas as pl
from jax.experimental.pallas import tpu as pltpu
from jax.sharding import PartitionSpec as P

discount_rate = 0.05
diffusion = 0.25
SCALE = 0.0625
FACE = diffusion * 0.5 * SCALE
LANES = 128
SUB = 8
WIDE = 7
EDGE = 10
DEEP = 5
PAD = 2 * SUB
VMEM_BYTES = 16 * 2**20
VM = pl.BlockSpec(memory_space=pltpu.VMEM)
BOTH = ("row", "col")


def two_sum(a, b):
    s = a + b
    t = s - a
    return s, (a - (s - t)) + (b - t)


def fast_sum(a, b):
    s = a + b
    return s, b - (s - a)


def halves(a):
    t = a * 4097.0
    hi = t - (t - a)
    return hi, a - hi


def two_prod(a, b):
    p = a * b
    ah, al = halves(a)
    bh, bl = halves(b)
    return p, ((ah * bh - p) + ah * bl + al * bh) + al * bl


def dmul(a, b):
    p, e = two_prod(a[0], b[0])
    return fast_sum(p, e + (a[0] * b[1] + a[1] * b[0]))


def dsub(a, b):
    s, e = two_sum(a[0], -b[0])
    return fast_sum(s, e + (a[1] - b[1]))


def ddiv(a, b):
    q = a[0] / b[0]
    r = dsub(a, dmul((q, jnp.zeros_like(q)), b))
    return fast_sum(q, r[0] / b[0])


def galerkin(dots):
    d00, d01, d02, d03, d11, d12, d13, d22, d23 = dots
    zero = jnp.zeros_like(d00[0])
    l1 = ddiv(d11, d01)
    l2 = ddiv(d12, d01)
    s11 = dsub(d12, dmul(l1, d02))
    s12 = dsub(d13, dmul(l1, d03))
    s21 = dsub(d22, dmul(l2, d02))
    s22 = dsub(d23, dmul(l2, d03))
    g0 = (d00[0] * SCALE, d00[1] * SCALE)
    g1 = dsub((d01[0] * SCALE, d01[1] * SCALE), dmul(l1, g0))
    g2 = dsub((d02[0] * SCALE, d02[1] * SCALE), dmul(l2, g0))
    l3 = ddiv(s21, s11)
    t22 = dsub(s22, dmul(l3, s12))
    g2 = dsub(g2, dmul(l3, g1))
    full1 = s11[0] > 1e-12 * d12[0]
    full2 = full1 & (t22[0] > 1e-12 * d23[0])
    c2 = jnp.where(full2, ddiv(g2, t22)[0], zero)
    c1 = ddiv(dsub(g1, dmul(s12, (c2, zero))), s11)[0]
    c1 = jnp.where(full1, c1, zero)
    r0 = dsub(dsub(g0, dmul(d02, (c1, zero))), dmul(d03, (c2, zero)))
    return ddiv(r0, d01)[0], c1, c2


PAIRS = ((0, 0), (0, 1), (0, 2), (0, 3), (1, 1), (1, 2), (1, 3), (2, 2), (2, 3))


def split_short(a):
    t = a * 65537.0
    hi = t - (t - a)
    return hi, a - hi


def dot_step(groups, sums):
    parts = [[split_short(v) for v in vs] for vs in groups]
    out = []
    for k, (i, j) in enumerate(PAIRS):
        main = None
        rest = None
        for vs, ps in zip(groups, parts):
            m = ps[i][0] * ps[j][0]
            if i == j:
                r = ps[i][1] * (vs[i] + ps[i][0])
            else:
                r = ps[i][0] * ps[j][1] + ps[i][1] * vs[j]
            main = m if main is None else main + m
            rest = r if rest is None else rest + r
        s, e = two_sum(sums[2 * k], main)
        out += [s, sums[2 * k + 1] + (e + rest)]
    return tuple(out)


def pack_sums(sums, extra=()):
    lane = lax.broadcasted_iota(jnp.int32, (1, LANES), 1)
    row = jnp.zeros((1, LANES), jnp.float32)
    total = lambda a: jnp.sum(jnp.sum(a, axis=0, keepdims=True), axis=1, keepdims=True)
    for k in range(len(PAIRS)):
        s, e = sums[2 * k], sums[2 * k + 1]
        peak = jnp.max(jnp.max(jnp.abs(s), axis=0, keepdims=True), axis=1, keepdims=True)
        lift = jnp.broadcast_to(peak * 2048.0, s.shape)
        main = (s + lift) - lift
        row = jnp.where(lane == k, total(main), row)
        row = jnp.where(lane == 64 + k, total((s - main) + e), row)
    for k, a in enumerate(extra):
        row = jnp.where(lane == len(PAIRS) + k, total(a), row)
    return row


def gathered_sums(ref, extra=0):
    rows = [(ref[d], None) for d in range(ref.shape[0])]
    while len(rows) > 1:
        merged = []
        for k in range(0, len(rows) - 1, 2):
            (a, ea), (b, eb) = rows[k], rows[k + 1]
            s, e = two_sum(a, b)
            e = e if ea is None else e + (ea + eb)
            merged.append((s, e))
        if len(rows) % 2:
            a, ea = rows[-1]
            merged.append((a, jnp.zeros_like(a) if ea is None else ea))
        rows = merged
    s, e = rows[0]
    lane = lax.broadcasted_iota(jnp.int32, s.shape, 1)
    pick = lambda a, k: jnp.sum(jnp.where(lane == k, a, 0.0), axis=1, keepdims=True)
    dots = []
    for k in range(len(PAIRS)):
        hi = pick(s, k)
        lo = pick(e, k) + pick(s, 64 + k)
        dots.append(fast_sum(hi, lo))
    return dots, [pick(s, len(PAIRS) + k) for k in range(extra)]


FIRST = EDGE + 2 * WIDE


def fields_of(rc, cx, cy):
    control_cost = 0.5 * (cx * cx + cy * cy)
    return rc + control_cost, 1.0 + control_cost


def edge_rows(rc, cx, cy, pd):
    return jnp.concatenate([*fields_of(rc, cx, cy), pd])


def neighbours_along(axis):
    i = lax.axis_index(axis)
    return i > 0, i < lax.axis_size(axis) - 1


def lanes():
    return lax.broadcasted_iota(jnp.int32, (SUB, LANES), 1)


def tile_cols(j):
    return slice(j * LANES, (j + 1) * LANES)


def halo_tile(ref, field, j, present):
    return jnp.where(present, ref[field * SUB : (field + 1) * SUB, tile_cols(j)], 0.0)


def packing(tiles):
    per = LANES // (2 * WIDE)
    return per, -(-tiles // per)


def pack_columns_kernel(f_ref, c_ref, p_ref, north_ref, south_ref, west_ref, east_ref):
    tiles = row_tiles(f_ref)
    per, groups = packing(tiles)
    end = p_ref.shape[1] // LANES - 1
    lane = lanes()
    has_north, has_south = neighbours_along("row")
    for field in range(3):

        def tile(j, t):
            if t == 0:
                return halo_tile(north_ref, field, j, has_north)
            if t == tiles - 1:
                return halo_tile(south_ref, field, j, has_south)
            if field == 2:
                return p_ref[(t - 1) * SUB : t * SUB, tile_cols(j)]
            return (f_ref, c_ref)[field][j, (t + 1) * SUB : (t + 2) * SUB]

        for v in range(groups):
            west = jnp.zeros((SUB, LANES), jnp.float32)
            east = west
            for g in range(min(per, tiles - v * per)):
                at = 2 * WIDE * g
                a, b = tile(0, v * per + g), tile(end, v * per + g)
                west = jnp.where((lane >= at) & (lane < at + WIDE), pltpu.roll(a, at, 1), west)
                there = (lane >= at + WIDE) & (lane < at + 2 * WIDE)
                east = jnp.where(there, pltpu.roll(b, (at + 2 * WIDE) % LANES, 1), east)
            at = (field * groups + v) * SUB
            west_ref[at : at + SUB] = west
            east_ref[at : at + SUB] = east


def beside(ref, r, which):
    lane = lanes()
    n = len(which)
    here = [ref[j, pl.ds(r, SUB), :] for j in which]
    south = [ref[j, pl.ds(r + 1, SUB), :] for j in which]
    north = [ref[j, pl.ds(r - 1, SUB), :] for j in which]
    east = [pltpu.roll(a, LANES - 1, 1) for a in here]
    west = [pltpu.roll(a, 1, 1) for a in here]
    if n > 1:
        east, west = (
            [jnp.where(lane == LANES - 1, east[(k + 1) % n], east[k]) for k in range(n)],
            [jnp.where(lane == 0, west[k - 1], west[k]) for k in range(n)],
        )
    return [dict(zip(which, x)) for x in (here, south, north, east, west)]


def beside_all(ref, r, parts):
    found = [beside(ref, r, which) for which in parts]
    return [{j: x for part in found for j, x in part[k].items()} for k in range(5)]


def weighted_apply(center, w, cells):
    here, south, north, east, west = cells
    return center * here - ((w[0] * south + w[1] * north) + (w[2] * east + w[3] * west))


def apply_tiles(ref, w_ref, center_ref, r, parts):
    cells = beside_all(ref, r, parts)
    at = pl.ds(r, SUB)
    out = {}
    for j in cells[0]:
        w = [w_ref[k, j, at, :] for k in range(4)]
        out[j] = weighted_apply(center_ref[j, at, :], w, [c[j] for c in cells])
    return out, cells[0]


def first_vector(f_ref, c_ref, v1_ref, w_ref, faces_ref, center_ref, r, which):
    at = pl.ds(r, SUB)
    cond = beside(c_ref, r, which)
    cells = beside(f_ref, r, which)
    out = []
    for j in which:
        c = cond[0][j]
        inside = jnp.minimum(c, 1.0)
        face = inside * FACE
        w = [face * (c + cond[k][j]) for k in (1, 2, 3, 4)]
        faces = (w[0] + w[1]) + (w[2] + w[3])
        center = inside * (discount_rate * SCALE) + faces
        out += [(w_ref.at[k], j, at, w[k]) for k in range(4)]
        out.append((faces_ref, j, at, faces))
        out.append((center_ref, j, at, center))
        out.append((v1_ref, j, at, weighted_apply(center, w, [x[j] for x in cells])))
    return out


def clear_pads(refs, which):
    zero = jnp.zeros((SUB, LANES), jnp.float32)
    for ref in refs:
        rows = ref.shape[1]
        for j in which:
            ref[j, 0:SUB] = zero
            ref[j, rows - SUB : rows] = zero


def row_tiles(ref):
    return (ref.shape[1] - 2 * SUB) // SUB


def sweep(start, stop, step, unroll=2):
    def group(rows):
        stores = [store for r in rows for store in step(r)]
        for ref, j, at, value in stores:
            ref[j, at, :] = value

    def some(t, _):
        base = start + t * unroll
        group([pl.multiple_of(SUB + (base + u) * SUB, SUB) for u in range(unroll)])
        return 0

    whole = (stop - start) // unroll
    lax.fori_loop(0, whole, some, 0)
    rest = range(start + whole * unroll, stop)
    if len(rest):
        group([SUB + t * SUB for t in rest])


def second_vector(v1_ref, v2_ref, w_ref, center_ref, parts, unroll=8):
    def step(r):
        out, _here = apply_tiles(v1_ref, w_ref, center_ref, r, parts)
        return [(v2_ref, j, pl.ds(r, SUB), x) for j, x in out.items()]

    sweep(0, row_tiles(v1_ref), step, unroll)


def no_sums():
    return (jnp.zeros((SUB, LANES), jnp.float32),) * (2 * len(PAIRS))


def own_products(v0_ref, v1_ref, v2_ref, w_ref, center_ref, sums, unroll=2):
    own = list(range(v0_ref.shape[0] - 1))
    lane = lanes()

    def step(t, sums):
        groups = []
        for u in range(unroll):
            r = pl.multiple_of(PAD + (t * unroll + u) * SUB, SUB)
            out, here = apply_tiles(v2_ref, w_ref, center_ref, r, [own])
            at = pl.ds(r, SUB)
            for j in own:
                vs = [v0_ref[j, at, :], v1_ref[j, at, :], here[j]]
                if j == 0:
                    vs = [jnp.where(lane >= DEEP, v, 0.0) for v in vs]
                if j == own[-1]:
                    vs = [jnp.where(lane < LANES - DEEP, v, 0.0) for v in vs]
                groups.append((*vs, out[j]))
        return dot_step(groups, sums)

    return lax.fori_loop(0, (row_tiles(v0_ref) - 2) // unroll, step, sums)


def margin_products(v0_ref, v1_ref, v2_ref, w_ref, center_ref, sums):
    margin = v0_ref.shape[0] - 1
    lane = lanes()
    span = FIRST + DEEP - (EDGE - DEEP)
    runs = (FIRST - EDGE + DEEP) // DEEP
    block = span + (runs - 1) * DEEP
    slots = [block * b + DEEP * k for b in range(LANES // block) for k in range(runs)]
    tiles = row_tiles(v0_ref) - 2
    groups = []
    for start in range(0, tiles, len(slots)):
        packed = None
        for t, slot in zip(range(start, tiles), slots):
            at = slice(PAD + t * SUB, PAD + (t + 1) * SUB)
            out, here = apply_tiles(v2_ref, w_ref, center_ref, PAD + t * SUB, [[margin]])
            vs = [v0_ref[margin, at], v1_ref[margin, at], here[margin], out[margin]]
            put = (slot - (EDGE - DEEP)) % LANES
            vs = [pltpu.roll(v, put, 1) if put else v for v in vs]
            low, high = slot, slot + span - DEEP
            mask = ((lane >= low) & (lane < low + DEEP)) | ((lane >= high) & (lane < high + DEEP))
            if packed is None:
                packed = [jnp.where(mask, v, 0.0) for v in vs]
            else:
                packed = [jnp.where(mask, v, x) for v, x in zip(vs, packed)]
        groups.append(tuple(packed))
    return dot_step(groups, sums)


def with_sides(tile, side, j, count):
    lane = lanes()
    if j == 0:
        tile = jnp.where(lane < DEEP, pltpu.roll(side, LANES - FIRST, 1), tile)
    if j == count - 1:
        tile = jnp.where(lane >= LANES - DEEP, pltpu.roll(side, LANES - EDGE, 1), tile)
    return tile


def inner_first_kernel(f_in, c_in, f_ref, c_ref, v1_ref, w_ref, faces_ref, center_ref):
    own = list(range(f_ref.shape[0] - 1))
    rows = f_in.shape[0]
    clear_pads((f_ref, c_ref, v1_ref), own)
    for j in own:
        f_ref[j, PAD : PAD + rows] = f_in[:, tile_cols(j)]
        c_ref[j, PAD : PAD + rows] = c_in[:, tile_cols(j)]
    sweep(2, row_tiles(f_ref) - 2,
          lambda r: first_vector(f_ref, c_ref, v1_ref, w_ref, faces_ref, center_ref, r, own), 6)


def inner_rest_kernel(after, p_in, north_ref, south_ref, f_in, c_in, v1_in, w_in, faces_in, center_in,
                      f_ref, c_ref, v1_ref, w_ref, faces_ref, center_ref, p_ref, v2_ref, sums_ref):
    count = f_ref.shape[0] - 1
    own = list(range(count))
    rows = f_ref.shape[1]
    tiles = row_tiles(f_ref)
    has_north, has_south = neighbours_along("row")
    clear_pads((p_ref, v2_ref), own)
    lane = lanes()
    for j in own:
        p_ref[j, PAD : rows - PAD] = p_in[:, tile_cols(j)]
    for field, ref in enumerate((f_ref, c_ref, p_ref)):
        for j in own:
            ref[j, SUB : 2 * SUB] = halo_tile(north_ref, field, j, has_north)
            ref[j, rows - 2 * SUB : rows - SUB] = halo_tile(south_ref, field, j, has_south)
        for t in range(1, tiles + 1):
            at = slice(t * SUB, (t + 1) * SUB)
            last = pltpu.roll(ref[count - 1, at], EDGE, 1)
            first = pltpu.roll(ref[0, at], FIRST, 1)
            keep = (lane >= FIRST) & (lane < FIRST + EDGE)
            ref[count, at] = jnp.where(lane < EDGE, last, jnp.where(keep, first, 0.0))
    for start in (0, tiles - 2):
        sweep(start, start + 2,
              lambda r: first_vector(f_ref, c_ref, v1_ref, w_ref, faces_ref, center_ref, r, own))
    second_vector(v1_ref, v2_ref, w_ref, center_ref, [own])
    sums = own_products(f_ref, v1_ref, v2_ref, w_ref, center_ref, no_sums())
    for k, a in enumerate(sums):
        sums_ref[k] = a


def margin_kernel(west_ref, east_ref, sums_in, f_in, c_in, p_in, v1_in, v2_in, w_in, faces_in, center_in,
                  f_ref, c_ref, p_ref, v1_ref, v2_ref, w_ref, faces_ref, center_ref, row_ref):
    count = f_ref.shape[0] - 1
    tiles = row_tiles(f_ref)
    per, groups = packing(tiles)
    lane = lanes()
    has_west, has_east = neighbours_along("col")
    from_east = lax.rem(lane, 2 * WIDE) < WIDE
    halo = (lane >= EDGE) & (lane < FIRST)
    clear_pads((f_ref, c_ref, p_ref, v1_ref, v2_ref), [count])
    for field, ref in enumerate((f_ref, c_ref, p_ref)):
        for v in range(groups):
            src = slice((field * groups + v) * SUB, (field * groups + v + 1) * SUB)
            east = jnp.where(has_east, east_ref[src], 0.0)
            west = jnp.where(has_west, west_ref[src], 0.0)
            both = jnp.where(from_east, east, west)
            for g in range(min(per, tiles - v * per)):
                t = v * per + g
                at = slice(SUB + t * SUB, 2 * SUB + t * SUB)
                ref[count, at] = jnp.where(halo, pltpu.roll(both, (EDGE - 2 * WIDE * g) % LANES, 1), ref[count, at])
    sweep(0, tiles, lambda r: first_vector(
        f_ref, c_ref, v1_ref, w_ref, faces_ref, center_ref, r, [count]), 8)
    second_vector(v1_ref, v2_ref, w_ref, center_ref, [[count]], 8)
    sums = tuple(sums_in[k] for k in range(2 * len(PAIRS)))
    sums = margin_products(f_ref, v1_ref, v2_ref, w_ref, center_ref, sums)
    row_ref[...] = jnp.broadcast_to(pack_sums(sums)[None], row_ref.shape)


def density_kernel(rows_ref, f_ref, c_ref, p_ref, v1_ref, v2_ref, w_ref, faces_ref,
                   value_ref, u1_ref, u2_ref, row_ref, vx_ref, center_ref):
    dots, _unused = gathered_sums(rows_ref)
    c0, c1, c2 = [jnp.broadcast_to(c, (SUB, LANES)) for c in galerkin(dots)]
    which = list(range(f_ref.shape[0]))
    own = which[:-1]
    parts = [own, which[-1:]]
    tiles = row_tiles(f_ref)
    clear_pads((vx_ref, u1_ref, u2_ref), which)

    def value(r):
        at = pl.ds(r, SUB)
        return [
            (vx_ref, j, at, (c0 * f_ref[j, at, :] + c1 * v1_ref[j, at, :]) + c2 * v2_ref[j, at, :])
            for j in which
        ]

    sweep(0, tiles, value, 4)

    def first(r):
        at = pl.ds(r, SUB)
        val = beside_all(vx_ref, r, parts)
        cells = beside_all(p_ref, r, parts)
        out = []
        for j in which:
            inside = jnp.minimum(c_ref[j, at, :], 1.0)
            slope_row = 0.5 * (val[1][j] - val[2][j])
            slope_col = 0.5 * (val[3][j] - val[4][j])
            congestion = (slope_row * slope_row + slope_col * slope_col) * (0.5 / diffusion)
            zeroth = (discount_rate + congestion) * SCALE
            center = inside * zeroth + faces_ref[j, at, :]
            w = [w_ref[k, j, at, :] for k in range(4)]
            out.append((center_ref, j, at, center))
            out.append((u1_ref, j, at, weighted_apply(center, w, [x[j] for x in cells])))
        return out

    sweep(0, tiles, first, 8)

    def outer(t, sums):
        cost, weight = sums
        for u in range(8):
            at = pl.ds(pl.multiple_of(PAD + (8 * t + u) * SUB, SUB), SUB)
            to = pl.ds(pl.multiple_of((8 * t + u) * SUB, SUB), SUB)
            for j in own:
                v = with_sides(vx_ref[j, at, :], vx_ref[len(own), at, :], j, len(own))
                p = p_ref[j, at, :]
                value_ref[to, tile_cols(j)] = v
                cost = cost + p * (f_ref[j, at, :] - discount_rate * v)
                weight = weight + p
        return cost, weight

    zero = jnp.zeros((SUB, LANES), jnp.float32)
    extra = lax.fori_loop(0, (tiles - 2) // 8, outer, (zero, zero))
    second_vector(u1_ref, u2_ref, w_ref, center_ref, parts)
    sums = own_products(p_ref, u1_ref, u2_ref, w_ref, center_ref, no_sums())
    sums = margin_products(p_ref, u1_ref, u2_ref, w_ref, center_ref, sums)
    row_ref[...] = jnp.broadcast_to(pack_sums(sums, extra)[None], row_ref.shape)


def finish_kernel(rows_ref, p_ref, u1_ref, u2_ref, density_ref, ergodic_ref):
    dots, (cost, weight) = gathered_sums(rows_ref, 2)
    ergodic_ref[...] = cost / weight
    c0, c1, c2 = [jnp.broadcast_to(c, (SUB, LANES)) for c in galerkin(dots)]
    count = p_ref.shape[0] - 1

    def tile(t, _):
        for u in range(8):
            at = pl.ds(pl.multiple_of(PAD + (8 * t + u) * SUB, SUB), SUB)
            to = pl.ds(pl.multiple_of((8 * t + u) * SUB, SUB), SUB)
            made = [(c0 * p_ref[j, at, :] + c1 * u1_ref[j, at, :]) + c2 * u2_ref[j, at, :] for j in range(count + 1)]
            for j in range(count):
                density_ref[to, tile_cols(j)] = with_sides(made[j], made[count], j, count)
        return 0

    lax.fori_loop(0, density_ref.shape[0] // (8 * SUB), tile, 0)


def f32(*shape):
    return jax.ShapeDtypeStruct(shape, jnp.float32)


def exchange(back, ahead, axis):
    count = lax.axis_size(axis)
    after = lax.ppermute(back, axis, [((i + 1) % count, i) for i in range(count)])
    before = lax.ppermute(ahead, axis, [(i, (i + 1) % count) for i in range(count)])
    return before, after


def everyone(row):
    return lax.all_to_all(row, BOTH, 0, 0, tiled=True)


def body(*args):
    rows, cols = args[0].shape
    devices = lax.axis_size("row") * lax.axis_size("col")
    count = cols // LANES
    ext = f32(count + 1, rows + 2 * PAD, LANES)
    ext4 = f32(4, *ext.shape)
    everyones = f32(devices, 1, LANES)
    _per, groups = packing(rows // SUB + 2)
    small = pltpu.CompilerParams(vmem_limit_bytes=VMEM_BYTES)

    def call(kernel, ins, outs, scratch=0, **more):
        return pl.pallas_call(
            kernel,
            in_specs=[VM] * len(ins),
            out_specs=[VM] * len(outs),
            out_shape=outs,
            scratch_shapes=[pltpu.VMEM(ext.shape, jnp.float32)] * scratch,
            compiler_params=small,
            **more,
        )(*ins)

    cost = lambda us: pl.CostEstimate(flops=0, bytes_accessed=int(us * 2e6), transcendentals=0)
    up, down = [edge_rows(*[x[at] for x in args]) for at in (slice(0, SUB), slice(rows - SUB, rows))]
    north, south = exchange(up, down, "row")
    forcing, conduct = fields_of(*args[:3])
    prior = args[3]
    f, c, v1, w, faces, center = call(
        inner_first_kernel, (forcing, conduct), [ext] * 3 + [ext4, ext, ext], cost_estimate=cost(1.5))
    packs = call(
        pack_columns_kernel, (f, c, prior, north, south), [f32(3 * groups * SUB, LANES)] * 2)
    west, east = exchange(*packs, "col")
    f, c, v1, w, faces, center, p, v2, sums = call(
        inner_rest_kernel, (packs[0], prior, north, south, f, c, v1, w, faces, center),
        [ext] * 3 + [ext4] + [ext] * 4 + [f32(2 * len(PAIRS), SUB, LANES)],
        input_output_aliases={4 + k: k for k in range(6)}, cost_estimate=cost(4))
    f, c, p, v1, v2, w, faces, _center, row = call(
        margin_kernel, (west, east, sums, f, c, p, v1, v2, w, faces, center),
        [ext] * 5 + [ext4, ext, ext, everyones], input_output_aliases={3 + k: k for k in range(8)})
    value, u1, u2, row = call(
        density_kernel, (everyone(row), f, c, p, v1, v2, w, faces),
        [f32(rows, cols), ext, ext, everyones], 2)
    density, ergodic = call(finish_kernel, (everyone(row), p, u1, u2), [f32(rows, cols), f32(1, 1)])
    return value, density, ergodic[0, 0]


def solution(mesh):
    spec = P("row", "col")
    return jax.shard_map(body, mesh=mesh, in_specs=(spec,) * 4, out_specs=(spec, spec, P()), check_vma=False)
```

```python
import functools

import jax
import jax.numpy as jnp
from jax import lax
from jax.experimental import pallas as pl
from jax.experimental.pallas import tpu as pltpu
from jax.sharding import PartitionSpec as P

discount_rate = 0.05
diffusion = 0.25
SCALE = 0.0625
FACE = diffusion * 0.5 * SCALE
LANES = 128
SUB = 8
WIDE = 5
EDGE = 10
DEEP = 5
PAD = 2 * SUB
VMEM_BYTES = 16 * 2**20
VM = pl.BlockSpec(memory_space=pltpu.VMEM)
BOTH = ("row", "col")


def two_sum(a, b):
    s = a + b
    t = s - a
    return s, (a - (s - t)) + (b - t)


def fast_sum(a, b):
    s = a + b
    return s, b - (s - a)


def halves(a):
    t = a * 4097.0
    hi = t - (t - a)
    return hi, a - hi


def two_prod(a, b):
    p = a * b
    ah, al = halves(a)
    bh, bl = halves(b)
    return p, ((ah * bh - p) + ah * bl + al * bh) + al * bl


def dmul(a, b):
    p, e = two_prod(a[0], b[0])
    return fast_sum(p, e + (a[0] * b[1] + a[1] * b[0]))


def dsub(a, b):
    s, e = two_sum(a[0], -b[0])
    return fast_sum(s, e + (a[1] - b[1]))


def ddiv(a, b):
    q = a[0] / b[0]
    r = dsub(a, dmul((q, jnp.zeros_like(q)), b))
    return fast_sum(q, r[0] / b[0])


def galerkin(dots):
    d00, d01, d02, d03, d11, d12, d13, d22, d23 = dots
    zero = jnp.zeros_like(d00[0])
    l1 = ddiv(d11, d01)
    l2 = ddiv(d12, d01)
    s11 = dsub(d12, dmul(l1, d02))
    s12 = dsub(d13, dmul(l1, d03))
    s21 = dsub(d22, dmul(l2, d02))
    s22 = dsub(d23, dmul(l2, d03))
    g0 = (d00[0] * SCALE, d00[1] * SCALE)
    g1 = dsub((d01[0] * SCALE, d01[1] * SCALE), dmul(l1, g0))
    g2 = dsub((d02[0] * SCALE, d02[1] * SCALE), dmul(l2, g0))
    l3 = ddiv(s21, s11)
    t22 = dsub(s22, dmul(l3, s12))
    g2 = dsub(g2, dmul(l3, g1))
    full1 = s11[0] > 1e-12 * d12[0]
    full2 = full1 & (t22[0] > 1e-12 * d23[0])
    c2 = jnp.where(full2, ddiv(g2, t22)[0], zero)
    c1 = ddiv(dsub(g1, dmul(s12, (c2, zero))), s11)[0]
    c1 = jnp.where(full1, c1, zero)
    r0 = dsub(dsub(g0, dmul(d02, (c1, zero))), dmul(d03, (c2, zero)))
    return ddiv(r0, d01)[0], c1, c2


PAIRS = ((0, 0), (0, 1), (0, 2), (0, 3), (1, 1), (1, 2), (1, 3), (2, 2), (2, 3))


def split_short(a):
    t = a * 65537.0
    hi = t - (t - a)
    return hi, a - hi


def dot_step(groups, sums):
    parts = [[split_short(v) for v in vs] for vs in groups]
    out = []
    for k, (i, j) in enumerate(PAIRS):
        main = None
        rest = None
        for vs, ps in zip(groups, parts):
            m = ps[i][0] * ps[j][0]
            if i == j:
                r = ps[i][1] * (vs[i] + ps[i][0])
            else:
                r = ps[i][0] * ps[j][1] + ps[i][1] * vs[j]
            main = m if main is None else main + m
            rest = r if rest is None else rest + r
        s, e = two_sum(sums[2 * k], main)
        out += [s, sums[2 * k + 1] + (e + rest)]
    return tuple(out)


def pack_sums(sums, extra=()):
    lane = lax.broadcasted_iota(jnp.int32, (1, LANES), 1)
    row = jnp.zeros((1, LANES), jnp.float32)
    total = lambda a: jnp.sum(jnp.sum(a, axis=0, keepdims=True), axis=1, keepdims=True)
    for k in range(len(PAIRS)):
        s, e = sums[2 * k], sums[2 * k + 1]
        peak = jnp.max(jnp.max(jnp.abs(s), axis=0, keepdims=True), axis=1, keepdims=True)
        lift = jnp.broadcast_to(peak * 2048.0, s.shape)
        main = (s + lift) - lift
        row = jnp.where(lane == k, total(main), row)
        row = jnp.where(lane == 64 + k, total((s - main) + e), row)
    for k, a in enumerate(extra):
        row = jnp.where(lane == len(PAIRS) + k, total(a), row)
    return row


def gathered_sums(ref, extra=0):
    rows = [(ref[d], None) for d in range(ref.shape[0])]
    while len(rows) > 1:
        merged = []
        for k in range(0, len(rows) - 1, 2):
            (a, ea), (b, eb) = rows[k], rows[k + 1]
            s, e = two_sum(a, b)
            e = e if ea is None else e + (ea + eb)
            merged.append((s, e))
        if len(rows) % 2:
            a, ea = rows[-1]
            merged.append((a, jnp.zeros_like(a) if ea is None else ea))
        rows = merged
    s, e = rows[0]
    lane = lax.broadcasted_iota(jnp.int32, s.shape, 1)
    pick = lambda a, k: jnp.sum(jnp.where(lane == k, a, 0.0), axis=1, keepdims=True)
    dots = []
    for k in range(len(PAIRS)):
        hi = pick(s, k)
        lo = pick(e, k) + pick(s, 64 + k)
        dots.append(fast_sum(hi, lo))
    return dots, [pick(s, len(PAIRS) + k) for k in range(extra)]


FIRST = EDGE + 2 * WIDE


def fields_of(rc, cx, cy):
    control_cost = 0.5 * (cx * cx + cy * cy)
    return rc + control_cost, 1.0 + control_cost


def edge_rows(rc, cx, cy, pd):
    rows, cols = rc.shape
    few = WIDE - 2
    gap = jnp.zeros((2 * SUB - 2 * WIDE - few, cols), jnp.float32)
    ends = [[x[:SUB] for x in (rc, cx, cy, pd)], [x[rows - SUB :] for x in (rc, cx, cy, pd)]]
    (f, c, p), (g, d, q) = lax.optimization_barrier([(*fields_of(*x[:3]), x[3]) for x in ends])
    up = jnp.concatenate([p[:few], f[:WIDE], c[:WIDE], gap])
    return up, jnp.concatenate([gap, d[SUB - WIDE :], g[SUB - WIDE :], q[SUB - few :]])


def neighbours_along(axis):
    i = lax.axis_index(axis)
    return i > 0, i < lax.axis_size(axis) - 1


def is_even(axis):
    return lax.rem(lax.axis_index(axis), 2) == 0


def lanes():
    return lax.broadcasted_iota(jnp.int32, (SUB, LANES), 1)


def tile_cols(j):
    return slice(j * LANES, (j + 1) * LANES)


def halo_tile(refs, field, j, south):
    at = ((3, 8, 0) if south else (5, 0, 8))[field]
    first, second = [ref[at : at + SUB, tile_cols(j)] for ref in refs]
    tile = jnp.where(is_even("row"), first, second) if south else jnp.where(is_even("row"), second, first)
    return jnp.where(neighbours_along("row")[int(south)], tile, 0.0)


def packing(tiles):
    per = LANES // (2 * WIDE)
    return per, -(-tiles // per)


def pack_columns_kernel(f_ref, c_ref, p_ref, near_ref, far_ref, first_ref, second_ref):
    tiles = row_tiles(f_ref)
    per, groups = packing(tiles)
    end = p_ref.shape[0] - 2
    lane = lanes()
    even = is_even("col")
    for field in range(3):

        def tile(j, t):
            if t == 0:
                return halo_tile((near_ref, far_ref), field, j, False)
            if t == tiles - 1:
                return halo_tile((near_ref, far_ref), field, j, True)
            return (f_ref, c_ref, p_ref)[field][j, (t + 1) * SUB : (t + 2) * SUB]

        for v in range(groups):
            west = jnp.zeros((SUB, LANES), jnp.float32)
            east = west
            for g in range(min(per, tiles - v * per)):
                at = 2 * WIDE * g
                a, b = tile(0, v * per + g), tile(end, v * per + g)
                west = jnp.where((lane >= at) & (lane < at + WIDE), pltpu.roll(a, at, 1), west)
                there = (lane >= at + WIDE) & (lane < at + 2 * WIDE)
                east = jnp.where(there, pltpu.roll(b, (at + 2 * WIDE) % LANES, 1), east)
            at = (field * groups + v) * SUB
            first_ref[at : at + SUB] = jnp.where(even, east, west)
            second_ref[at : at + SUB] = jnp.where(even, west, east)


def beside(ref, r, which):
    lane = lanes()
    n = len(which)
    here = [ref[j, pl.ds(r, SUB), :] for j in which]
    south = [ref[j, pl.ds(r + 1, SUB), :] for j in which]
    north = [ref[j, pl.ds(r - 1, SUB), :] for j in which]
    east = [pltpu.roll(a, LANES - 1, 1) for a in here]
    west = [pltpu.roll(a, 1, 1) for a in here]
    if n > 1:
        east, west = (
            [jnp.where(lane == LANES - 1, east[(k + 1) % n], east[k]) for k in range(n)],
            [jnp.where(lane == 0, west[k - 1], west[k]) for k in range(n)],
        )
    return [dict(zip(which, x)) for x in (here, south, north, east, west)]


def beside_all(ref, r, parts):
    found = [beside(ref, r, which) for which in parts]
    return [{j: x for part in found for j, x in part[k].items()} for k in range(5)]


def weighted_apply(center, w, cells):
    here, south, north, east, west = cells
    return center * here - ((w[0] * south + w[1] * north) + (w[2] * east + w[3] * west))


def apply_tiles(ref, w_ref, center_ref, r, parts):
    cells = beside_all(ref, r, parts)
    at = pl.ds(r, SUB)
    out = {}
    for j in cells[0]:
        w = [w_ref[k, j, at, :] for k in range(4)]
        out[j] = weighted_apply(center_ref[j, at, :], w, [c[j] for c in cells])
    return out, cells[0]


def first_vector(f_ref, c_ref, v1_ref, w_ref, faces_ref, center_ref, r, which):
    at = pl.ds(r, SUB)
    cond = beside(c_ref, r, which)
    cells = beside(f_ref, r, which)
    out = []
    for j in which:
        c = cond[0][j]
        inside = jnp.minimum(c, 1.0)
        face = inside * FACE
        w = [face * (c + cond[k][j]) for k in (1, 2, 3, 4)]
        faces = (w[0] + w[1]) + (w[2] + w[3])
        center = inside * (discount_rate * SCALE) + faces
        out += [(w_ref.at[k], j, at, w[k]) for k in range(4)]
        out.append((faces_ref, j, at, faces))
        out.append((center_ref, j, at, center))
        out.append((v1_ref, j, at, weighted_apply(center, w, [x[j] for x in cells])))
    return out


def clear_pads(refs, which):
    zero = jnp.zeros((SUB, LANES), jnp.float32)
    for ref in refs:
        rows = ref.shape[1]
        for j in which:
            ref[j, 0:SUB] = zero
            ref[j, rows - SUB : rows] = zero


def row_tiles(ref):
    return (ref.shape[1] - 2 * SUB) // SUB


def sweep(start, stop, step, unroll=2):
    def group(rows):
        stores = [store for r in rows for store in step(r)]
        for ref, j, at, value in stores:
            ref[j, at, :] = value

    def some(t, _):
        base = start + t * unroll
        group([pl.multiple_of(SUB + (base + u) * SUB, SUB) for u in range(unroll)])
        return 0

    whole = (stop - start) // unroll
    lax.fori_loop(0, whole, some, 0)
    rest = range(start + whole * unroll, stop)
    if len(rest):
        group([SUB + t * SUB for t in rest])


def second_vector(v1_ref, v2_ref, w_ref, center_ref, parts, unroll=17, start=0, stop=None):
    def step(r):
        out, _here = apply_tiles(v1_ref, w_ref, center_ref, r, parts)
        return [(v2_ref, j, pl.ds(r, SUB), x) for j, x in out.items()]

    sweep(start, row_tiles(v1_ref) if stop is None else stop, step, unroll)


def no_sums():
    return (jnp.zeros((SUB, LANES), jnp.float32),) * (2 * len(PAIRS))


def own_products(v0_ref, v1_ref, v2_ref, w_ref, center_ref, sums, unroll=2):
    own = list(range(v0_ref.shape[0] - 1))
    lane = lanes()

    def step(t, sums):
        groups = []
        for u in range(unroll):
            r = pl.multiple_of(PAD + (t * unroll + u) * SUB, SUB)
            out, here = apply_tiles(v2_ref, w_ref, center_ref, r, [own])
            at = pl.ds(r, SUB)
            for j in own:
                vs = [v0_ref[j, at, :], v1_ref[j, at, :], here[j]]
                if j == 0:
                    vs = [jnp.where(lane >= DEEP, v, 0.0) for v in vs]
                if j == own[-1]:
                    vs = [jnp.where(lane < LANES - DEEP, v, 0.0) for v in vs]
                groups.append((*vs, out[j]))
        return dot_step(groups, sums)

    return lax.fori_loop(0, (row_tiles(v0_ref) - 2) // unroll, step, sums)


def margin_products(v0_ref, v1_ref, v2_ref, w_ref, center_ref, sums):
    margin = v0_ref.shape[0] - 1
    lane = lanes()
    span = FIRST + DEEP - (EDGE - DEEP)
    runs = (FIRST - EDGE + DEEP) // DEEP
    block = span + (runs - 1) * DEEP
    slots = [block * b + DEEP * k for b in range(LANES // block) for k in range(runs)]
    tiles = row_tiles(v0_ref) - 2
    groups = []
    for start in range(0, tiles, len(slots)):
        packed = None
        for t, slot in zip(range(start, tiles), slots):
            at = slice(PAD + t * SUB, PAD + (t + 1) * SUB)
            out, here = apply_tiles(v2_ref, w_ref, center_ref, PAD + t * SUB, [[margin]])
            vs = [v0_ref[margin, at], v1_ref[margin, at], here[margin], out[margin]]
            put = (slot - (EDGE - DEEP)) % LANES
            vs = [pltpu.roll(v, put, 1) if put else v for v in vs]
            low, high = slot, slot + span - DEEP
            mask = ((lane >= low) & (lane < low + DEEP)) | ((lane >= high) & (lane < high + DEEP))
            if packed is None:
                packed = [jnp.where(mask, v, 0.0) for v in vs]
            else:
                packed = [jnp.where(mask, v, x) for v, x in zip(vs, packed)]
        groups.append(tuple(packed))
    return dot_step(groups, sums)


def with_sides(tile, side, j, count):
    lane = lanes()
    if j == 0:
        tile = jnp.where(lane < DEEP, pltpu.roll(side, LANES - FIRST, 1), tile)
    if j == count - 1:
        tile = jnp.where(lane >= LANES - DEEP, pltpu.roll(side, LANES - EDGE, 1), tile)
    return tile


def repeat_sides(ref, t):
    count = ref.shape[0] - 1
    lane = lanes()
    at = slice((t + 1) * SUB, (t + 2) * SUB)
    last = pltpu.roll(ref[count - 1, at], EDGE, 1)
    first = pltpu.roll(ref[0, at], FIRST, 1)
    keep = (lane >= FIRST) & (lane < FIRST + EDGE)
    ref[count, at] = jnp.where(lane < EDGE, last, jnp.where(keep, first, 0.0))


def inner_first_kernel(f_in, c_in, p_in,
                       f_ref, c_ref, p_ref, v1_ref, v2_ref, w_ref, faces_ref, center_ref):
    own = list(range(f_ref.shape[0] - 1))
    rows = f_in.shape[0]
    tiles = row_tiles(f_ref)
    clear_pads((f_ref, c_ref, p_ref, v1_ref, v2_ref), own)
    for ref, source in ((f_ref, f_in), (c_ref, c_in), (p_ref, p_in)):
        for j in own:
            ref[j, PAD : PAD + rows] = source[:, tile_cols(j)]
        for t in range(1, tiles - 1):
            repeat_sides(ref, t)
    sweep(2, tiles - 2,
          lambda r: first_vector(f_ref, c_ref, v1_ref, w_ref, faces_ref, center_ref, r, own), 6)
    second_vector(v1_ref, v2_ref, w_ref, center_ref, [own], 7, 3, tiles - 3)


def inner_rest_kernel(after, near_ref, far_ref, f_in, c_in, p_in, v1_in, v2_in, w_in, faces_in, center_in,
                      f_ref, c_ref, p_ref, v1_ref, v2_ref, w_ref, faces_ref, center_ref, sums_ref):
    own = list(range(f_ref.shape[0] - 1))
    rows = f_ref.shape[1]
    tiles = row_tiles(f_ref)
    for field, ref in enumerate((f_ref, c_ref, p_ref)):
        for j in own:
            ref[j, SUB : 2 * SUB] = halo_tile((near_ref, far_ref), field, j, False)
            ref[j, rows - 2 * SUB : rows - SUB] = halo_tile((near_ref, far_ref), field, j, True)
        repeat_sides(ref, 0)
        repeat_sides(ref, tiles - 1)
    for start in (0, tiles - 2):
        sweep(start, start + 2,
              lambda r: first_vector(f_ref, c_ref, v1_ref, w_ref, faces_ref, center_ref, r, own))
    for start in (0, tiles - 3):
        second_vector(v1_ref, v2_ref, w_ref, center_ref, [own], 3, start, start + 3)
    sums = own_products(f_ref, v1_ref, v2_ref, w_ref, center_ref, no_sums())
    for k, a in enumerate(sums):
        sums_ref[k] = a


def margin_kernel(near_ref, far_ref, sums_in, f_in, c_in, p_in, v1_in, v2_in, w_in, faces_in, center_in,
                  f_ref, c_ref, p_ref, v1_ref, v2_ref, w_ref, faces_ref, center_ref, row_ref):
    count = f_ref.shape[0] - 1
    tiles = row_tiles(f_ref)
    per, groups = packing(tiles)
    lane = lanes()
    has_west, has_east = neighbours_along("col")
    even = is_even("col")
    from_east = lax.rem(lane, 2 * WIDE) < WIDE
    halo = (lane >= EDGE) & (lane < FIRST)
    clear_pads((f_ref, c_ref, p_ref, v1_ref, v2_ref), [count])
    for field, ref in enumerate((f_ref, c_ref, p_ref)):
        for v in range(groups):
            src = slice((field * groups + v) * SUB, (field * groups + v + 1) * SUB)
            near, far = near_ref[src], far_ref[src]
            east = jnp.where(has_east, jnp.where(even, near, far), 0.0)
            west = jnp.where(has_west, jnp.where(even, far, near), 0.0)
            both = jnp.where(from_east, east, west)
            for g in range(min(per, tiles - v * per)):
                t = v * per + g
                at = slice(SUB + t * SUB, 2 * SUB + t * SUB)
                ref[count, at] = jnp.where(halo, pltpu.roll(both, (EDGE - 2 * WIDE * g) % LANES, 1), ref[count, at])
    sweep(0, tiles, lambda r: first_vector(
        f_ref, c_ref, v1_ref, w_ref, faces_ref, center_ref, r, [count]), 8)
    second_vector(v1_ref, v2_ref, w_ref, center_ref, [[count]], 8)
    sums = tuple(sums_in[k] for k in range(2 * len(PAIRS)))
    sums = margin_products(f_ref, v1_ref, v2_ref, w_ref, center_ref, sums)
    row_ref[...] = jnp.broadcast_to(pack_sums(sums)[None], row_ref.shape)


def density_kernel(rows_ref, f_ref, c_ref, p_ref, v1_ref, v2_ref, w_ref, faces_ref,
                   value_out, u1_ref, u2_ref, row_ref, vx_ref, center_ref, value_ref, sem):
    dots, _unused = gathered_sums(rows_ref)
    c0, c1, c2 = [jnp.broadcast_to(c, (SUB, LANES)) for c in galerkin(dots)]
    which = list(range(f_ref.shape[0]))
    own = which[:-1]
    parts = [own, which[-1:]]
    tiles = row_tiles(f_ref)
    clear_pads((vx_ref, u1_ref, u2_ref), which)

    def value(r):
        at = pl.ds(r, SUB)
        return [
            (vx_ref, j, at, (c0 * f_ref[j, at, :] + c1 * v1_ref[j, at, :]) + c2 * v2_ref[j, at, :])
            for j in which
        ]

    sweep(0, tiles, value, 4)

    def first(r):
        at = pl.ds(r, SUB)
        val = beside_all(vx_ref, r, parts)
        cells = beside_all(p_ref, r, parts)
        out = []
        for j in which:
            inside = jnp.minimum(c_ref[j, at, :], 1.0)
            slope_row = 0.5 * (val[1][j] - val[2][j])
            slope_col = 0.5 * (val[3][j] - val[4][j])
            congestion = (slope_row * slope_row + slope_col * slope_col) * (0.5 / diffusion)
            zeroth = (discount_rate + congestion) * SCALE
            center = inside * zeroth + faces_ref[j, at, :]
            w = [w_ref[k, j, at, :] for k in range(4)]
            out.append((center_ref, j, at, center))
            out.append((u1_ref, j, at, weighted_apply(center, w, [x[j] for x in cells])))
        return out

    sweep(0, tiles, first, 17)

    def outer(t, sums):
        cost, weight = [list(x) for x in sums]
        for u in range(8):
            at = pl.ds(pl.multiple_of(PAD + (8 * t + u) * SUB, SUB), SUB)
            to = pl.ds(pl.multiple_of((8 * t + u) * SUB, SUB), SUB)
            for j in own:
                v = with_sides(vx_ref[j, at, :], vx_ref[len(own), at, :], j, len(own))
                p = p_ref[j, at, :]
                value_ref[to, tile_cols(j)] = v
                cost[j] = cost[j] + p * (f_ref[j, at, :] - discount_rate * v)
                weight[j] = weight[j] + p
        return tuple(cost), tuple(weight)

    zeros = (jnp.zeros((SUB, LANES), jnp.float32),) * len(own)
    extra = [sum(x) for x in lax.fori_loop(0, (tiles - 2) // 8, outer, (zeros, zeros))]
    copy = pltpu.make_async_copy(value_ref, value_out, sem)
    copy.start()
    second_vector(u1_ref, u2_ref, w_ref, center_ref, parts)
    sums = own_products(p_ref, u1_ref, u2_ref, w_ref, center_ref, no_sums())
    sums = margin_products(p_ref, u1_ref, u2_ref, w_ref, center_ref, sums)
    row_ref[...] = jnp.broadcast_to(pack_sums(sums, extra)[None], row_ref.shape)
    copy.wait()


def finish_kernel(rows_ref, p_ref, u1_ref, u2_ref, density_ref, ergodic_ref):
    dots, (cost, weight) = gathered_sums(rows_ref, 2)
    ergodic_ref[...] = cost / weight
    c0, c1, c2 = [jnp.broadcast_to(c, (SUB, LANES)) for c in galerkin(dots)]
    count = p_ref.shape[0] - 1

    unroll = 8

    def some(t, _):
        for u in range(unroll):
            at = pl.ds(pl.multiple_of(PAD + (unroll * t + u) * SUB, SUB), SUB)
            to = pl.ds(pl.multiple_of((unroll * t + u) * SUB, SUB), SUB)
            made = [(c0 * p_ref[j, at, :] + c1 * u1_ref[j, at, :]) + c2 * u2_ref[j, at, :] for j in range(count + 1)]
            for j in range(count):
                density_ref[to, tile_cols(j)] = with_sides(made[j], made[count], j, count)
        return 0

    lax.fori_loop(0, density_ref.shape[0] // (unroll * SUB), some, 0)


def f32(*shape):
    return jax.ShapeDtypeStruct(shape, jnp.float32)


def exchange(near, far, axis):
    n = lax.axis_size(axis)
    assert n % 2 == 0
    near = lax.ppermute(near, axis, [(i, i ^ 1) for i in range(n)])
    far = lax.ppermute(far, axis, [(i, (((i + 1) % n ^ 1) - 1) % n) for i in range(n)])
    return near, far


def everyone(row):
    return lax.all_to_all(row, BOTH, 0, 0, tiled=True)


def body(*args):
    rows, cols = args[0].shape
    devices = lax.axis_size("row") * lax.axis_size("col")
    count = cols // LANES
    ext = f32(count + 1, rows + 2 * PAD, LANES)
    ext4 = f32(4, *ext.shape)
    everyones = f32(devices, 1, LANES)
    _per, groups = packing(rows // SUB + 2)
    small = pltpu.CompilerParams(vmem_limit_bytes=VMEM_BYTES)

    def call(kernel, ins, outs, scratch=(), to_hbm=0, **more):
        return pl.pallas_call(
            kernel,
            in_specs=[VM] * len(ins),
            out_specs=[pl.BlockSpec(memory_space=pltpu.HBM)] * to_hbm + [VM] * (len(outs) - to_hbm),
            out_shape=outs,
            scratch_shapes=scratch,
            compiler_params=small,
            **more,
        )(*ins)

    cost = lambda us: pl.CostEstimate(flops=0, bytes_accessed=int(us * 2e6), transcendentals=0)
    up, down = edge_rows(*args)
    even = is_even("row")
    near, far = exchange(jnp.where(even, down, up), jnp.where(even, up, down), "row")
    forcing, conduct = fields_of(*args[:3])
    prior = args[3]
    state = call(
        inner_first_kernel, (forcing, conduct, prior),
        [ext] * 5 + [ext4, ext, ext], cost_estimate=cost(1.5))
    packs = call(pack_columns_kernel, (*state[:3], near, far), [f32(3 * groups * SUB, LANES)] * 2)
    sides = exchange(*packs, "col")
    *state, sums = call(
        inner_rest_kernel, (packs[0], near, far, *state),
        [ext] * 5 + [ext4, ext, ext, f32(2 * len(PAIRS), SUB, LANES)],
        input_output_aliases={3 + k: k for k in range(8)}, cost_estimate=cost(4))
    f, c, p, v1, v2, w, faces, _center, row = call(
        margin_kernel, (*sides, sums, *state),
        [ext] * 5 + [ext4, ext, ext, everyones], input_output_aliases={3 + k: k for k in range(8)})
    vmem = lambda like: pltpu.VMEM(like.shape, jnp.float32)
    block = f32(rows, cols)
    value, u1, u2, row = call(
        density_kernel, (everyone(row), f, c, p, v1, v2, w, faces), [block, ext, ext, everyones],
        [vmem(ext), vmem(ext), vmem(block), pltpu.SemaphoreType.DMA], 1)
    density, ergodic = call(
        finish_kernel, (everyone(row), p, u1, u2), [block, f32(1, 1)])
    return value, density, ergodic[0, 0]


def solution(mesh):
    spec = P("row", "col")
    return jax.shard_map(body, mesh=mesh, in_specs=(spec,) * 4, out_specs=(spec, spec, P()), check_vma=False)
```

```python
import functools

import jax
import jax.numpy as jnp
from jax import lax
from jax.experimental import pallas as pl
from jax.experimental.pallas import tpu as pltpu
from jax.sharding import PartitionSpec as P

discount_rate = 0.05
diffusion = 0.25
SCALE = 0.0625
FACE = diffusion * 0.5 * SCALE
LANES = 128
SUB = 8
WIDE = 5
EDGE = 10
DEEP = 5
PAD = 2 * SUB
VMEM_BYTES = 16 * 2**20
VM = pl.BlockSpec(memory_space=pltpu.VMEM)
BOTH = ("row", "col")
CHAIN = 8


def two_sum(a, b):
    s = a + b
    t = s - a
    return s, (a - (s - t)) + (b - t)


def fast_sum(a, b):
    s = a + b
    return s, b - (s - a)


def halves(a):
    t = a * 4097.0
    hi = t - (t - a)
    return hi, a - hi


def two_prod(a, b):
    p = a * b
    ah, al = halves(a)
    bh, bl = halves(b)
    return p, ((ah * bh - p) + ah * bl + al * bh) + al * bl


def dmul(a, b):
    p, e = two_prod(a[0], b[0])
    return fast_sum(p, e + (a[0] * b[1] + a[1] * b[0]))


def dsub(a, b):
    s, e = two_sum(a[0], -b[0])
    return fast_sum(s, e + (a[1] - b[1]))


def ddiv(a, b):
    q = a[0] / b[0]
    r = dsub(a, dmul((q, jnp.zeros_like(q)), b))
    return fast_sum(q, r[0] / b[0])


def galerkin(dots):
    d00, d01, d02, d03, d11, d12, d13, d22, d23 = dots
    zero = jnp.zeros_like(d00[0])
    l1 = ddiv(d11, d01)
    l2 = ddiv(d12, d01)
    s11 = dsub(d12, dmul(l1, d02))
    s12 = dsub(d13, dmul(l1, d03))
    s21 = dsub(d22, dmul(l2, d02))
    s22 = dsub(d23, dmul(l2, d03))
    g0 = (d00[0] * SCALE, d00[1] * SCALE)
    g1 = dsub((d01[0] * SCALE, d01[1] * SCALE), dmul(l1, g0))
    g2 = dsub((d02[0] * SCALE, d02[1] * SCALE), dmul(l2, g0))
    l3 = ddiv(s21, s11)
    t22 = dsub(s22, dmul(l3, s12))
    g2 = dsub(g2, dmul(l3, g1))
    full1 = s11[0] > 1e-12 * d12[0]
    full2 = full1 & (t22[0] > 1e-12 * d23[0])
    c2 = jnp.where(full2, g2[0] / t22[0], zero)
    c1 = dsub(g1, dmul(s12, (c2, zero)))[0] / s11[0]
    c1 = jnp.where(full1, c1, zero)
    r0 = dsub(dsub(g0, dmul(d02, (c1, zero))), dmul(d03, (c2, zero)))
    return r0[0] / d01[0], c1, c2


PAIRS = ((0, 0), (0, 1), (0, 2), (0, 3), (1, 1), (1, 2), (1, 3), (2, 2), (2, 3))


def split_short(a):
    t = a * 65537.0
    hi = t - (t - a)
    return hi, a - hi


def dot_step(groups, sums):
    mains, rests = [None] * len(PAIRS), [None] * len(PAIRS)
    for vs in groups:
        parts = [split_short(v) for v in vs]
        for k, (i, j) in enumerate(PAIRS):
            m = parts[i][0] * parts[j][0]
            if i == j:
                r = parts[i][1] * (vs[i] + parts[i][0])
            else:
                r = parts[i][0] * parts[j][1] + parts[i][1] * vs[j]
            mains[k] = m if mains[k] is None else mains[k] + m
            rests[k] = r if rests[k] is None else rests[k] + r
    out = []
    for k, (main, rest) in enumerate(zip(mains, rests)):
        s, e = two_sum(sums[2 * k], main)
        out += [s, sums[2 * k + 1] + (e + rest)]
    return tuple(out)


def pack_sums(sums, extra=()):
    lane = lax.broadcasted_iota(jnp.int32, (1, LANES), 1)
    row = jnp.zeros((1, LANES), jnp.float32)
    total = lambda a: jnp.sum(jnp.sum(a, axis=0, keepdims=True), axis=1, keepdims=True)
    for k in range(len(PAIRS)):
        s, e = sums[2 * k], sums[2 * k + 1]
        peak = jnp.max(jnp.max(jnp.abs(s), axis=0, keepdims=True), axis=1, keepdims=True)
        lift = jnp.broadcast_to(peak * 2048.0, s.shape)
        main = (s + lift) - lift
        row = jnp.where(lane == k, total(main), row)
        row = jnp.where(lane == 64 + k, total((s - main) + e), row)
    for k, a in enumerate(extra):
        row = jnp.where(lane == len(PAIRS) + k, total(a), row)
    return row


def gathered_sums(ref, extra=0):
    rows = [(ref[d], None) for d in range(ref.shape[0])]
    while len(rows) > 1:
        merged = []
        for k in range(0, len(rows) - 1, 2):
            (a, ea), (b, eb) = rows[k], rows[k + 1]
            s, e = two_sum(a, b)
            e = e if ea is None else e + (ea + eb)
            merged.append((s, e))
        if len(rows) % 2:
            a, ea = rows[-1]
            merged.append((a, jnp.zeros_like(a) if ea is None else ea))
        rows = merged
    s, e = rows[0]
    lane = lax.broadcasted_iota(jnp.int32, s.shape, 1)
    pick = lambda a, k: jnp.sum(jnp.where(lane == k, a, 0.0), axis=1, keepdims=True)
    dots = []
    for k in range(len(PAIRS)):
        hi = pick(s, k)
        lo = pick(e, k) + pick(s, 64 + k)
        dots.append(fast_sum(hi, lo))
    return dots, [pick(s, len(PAIRS) + k) for k in range(extra)]


FIRST = EDGE + 2 * WIDE


def fields_of(rc, cx, cy):
    control_cost = 0.5 * (cx * cx + cy * cy)
    return rc + control_cost, 1.0 + control_cost


def edge_rows(rc, cx, cy, pd):
    rows, cols = rc.shape
    few = WIDE - 2
    gap = jnp.zeros((2 * SUB - 2 * WIDE - few, cols), jnp.float32)
    ends = [[x[:SUB] for x in (rc, cx, cy, pd)], [x[rows - SUB :] for x in (rc, cx, cy, pd)]]
    (f, c, p), (g, d, q) = lax.optimization_barrier([(*fields_of(*x[:3]), x[3]) for x in ends])
    up = jnp.concatenate([p[:few], f[:WIDE], c[:WIDE], gap])
    return up, jnp.concatenate([gap, d[SUB - WIDE :], g[SUB - WIDE :], q[SUB - few :]])


def neighbours_along(axis):
    i = lax.axis_index(axis)
    return i > 0, i < lax.axis_size(axis) - 1


def is_even(axis):
    return lax.rem(lax.axis_index(axis), 2) == 0


def lanes():
    return lax.broadcasted_iota(jnp.int32, (SUB, LANES), 1)


def tile_cols(j):
    return slice(j * LANES, (j + 1) * LANES)


def halo_tile(refs, field, j, south):
    at = ((3, 8, 0) if south else (5, 0, 8))[field]
    first, second = [ref[at : at + SUB, tile_cols(j)] for ref in refs]
    tile = jnp.where(is_even("row"), first, second) if south else jnp.where(is_even("row"), second, first)
    return jnp.where(neighbours_along("row")[int(south)], tile, 0.0)


def packing(tiles):
    per = LANES // (2 * WIDE)
    return per, -(-tiles // per)


def pack_columns_kernel(f_ref, c_ref, p_ref, near_ref, far_ref, first_ref, second_ref):
    tiles = row_tiles(f_ref)
    per, groups = packing(tiles)
    end = p_ref.shape[0] - 2
    lane = lanes()
    even = is_even("col")
    for field in range(3):

        def tile(j, t):
            if t == 0:
                return halo_tile((near_ref, far_ref), field, j, False)
            if t == tiles - 1:
                return halo_tile((near_ref, far_ref), field, j, True)
            return (f_ref, c_ref, p_ref)[field][j, (t + 1) * SUB : (t + 2) * SUB]

        for v in range(groups):
            west = jnp.zeros((SUB, LANES), jnp.float32)
            east = west
            for g in range(min(per, tiles - v * per)):
                at = 2 * WIDE * g
                a, b = tile(0, v * per + g), tile(end, v * per + g)
                west = jnp.where((lane >= at) & (lane < at + WIDE), pltpu.roll(a, at, 1), west)
                there = (lane >= at + WIDE) & (lane < at + 2 * WIDE)
                east = jnp.where(there, pltpu.roll(b, (at + 2 * WIDE) % LANES, 1), east)
            at = (field * groups + v) * SUB
            first_ref[at : at + SUB] = jnp.where(even, east, west)
            second_ref[at : at + SUB] = jnp.where(even, west, east)


def beside(ref, r, which):
    lane = lanes()
    n = len(which)
    here = [ref[j, pl.ds(r, SUB), :] for j in which]
    south = [ref[j, pl.ds(r + 1, SUB), :] for j in which]
    north = [ref[j, pl.ds(r - 1, SUB), :] for j in which]
    east = [pltpu.roll(a, LANES - 1, 1) for a in here]
    west = [pltpu.roll(a, 1, 1) for a in here]
    if n > 1:
        east, west = (
            [jnp.where(lane == LANES - 1, east[(k + 1) % n], east[k]) for k in range(n)],
            [jnp.where(lane == 0, west[k - 1], west[k]) for k in range(n)],
        )
    return [dict(zip(which, x)) for x in (here, south, north, east, west)]


def beside_all(ref, r, parts):
    found = [beside(ref, r, which) for which in parts]
    return [{j: x for part in found for j, x in part[k].items()} for k in range(5)]


def weighted_apply(center, w, cells):
    here, south, north, east, west = cells
    return center * here - ((w[0] * south + w[1] * north) + (w[2] * east + w[3] * west))


def apply_tiles(ref, w_ref, center_ref, r, parts):
    cells = beside_all(ref, r, parts)
    at = pl.ds(r, SUB)
    out = {}
    for j in cells[0]:
        w = [w_ref[k, j, at, :] for k in range(4)]
        out[j] = weighted_apply(center_ref[j, at, :], w, [c[j] for c in cells])
    return out, cells[0]


def first_vector(f_ref, c_ref, v1_ref, w_ref, faces_ref, center_ref, r, which):
    at = pl.ds(r, SUB)
    cond = beside(c_ref, r, which)
    cells = beside(f_ref, r, which)
    out = []
    for j in which:
        c = cond[0][j]
        inside = jnp.minimum(c, 1.0)
        face = inside * FACE
        w = [face * (c + cond[k][j]) for k in (1, 2, 3, 4)]
        faces = (w[0] + w[1]) + (w[2] + w[3])
        center = inside * (discount_rate * SCALE) + faces
        out += [(w_ref.at[k], j, at, w[k]) for k in range(4)]
        out.append((faces_ref, j, at, faces))
        out.append((center_ref, j, at, center))
        out.append((v1_ref, j, at, weighted_apply(center, w, [x[j] for x in cells])))
    return out


def clear_pads(refs, which):
    zero = jnp.zeros((SUB, LANES), jnp.float32)
    for ref in refs:
        rows = ref.shape[1]
        for j in which:
            ref[j, 0:SUB] = zero
            ref[j, rows - SUB : rows] = zero


def row_tiles(ref):
    return (ref.shape[1] - 2 * SUB) // SUB


def sweep(start, stop, step, unroll=2):
    def group(rows):
        stores = [store for r in rows for store in step(r)]
        for ref, j, at, value in stores:
            ref[j, at, :] = value

    def some(t, _):
        base = start + t * unroll
        group([pl.multiple_of(SUB + (base + u) * SUB, SUB) for u in range(unroll)])
        return 0

    whole = (stop - start) // unroll
    lax.fori_loop(0, whole, some, 0)
    rest = range(start + whole * unroll, stop)
    if len(rest):
        group([SUB + t * SUB for t in rest])


def second_vector(v1_ref, v2_ref, w_ref, center_ref, parts, unroll=17, start=0, stop=None):
    def step(r):
        out, _here = apply_tiles(v1_ref, w_ref, center_ref, r, parts)
        return [(v2_ref, j, pl.ds(r, SUB), x) for j, x in out.items()]

    sweep(start, row_tiles(v1_ref) if stop is None else stop, step, unroll)


def no_sums():
    return (jnp.zeros((SUB, LANES), jnp.float32),) * (2 * len(PAIRS))


def own_products(v0_ref, v1_ref, v2_ref, w_ref, center_ref, sums, unroll=4):
    own = list(range(v0_ref.shape[0] - 1))
    lane = lanes()

    def step(t, sums):
        groups = []
        for u in range(unroll):
            r = pl.multiple_of(PAD + (t * unroll + u) * SUB, SUB)
            out, here = apply_tiles(v2_ref, w_ref, center_ref, r, [own])
            at = pl.ds(r, SUB)
            for j in own:
                vs = [v0_ref[j, at, :], v1_ref[j, at, :], here[j]]
                if j == 0:
                    vs = [jnp.where(lane >= DEEP, v, 0.0) for v in vs]
                if j == own[-1]:
                    vs = [jnp.where(lane < LANES - DEEP, v, 0.0) for v in vs]
                groups.append((*vs, out[j]))
        for k in range(0, len(groups), CHAIN):
            sums = dot_step(groups[k : k + CHAIN], sums)
        return sums

    return lax.fori_loop(0, (row_tiles(v0_ref) - 2) // unroll, step, sums)


def margin_products(v0_ref, v1_ref, v2_ref, w_ref, center_ref, sums):
    margin = v0_ref.shape[0] - 1
    lane = lanes()
    span = FIRST + DEEP - (EDGE - DEEP)
    runs = (FIRST - EDGE + DEEP) // DEEP
    block = span + (runs - 1) * DEEP
    slots = [block * b + DEEP * k for b in range(LANES // block) for k in range(runs)]
    tiles = row_tiles(v0_ref) - 2
    groups = []
    for start in range(0, tiles, len(slots)):
        packed = None
        for t, slot in zip(range(start, tiles), slots):
            at = slice(PAD + t * SUB, PAD + (t + 1) * SUB)
            out, here = apply_tiles(v2_ref, w_ref, center_ref, PAD + t * SUB, [[margin]])
            vs = [v0_ref[margin, at], v1_ref[margin, at], here[margin], out[margin]]
            put = (slot - (EDGE - DEEP)) % LANES
            vs = [pltpu.roll(v, put, 1) if put else v for v in vs]
            low, high = slot, slot + span - DEEP
            mask = ((lane >= low) & (lane < low + DEEP)) | ((lane >= high) & (lane < high + DEEP))
            if packed is None:
                packed = [jnp.where(mask, v, 0.0) for v in vs]
            else:
                packed = [jnp.where(mask, v, x) for v, x in zip(vs, packed)]
        groups.append(tuple(packed))
    return dot_step(groups, sums)


def with_sides(tile, side, j, count):
    lane = lanes()
    if j == 0:
        tile = jnp.where(lane < DEEP, pltpu.roll(side, LANES - FIRST, 1), tile)
    if j == count - 1:
        tile = jnp.where(lane >= LANES - DEEP, pltpu.roll(side, LANES - EDGE, 1), tile)
    return tile


def repeat_sides(ref, t):
    count = ref.shape[0] - 1
    lane = lanes()
    at = slice((t + 1) * SUB, (t + 2) * SUB)
    last = pltpu.roll(ref[count - 1, at], EDGE, 1)
    first = pltpu.roll(ref[0, at], FIRST, 1)
    keep = (lane >= FIRST) & (lane < FIRST + EDGE)
    ref[count, at] = jnp.where(lane < EDGE, last, jnp.where(keep, first, 0.0))


def inner_first_kernel(f_in, c_in, p_in,
                       f_ref, c_ref, p_ref, v1_ref, v2_ref, w_ref, faces_ref, center_ref):
    own = list(range(f_ref.shape[0] - 1))
    rows = f_in.shape[0]
    tiles = row_tiles(f_ref)
    clear_pads((f_ref, c_ref, p_ref, v1_ref, v2_ref), own)
    for ref, source in ((f_ref, f_in), (c_ref, c_in), (p_ref, p_in)):
        for j in own:
            ref[j, PAD : PAD + rows] = source[:, tile_cols(j)]
        for t in range(1, tiles - 1):
            repeat_sides(ref, t)
    sweep(2, tiles - 2,
          lambda r: first_vector(f_ref, c_ref, v1_ref, w_ref, faces_ref, center_ref, r, own), 6)
    second_vector(v1_ref, v2_ref, w_ref, center_ref, [own], 7, 3, tiles - 3)


def inner_rest_kernel(after, near_ref, far_ref, f_in, c_in, p_in, v1_in, v2_in, w_in, faces_in, center_in,
                      f_ref, c_ref, p_ref, v1_ref, v2_ref, w_ref, faces_ref, center_ref, sums_ref):
    own = list(range(f_ref.shape[0] - 1))
    rows = f_ref.shape[1]
    tiles = row_tiles(f_ref)
    for field, ref in enumerate((f_ref, c_ref, p_ref)):
        for j in own:
            ref[j, SUB : 2 * SUB] = halo_tile((near_ref, far_ref), field, j, False)
            ref[j, rows - 2 * SUB : rows - SUB] = halo_tile((near_ref, far_ref), field, j, True)
        repeat_sides(ref, 0)
        repeat_sides(ref, tiles - 1)
    for start in (0, tiles - 2):
        sweep(start, start + 2,
              lambda r: first_vector(f_ref, c_ref, v1_ref, w_ref, faces_ref, center_ref, r, own))
    for start in (0, tiles - 3):
        second_vector(v1_ref, v2_ref, w_ref, center_ref, [own], 3, start, start + 3)
    sums = own_products(f_ref, v1_ref, v2_ref, w_ref, center_ref, no_sums())
    for k, a in enumerate(sums):
        sums_ref[k] = a


def margin_kernel(near_ref, far_ref, sums_in, f_in, c_in, p_in, v1_in, v2_in, w_in, faces_in, center_in,
                  f_ref, c_ref, p_ref, v1_ref, v2_ref, w_ref, faces_ref, center_ref, row_ref):
    count = f_ref.shape[0] - 1
    tiles = row_tiles(f_ref)
    per, groups = packing(tiles)
    lane = lanes()
    has_west, has_east = neighbours_along("col")
    even = is_even("col")
    from_east = lax.rem(lane, 2 * WIDE) < WIDE
    halo = (lane >= EDGE) & (lane < FIRST)
    clear_pads((f_ref, c_ref, p_ref, v1_ref, v2_ref), [count])
    for field, ref in enumerate((f_ref, c_ref, p_ref)):
        for v in range(groups):
            src = slice((field * groups + v) * SUB, (field * groups + v + 1) * SUB)
            near, far = near_ref[src], far_ref[src]
            east = jnp.where(has_east, jnp.where(even, near, far), 0.0)
            west = jnp.where(has_west, jnp.where(even, far, near), 0.0)
            both = jnp.where(from_east, east, west)
            for g in range(min(per, tiles - v * per)):
                t = v * per + g
                at = slice(SUB + t * SUB, 2 * SUB + t * SUB)
                ref[count, at] = jnp.where(halo, pltpu.roll(both, (EDGE - 2 * WIDE * g) % LANES, 1), ref[count, at])
    sweep(0, tiles, lambda r: first_vector(
        f_ref, c_ref, v1_ref, w_ref, faces_ref, center_ref, r, [count]), 17)
    second_vector(v1_ref, v2_ref, w_ref, center_ref, [[count]], 17)
    sums = tuple(sums_in[k] for k in range(2 * len(PAIRS)))
    sums = margin_products(f_ref, v1_ref, v2_ref, w_ref, center_ref, sums)
    row_ref[...] = jnp.broadcast_to(pack_sums(sums)[None], row_ref.shape)


def density_kernel(rows_ref, f_ref, c_ref, p_ref, v1_ref, v2_ref, w_ref, faces_ref,
                   value_out, u1_ref, u2_ref, row_ref, vx_ref, center_ref, value_ref, sem):
    dots, _unused = gathered_sums(rows_ref)
    c0, c1, c2 = [jnp.broadcast_to(c, (SUB, LANES)) for c in galerkin(dots)]
    which = list(range(f_ref.shape[0]))
    own = which[:-1]
    parts = [own, which[-1:]]
    tiles = row_tiles(f_ref)
    clear_pads((vx_ref, u1_ref, u2_ref), which)

    def value(r):
        at = pl.ds(r, SUB)
        return [
            (vx_ref, j, at, (c0 * f_ref[j, at, :] + c1 * v1_ref[j, at, :]) + c2 * v2_ref[j, at, :])
            for j in which
        ]

    sweep(0, tiles, value, 4)

    def first(r):
        at = pl.ds(r, SUB)
        val = beside_all(vx_ref, r, parts)
        cells = beside_all(p_ref, r, parts)
        out = []
        for j in which:
            inside = jnp.minimum(c_ref[j, at, :], 1.0)
            slope_row = 0.5 * (val[1][j] - val[2][j])
            slope_col = 0.5 * (val[3][j] - val[4][j])
            congestion = (slope_row * slope_row + slope_col * slope_col) * (0.5 / diffusion)
            zeroth = (discount_rate + congestion) * SCALE
            center = inside * zeroth + faces_ref[j, at, :]
            w = [w_ref[k, j, at, :] for k in range(4)]
            out.append((center_ref, j, at, center))
            out.append((u1_ref, j, at, weighted_apply(center, w, [x[j] for x in cells])))
        return out

    sweep(0, tiles, first, 17)

    def outer(t, sums):
        cost, weight = [list(x) for x in sums]
        for u in range(8):
            at = pl.ds(pl.multiple_of(PAD + (8 * t + u) * SUB, SUB), SUB)
            to = pl.ds(pl.multiple_of((8 * t + u) * SUB, SUB), SUB)
            for j in own:
                v = with_sides(vx_ref[j, at, :], vx_ref[len(own), at, :], j, len(own))
                p = p_ref[j, at, :]
                value_ref[to, tile_cols(j)] = v
                cost[j] = cost[j] + p * (f_ref[j, at, :] - discount_rate * v)
                weight[j] = weight[j] + p
        return tuple(cost), tuple(weight)

    zeros = (jnp.zeros((SUB, LANES), jnp.float32),) * len(own)
    extra = [sum(x) for x in lax.fori_loop(0, (tiles - 2) // 8, outer, (zeros, zeros))]
    copy = pltpu.make_async_copy(value_ref, value_out, sem)
    copy.start()
    second_vector(u1_ref, u2_ref, w_ref, center_ref, parts)
    sums = own_products(p_ref, u1_ref, u2_ref, w_ref, center_ref, no_sums())
    sums = margin_products(p_ref, u1_ref, u2_ref, w_ref, center_ref, sums)
    row_ref[...] = jnp.broadcast_to(pack_sums(sums, extra)[None], row_ref.shape)
    copy.wait()


def finish_kernel(rows_ref, p_ref, u1_ref, u2_ref, density_ref, ergodic_ref):
    dots, (cost, weight) = gathered_sums(rows_ref, 2)
    ergodic_ref[...] = cost / weight
    c0, c1, c2 = [jnp.broadcast_to(c, (SUB, LANES)) for c in galerkin(dots)]
    count = p_ref.shape[0] - 1

    unroll = 8

    def some(t, _):
        for u in range(unroll):
            at = pl.ds(pl.multiple_of(PAD + (unroll * t + u) * SUB, SUB), SUB)
            to = pl.ds(pl.multiple_of((unroll * t + u) * SUB, SUB), SUB)
            made = [(c0 * p_ref[j, at, :] + c1 * u1_ref[j, at, :]) + c2 * u2_ref[j, at, :] for j in range(count + 1)]
            for j in range(count):
                density_ref[to, tile_cols(j)] = with_sides(made[j], made[count], j, count)
        return 0

    lax.fori_loop(0, density_ref.shape[0] // (unroll * SUB), some, 0)


def f32(*shape):
    return jax.ShapeDtypeStruct(shape, jnp.float32)


def exchange(near, far, axis):
    n = lax.axis_size(axis)
    assert n % 2 == 0
    near = lax.ppermute(near, axis, [(i, i ^ 1) for i in range(n)])
    far = lax.ppermute(far, axis, [(i, (((i + 1) % n ^ 1) - 1) % n) for i in range(n)])
    return near, far


def everyone(row):
    return lax.all_to_all(row, BOTH, 0, 0, tiled=True)


def body(*args):
    rows, cols = args[0].shape
    devices = lax.axis_size("row") * lax.axis_size("col")
    count = cols // LANES
    ext = f32(count + 1, rows + 2 * PAD, LANES)
    ext4 = f32(4, *ext.shape)
    everyones = f32(devices, 1, LANES)
    _per, groups = packing(rows // SUB + 2)
    small = pltpu.CompilerParams(vmem_limit_bytes=VMEM_BYTES)

    def call(kernel, ins, outs, scratch=(), to_hbm=0, **more):
        return pl.pallas_call(
            kernel,
            in_specs=[VM] * len(ins),
            out_specs=[pl.BlockSpec(memory_space=pltpu.HBM)] * to_hbm + [VM] * (len(outs) - to_hbm),
            out_shape=outs,
            scratch_shapes=scratch,
            compiler_params=small,
            **more,
        )(*ins)

    cost = lambda us: pl.CostEstimate(flops=0, bytes_accessed=int(us * 2e6), transcendentals=0)
    up, down = edge_rows(*args)
    even = is_even("row")
    near, far = exchange(jnp.where(even, down, up), jnp.where(even, up, down), "row")
    forcing, conduct = fields_of(*args[:3])
    prior = args[3]
    state = call(
        inner_first_kernel, (forcing, conduct, prior),
        [ext] * 5 + [ext4, ext, ext], cost_estimate=cost(1.5))
    packs = call(pack_columns_kernel, (*state[:3], near, far), [f32(3 * groups * SUB, LANES)] * 2)
    sides = exchange(*packs, "col")
    *state, sums = call(
        inner_rest_kernel, (packs[0], near, far, *state),
        [ext] * 5 + [ext4, ext, ext, f32(2 * len(PAIRS), SUB, LANES)],
        input_output_aliases={3 + k: k for k in range(8)}, cost_estimate=cost(4))
    f, c, p, v1, v2, w, faces, _center, row = call(
        margin_kernel, (*sides, sums, *state),
        [ext] * 5 + [ext4, ext, ext, everyones], input_output_aliases={3 + k: k for k in range(8)})
    vmem = lambda like: pltpu.VMEM(like.shape, jnp.float32)
    block = f32(rows, cols)
    value, u1, u2, row = call(
        density_kernel, (everyone(row), f, c, p, v1, v2, w, faces), [block, ext, ext, everyones],
        [vmem(ext), vmem(ext), vmem(block), pltpu.SemaphoreType.DMA], 1)
    density, ergodic = call(
        finish_kernel, (everyone(row), p, u1, u2), [block, f32(1, 1)])
    return value, density, ergodic[0, 0]


def solution(mesh):
    spec = P("row", "col")
    return jax.shard_map(body, mesh=mesh, in_specs=(spec,) * 4, out_specs=(spec, spec, P()), check_vma=False)
```

```python
import functools

import jax
import jax.numpy as jnp
from jax import lax
from jax.experimental import pallas as pl
from jax.experimental.pallas import tpu as pltpu
from jax.sharding import PartitionSpec as P

discount_rate = 0.05
diffusion = 0.25
SCALE = 0.0625
FACE = diffusion * 0.5 * SCALE
LANES = 128
SUB = 8
WIDE = 5
EDGE = 10
DEEP = 5
PAD = 2 * SUB
VMEM_BYTES = 16 * 2**20
VM = pl.BlockSpec(memory_space=pltpu.VMEM)
BOTH = ("row", "col")
CHAIN = 8


def two_sum(a, b):
    s = a + b
    t = s - a
    return s, (a - (s - t)) + (b - t)


def fast_sum(a, b):
    s = a + b
    return s, b - (s - a)


def halves(a):
    t = a * 4097.0
    hi = t - (t - a)
    return hi, a - hi


def two_prod(a, b):
    p = a * b
    ah, al = halves(a)
    bh, bl = halves(b)
    return p, ((ah * bh - p) + ah * bl + al * bh) + al * bl


def dmul(a, b):
    p, e = two_prod(a[0], b[0])
    return fast_sum(p, e + (a[0] * b[1] + a[1] * b[0]))


def dsub(a, b):
    s, e = two_sum(a[0], -b[0])
    return fast_sum(s, e + (a[1] - b[1]))


def ddiv(a, b):
    q = a[0] / b[0]
    r = dsub(a, dmul((q, jnp.zeros_like(q)), b))
    return fast_sum(q, r[0] / b[0])


def galerkin(dots):
    d00, d01, d02, d03, d11, d12, d13, d22, d23 = dots
    zero = jnp.zeros_like(d00[0])
    l1 = ddiv(d11, d01)
    l2 = ddiv(d12, d01)
    s11 = dsub(d12, dmul(l1, d02))
    s12 = dsub(d13, dmul(l1, d03))
    s21 = dsub(d22, dmul(l2, d02))
    s22 = dsub(d23, dmul(l2, d03))
    g0 = (d00[0] * SCALE, d00[1] * SCALE)
    g1 = dsub((d01[0] * SCALE, d01[1] * SCALE), dmul(l1, g0))
    g2 = dsub((d02[0] * SCALE, d02[1] * SCALE), dmul(l2, g0))
    l3 = ddiv(s21, s11)
    t22 = dsub(s22, dmul(l3, s12))
    g2 = dsub(g2, dmul(l3, g1))
    full1 = s11[0] > 1e-12 * d12[0]
    full2 = full1 & (t22[0] > 1e-12 * d23[0])
    c2 = jnp.where(full2, g2[0] / t22[0], zero)
    c1 = dsub(g1, dmul(s12, (c2, zero)))[0] / s11[0]
    c1 = jnp.where(full1, c1, zero)
    r0 = dsub(dsub(g0, dmul(d02, (c1, zero))), dmul(d03, (c2, zero)))
    return r0[0] / d01[0], c1, c2


PAIRS = ((0, 0), (0, 1), (0, 2), (0, 3), (1, 1), (1, 2), (1, 3), (2, 2), (2, 3))


def split_short(a):
    t = a * 65537.0
    hi = t - (t - a)
    return hi, a - hi


def dot_step(groups, sums):
    mains, rests = [None] * len(PAIRS), [None] * len(PAIRS)
    for vs in groups:
        parts = [split_short(v) for v in vs]
        for k, (i, j) in enumerate(PAIRS):
            m = parts[i][0] * parts[j][0]
            if i == j:
                r = parts[i][1] * (vs[i] + parts[i][0])
            else:
                r = parts[i][0] * parts[j][1] + parts[i][1] * vs[j]
            mains[k] = m if mains[k] is None else mains[k] + m
            rests[k] = r if rests[k] is None else rests[k] + r
    out = []
    for k, (main, rest) in enumerate(zip(mains, rests)):
        s, e = two_sum(sums[2 * k], main)
        out += [s, sums[2 * k + 1] + (e + rest)]
    return tuple(out)


def pack_sums(sums, extra=()):
    lane = lax.broadcasted_iota(jnp.int32, (1, LANES), 1)
    row = jnp.zeros((1, LANES), jnp.float32)
    total = lambda a: jnp.sum(jnp.sum(a, axis=0, keepdims=True), axis=1, keepdims=True)
    for k in range(len(PAIRS)):
        s, e = sums[2 * k], sums[2 * k + 1]
        peak = jnp.max(jnp.max(jnp.abs(s), axis=0, keepdims=True), axis=1, keepdims=True)
        lift = jnp.broadcast_to(peak * 2048.0, s.shape)
        main = (s + lift) - lift
        row = jnp.where(lane == k, total(main), row)
        row = jnp.where(lane == 64 + k, total((s - main) + e), row)
    for k, a in enumerate(extra):
        row = jnp.where(lane == len(PAIRS) + k, total(a), row)
    return row


def gathered_sums(ref, extra=0):
    rows = [(ref[d], None) for d in range(ref.shape[0])]
    while len(rows) > 1:
        merged = []
        for k in range(0, len(rows) - 1, 2):
            (a, ea), (b, eb) = rows[k], rows[k + 1]
            s, e = two_sum(a, b)
            e = e if ea is None else e + (ea + eb)
            merged.append((s, e))
        if len(rows) % 2:
            a, ea = rows[-1]
            merged.append((a, jnp.zeros_like(a) if ea is None else ea))
        rows = merged
    s, e = rows[0]
    lane = lax.broadcasted_iota(jnp.int32, s.shape, 1)
    pick = lambda a, k: jnp.sum(jnp.where(lane == k, a, 0.0), axis=1, keepdims=True)
    dots = []
    for k in range(len(PAIRS)):
        hi = pick(s, k)
        lo = pick(e, k) + pick(s, 64 + k)
        dots.append(fast_sum(hi, lo))
    return dots, [pick(s, len(PAIRS) + k) for k in range(extra)]


FIRST = EDGE + 2 * WIDE


def fields_of(rc, cx, cy):
    control_cost = 0.5 * (cx * cx + cy * cy)
    return rc + control_cost, 1.0 + control_cost


def edge_rows(rc, cx, cy, pd):
    rows, cols = rc.shape
    few = WIDE - 2
    gap = jnp.zeros((2 * SUB - 2 * WIDE - few, cols), jnp.float32)
    ends = [[x[:SUB] for x in (rc, cx, cy, pd)], [x[rows - SUB :] for x in (rc, cx, cy, pd)]]
    (f, c, p), (g, d, q) = lax.optimization_barrier([(*fields_of(*x[:3]), x[3]) for x in ends])
    up = jnp.concatenate([p[:few], f[:WIDE], c[:WIDE], gap])
    return up, jnp.concatenate([gap, d[SUB - WIDE :], g[SUB - WIDE :], q[SUB - few :]])


def neighbours_along(axis):
    i = lax.axis_index(axis)
    return i > 0, i < lax.axis_size(axis) - 1


def is_even(axis):
    return lax.rem(lax.axis_index(axis), 2) == 0


def even_share(n, most):
    return max(d for d in range(1, most + 1) if n % d == 0)


def lanes():
    return lax.broadcasted_iota(jnp.int32, (SUB, LANES), 1)


def tile_cols(j):
    return slice(j * LANES, (j + 1) * LANES)


def halo_tile(refs, field, j, south):
    at = ((3, 8, 0) if south else (5, 0, 8))[field]
    first, second = [ref[at : at + SUB, tile_cols(j)] for ref in refs]
    tile = jnp.where(is_even("row"), first, second) if south else jnp.where(is_even("row"), second, first)
    return jnp.where(neighbours_along("row")[int(south)], tile, 0.0)


def packing(tiles):
    per = LANES // (2 * WIDE)
    return per, -(-tiles // per)


def pack_columns_kernel(f_ref, c_ref, p_ref, near_ref, far_ref, first_ref, second_ref):
    tiles = row_tiles(f_ref)
    per, groups = packing(tiles)
    end = p_ref.shape[0] - 2
    lane = lanes()
    even = is_even("col")
    for field in range(3):

        def tile(j, t):
            if t == 0:
                return halo_tile((near_ref, far_ref), field, j, False)
            if t == tiles - 1:
                return halo_tile((near_ref, far_ref), field, j, True)
            return (f_ref, c_ref, p_ref)[field][j, (t + 1) * SUB : (t + 2) * SUB]

        for v in range(groups):
            west = jnp.zeros((SUB, LANES), jnp.float32)
            east = west
            for g in range(min(per, tiles - v * per)):
                at = 2 * WIDE * g
                a, b = tile(0, v * per + g), tile(end, v * per + g)
                west = jnp.where((lane >= at) & (lane < at + WIDE), pltpu.roll(a, at, 1), west)
                there = (lane >= at + WIDE) & (lane < at + 2 * WIDE)
                east = jnp.where(there, pltpu.roll(b, (at + 2 * WIDE) % LANES, 1), east)
            at = (field * groups + v) * SUB
            first_ref[at : at + SUB] = jnp.where(even, east, west)
            second_ref[at : at + SUB] = jnp.where(even, west, east)


def beside(ref, r, which):
    lane = lanes()
    n = len(which)
    here = [ref[j, pl.ds(r, SUB), :] for j in which]
    south = [ref[j, pl.ds(r + 1, SUB), :] for j in which]
    north = [ref[j, pl.ds(r - 1, SUB), :] for j in which]
    east = [pltpu.roll(a, LANES - 1, 1) for a in here]
    west = [pltpu.roll(a, 1, 1) for a in here]
    if n > 1:
        east, west = (
            [jnp.where(lane == LANES - 1, east[(k + 1) % n], east[k]) for k in range(n)],
            [jnp.where(lane == 0, west[k - 1], west[k]) for k in range(n)],
        )
    return [dict(zip(which, x)) for x in (here, south, north, east, west)]


def beside_all(ref, r, parts):
    found = [beside(ref, r, which) for which in parts]
    return [{j: x for part in found for j, x in part[k].items()} for k in range(5)]


def weighted_apply(center, w, cells):
    here, south, north, east, west = cells
    return center * here - ((w[0] * south + w[1] * north) + (w[2] * east + w[3] * west))


def apply_tiles(ref, w_ref, center_ref, r, parts):
    cells = beside_all(ref, r, parts)
    at = pl.ds(r, SUB)
    out = {}
    for j in cells[0]:
        w = [w_ref[k, j, at, :] for k in range(4)]
        out[j] = weighted_apply(center_ref[j, at, :], w, [c[j] for c in cells])
    return out, cells[0]


def first_vector(f_ref, c_ref, v1_ref, w_ref, faces_ref, center_ref, r, which):
    at = pl.ds(r, SUB)
    cond = beside(c_ref, r, which)
    cells = beside(f_ref, r, which)
    out = []
    for j in which:
        c = cond[0][j]
        inside = jnp.minimum(c, 1.0)
        face = inside * FACE
        w = [face * (c + cond[k][j]) for k in (1, 2, 3, 4)]
        faces = (w[0] + w[1]) + (w[2] + w[3])
        center = inside * (discount_rate * SCALE) + faces
        out += [(w_ref.at[k], j, at, w[k]) for k in range(4)]
        out.append((faces_ref, j, at, faces))
        out.append((center_ref, j, at, center))
        out.append((v1_ref, j, at, weighted_apply(center, w, [x[j] for x in cells])))
    return out


def clear_pads(refs, which):
    zero = jnp.zeros((SUB, LANES), jnp.float32)
    for ref in refs:
        rows = ref.shape[1]
        for j in which:
            ref[j, 0:SUB] = zero
            ref[j, rows - SUB : rows] = zero


def row_tiles(ref):
    return (ref.shape[1] - 2 * SUB) // SUB


def sweep(start, stop, step, unroll=2):
    def group(rows):
        stores = [store for r in rows for store in step(r)]
        for ref, j, at, value in stores:
            ref[j, at, :] = value

    def some(t, _):
        base = start + t * unroll
        group([pl.multiple_of(SUB + (base + u) * SUB, SUB) for u in range(unroll)])
        return 0

    whole = (stop - start) // unroll
    lax.fori_loop(0, whole, some, 0)
    rest = range(start + whole * unroll, stop)
    if len(rest):
        group([SUB + t * SUB for t in rest])


def second_vector(v1_ref, v2_ref, w_ref, center_ref, parts, unroll=34, start=0, stop=None):
    def step(r):
        out, _here = apply_tiles(v1_ref, w_ref, center_ref, r, parts)
        return [(v2_ref, j, pl.ds(r, SUB), x) for j, x in out.items()]

    sweep(start, row_tiles(v1_ref) if stop is None else stop, step, unroll)


def no_sums():
    return (jnp.zeros((SUB, LANES), jnp.float32),) * (2 * len(PAIRS))


def own_products(v0_ref, v1_ref, v2_ref, w_ref, center_ref, sums, most=8):
    own = list(range(v0_ref.shape[0] - 1))
    lane = lanes()
    unroll = even_share(row_tiles(v0_ref) - 2, most)

    def step(t, sums):
        groups = []
        for u in range(unroll):
            r = pl.multiple_of(PAD + (t * unroll + u) * SUB, SUB)
            out, here = apply_tiles(v2_ref, w_ref, center_ref, r, [own])
            at = pl.ds(r, SUB)
            for j in own:
                vs = [v0_ref[j, at, :], v1_ref[j, at, :], here[j]]
                if j == 0:
                    vs = [jnp.where(lane >= DEEP, v, 0.0) for v in vs]
                if j == own[-1]:
                    vs = [jnp.where(lane < LANES - DEEP, v, 0.0) for v in vs]
                groups.append((*vs, out[j]))
        for k in range(0, len(groups), CHAIN):
            sums = dot_step(groups[k : k + CHAIN], sums)
        return sums

    return lax.fori_loop(0, (row_tiles(v0_ref) - 2) // unroll, step, sums)


def margin_products(v0_ref, v1_ref, v2_ref, w_ref, center_ref, sums):
    margin = v0_ref.shape[0] - 1
    lane = lanes()
    span = FIRST + DEEP - (EDGE - DEEP)
    runs = (FIRST - EDGE + DEEP) // DEEP
    block = span + (runs - 1) * DEEP
    slots = [block * b + DEEP * k for b in range(LANES // block) for k in range(runs)]
    tiles = row_tiles(v0_ref) - 2
    groups = []
    for start in range(0, tiles, len(slots)):
        packed = None
        for t, slot in zip(range(start, tiles), slots):
            at = slice(PAD + t * SUB, PAD + (t + 1) * SUB)
            out, here = apply_tiles(v2_ref, w_ref, center_ref, PAD + t * SUB, [[margin]])
            vs = [v0_ref[margin, at], v1_ref[margin, at], here[margin], out[margin]]
            put = (slot - (EDGE - DEEP)) % LANES
            vs = [pltpu.roll(v, put, 1) if put else v for v in vs]
            low, high = slot, slot + span - DEEP
            mask = ((lane >= low) & (lane < low + DEEP)) | ((lane >= high) & (lane < high + DEEP))
            if packed is None:
                packed = [jnp.where(mask, v, 0.0) for v in vs]
            else:
                packed = [jnp.where(mask, v, x) for v, x in zip(vs, packed)]
        groups.append(tuple(packed))
    return dot_step(groups, sums)


def with_sides(tile, side, j, count):
    lane = lanes()
    if j == 0:
        tile = jnp.where(lane < DEEP, pltpu.roll(side, LANES - FIRST, 1), tile)
    if j == count - 1:
        tile = jnp.where(lane >= LANES - DEEP, pltpu.roll(side, LANES - EDGE, 1), tile)
    return tile


def repeat_sides(ref, t):
    count = ref.shape[0] - 1
    lane = lanes()
    at = slice((t + 1) * SUB, (t + 2) * SUB)
    last = pltpu.roll(ref[count - 1, at], EDGE, 1)
    first = pltpu.roll(ref[0, at], FIRST, 1)
    keep = (lane >= FIRST) & (lane < FIRST + EDGE)
    ref[count, at] = jnp.where(lane < EDGE, last, jnp.where(keep, first, 0.0))


def inner_first_kernel(f_in, c_in, p_in,
                       f_ref, c_ref, p_ref, v1_ref, v2_ref, w_ref, faces_ref, center_ref):
    own = list(range(f_ref.shape[0] - 1))
    rows = f_in.shape[0]
    tiles = row_tiles(f_ref)
    clear_pads((f_ref, c_ref, p_ref, v1_ref, v2_ref), own)
    for ref, source in ((f_ref, f_in), (c_ref, c_in), (p_ref, p_in)):
        for j in own:
            ref[j, PAD : PAD + rows] = source[:, tile_cols(j)]
        for t in range(1, tiles - 1):
            repeat_sides(ref, t)
    sweep(2, tiles - 2,
          lambda r: first_vector(f_ref, c_ref, v1_ref, w_ref, faces_ref, center_ref, r, own), 15)
    second_vector(v1_ref, v2_ref, w_ref, center_ref, [own], 14, 3, tiles - 3)


def inner_rest_kernel(after, near_ref, far_ref, f_in, c_in, p_in, v1_in, v2_in, w_in, faces_in, center_in,
                      f_ref, c_ref, p_ref, v1_ref, v2_ref, w_ref, faces_ref, center_ref, sums_ref):
    own = list(range(f_ref.shape[0] - 1))
    rows = f_ref.shape[1]
    tiles = row_tiles(f_ref)
    for field, ref in enumerate((f_ref, c_ref, p_ref)):
        for j in own:
            ref[j, SUB : 2 * SUB] = halo_tile((near_ref, far_ref), field, j, False)
            ref[j, rows - 2 * SUB : rows - SUB] = halo_tile((near_ref, far_ref), field, j, True)
        repeat_sides(ref, 0)
        repeat_sides(ref, tiles - 1)
    for start in (0, tiles - 2):
        sweep(start, start + 2,
              lambda r: first_vector(f_ref, c_ref, v1_ref, w_ref, faces_ref, center_ref, r, own))
    for start in (0, tiles - 3):
        second_vector(v1_ref, v2_ref, w_ref, center_ref, [own], 3, start, start + 3)
    sums = own_products(f_ref, v1_ref, v2_ref, w_ref, center_ref, no_sums())
    for k, a in enumerate(sums):
        sums_ref[k] = a


def margin_kernel(near_ref, far_ref, sums_in, f_in, c_in, p_in, v1_in, v2_in, w_in, faces_in, center_in,
                  f_ref, c_ref, p_ref, v1_ref, v2_ref, w_ref, faces_ref, center_ref, row_ref):
    count = f_ref.shape[0] - 1
    tiles = row_tiles(f_ref)
    per, groups = packing(tiles)
    lane = lanes()
    has_west, has_east = neighbours_along("col")
    even = is_even("col")
    from_east = lax.rem(lane, 2 * WIDE) < WIDE
    halo = (lane >= EDGE) & (lane < FIRST)
    clear_pads((f_ref, c_ref, p_ref, v1_ref, v2_ref), [count])
    for field, ref in enumerate((f_ref, c_ref, p_ref)):
        for v in range(groups):
            src = slice((field * groups + v) * SUB, (field * groups + v + 1) * SUB)
            near, far = near_ref[src], far_ref[src]
            east = jnp.where(has_east, jnp.where(even, near, far), 0.0)
            west = jnp.where(has_west, jnp.where(even, far, near), 0.0)
            both = jnp.where(from_east, east, west)
            for g in range(min(per, tiles - v * per)):
                t = v * per + g
                at = slice(SUB + t * SUB, 2 * SUB + t * SUB)
                ref[count, at] = jnp.where(halo, pltpu.roll(both, (EDGE - 2 * WIDE * g) % LANES, 1), ref[count, at])
    sweep(0, tiles, lambda r: first_vector(
        f_ref, c_ref, v1_ref, w_ref, faces_ref, center_ref, r, [count]), 34)
    second_vector(v1_ref, v2_ref, w_ref, center_ref, [[count]], 34)
    sums = tuple(sums_in[k] for k in range(2 * len(PAIRS)))
    sums = margin_products(f_ref, v1_ref, v2_ref, w_ref, center_ref, sums)
    row_ref[...] = jnp.broadcast_to(pack_sums(sums)[None], row_ref.shape)


def density_kernel(rows_ref, f_ref, c_ref, p_ref, v1_ref, v2_ref, w_ref, faces_ref,
                   value_out, u1_ref, u2_ref, row_ref, vx_ref, center_ref, value_ref, sem):
    dots, _unused = gathered_sums(rows_ref)
    c0, c1, c2 = [jnp.broadcast_to(c, (SUB, LANES)) for c in galerkin(dots)]
    which = list(range(f_ref.shape[0]))
    own = which[:-1]
    parts = [own, which[-1:]]
    tiles = row_tiles(f_ref)
    clear_pads((vx_ref, u1_ref, u2_ref), which)

    def value(r):
        at = pl.ds(r, SUB)
        return [
            (vx_ref, j, at, (c0 * f_ref[j, at, :] + c1 * v1_ref[j, at, :]) + c2 * v2_ref[j, at, :])
            for j in which
        ]

    sweep(0, tiles, value, 34)

    def first(r):
        at = pl.ds(r, SUB)
        val = beside_all(vx_ref, r, parts)
        cells = beside_all(p_ref, r, parts)
        out = []
        for j in which:
            inside = jnp.minimum(c_ref[j, at, :], 1.0)
            slope_row = 0.5 * (val[1][j] - val[2][j])
            slope_col = 0.5 * (val[3][j] - val[4][j])
            congestion = (slope_row * slope_row + slope_col * slope_col) * (0.5 / diffusion)
            zeroth = (discount_rate + congestion) * SCALE
            center = inside * zeroth + faces_ref[j, at, :]
            w = [w_ref[k, j, at, :] for k in range(4)]
            out.append((center_ref, j, at, center))
            out.append((u1_ref, j, at, weighted_apply(center, w, [x[j] for x in cells])))
        return out

    sweep(0, tiles, first, 34)

    unroll = even_share(tiles - 2, 32)

    def outer(t, sums):
        cost, weight = [list(x) for x in sums]
        for u in range(unroll):
            at = pl.ds(pl.multiple_of(PAD + (unroll * t + u) * SUB, SUB), SUB)
            to = pl.ds(pl.multiple_of((unroll * t + u) * SUB, SUB), SUB)
            for j in own:
                v = with_sides(vx_ref[j, at, :], vx_ref[len(own), at, :], j, len(own))
                p = p_ref[j, at, :]
                value_ref[to, tile_cols(j)] = v
                cost[j] = cost[j] + p * (f_ref[j, at, :] - discount_rate * v)
                weight[j] = weight[j] + p
        return tuple(cost), tuple(weight)

    zeros = (jnp.zeros((SUB, LANES), jnp.float32),) * len(own)
    extra = [sum(x) for x in lax.fori_loop(0, (tiles - 2) // unroll, outer, (zeros, zeros))]
    copy = pltpu.make_async_copy(value_ref, value_out, sem)
    copy.start()
    second_vector(u1_ref, u2_ref, w_ref, center_ref, parts)
    sums = own_products(p_ref, u1_ref, u2_ref, w_ref, center_ref, no_sums())
    sums = margin_products(p_ref, u1_ref, u2_ref, w_ref, center_ref, sums)
    row_ref[...] = jnp.broadcast_to(pack_sums(sums, extra)[None], row_ref.shape)
    copy.wait()


def finish_kernel(rows_ref, p_ref, u1_ref, u2_ref, density_ref, ergodic_ref):
    dots, (cost, weight) = gathered_sums(rows_ref, 2)
    ergodic_ref[...] = cost / weight
    c0, c1, c2 = [jnp.broadcast_to(c, (SUB, LANES)) for c in galerkin(dots)]
    count = p_ref.shape[0] - 1

    tiles = density_ref.shape[0] // SUB
    unroll = even_share(tiles, 32)

    def some(t, _):
        for u in range(unroll):
            at = pl.ds(pl.multiple_of(PAD + (unroll * t + u) * SUB, SUB), SUB)
            to = pl.ds(pl.multiple_of((unroll * t + u) * SUB, SUB), SUB)
            made = [(c0 * p_ref[j, at, :] + c1 * u1_ref[j, at, :]) + c2 * u2_ref[j, at, :] for j in range(count + 1)]
            for j in range(count):
                density_ref[to, tile_cols(j)] = with_sides(made[j], made[count], j, count)
        return 0

    lax.fori_loop(0, tiles // unroll, some, 0)


def f32(*shape):
    return jax.ShapeDtypeStruct(shape, jnp.float32)


def exchange(near, far, axis):
    n = lax.axis_size(axis)
    assert n % 2 == 0
    near = lax.ppermute(near, axis, [(i, i ^ 1) for i in range(n)])
    far = lax.ppermute(far, axis, [(i, (((i + 1) % n ^ 1) - 1) % n) for i in range(n)])
    return near, far


def everyone(row):
    return lax.all_to_all(row, BOTH, 0, 0, tiled=True)


def body(*args):
    rows, cols = args[0].shape
    devices = lax.axis_size("row") * lax.axis_size("col")
    count = cols // LANES
    ext = f32(count + 1, rows + 2 * PAD, LANES)
    ext4 = f32(4, *ext.shape)
    everyones = f32(devices, 1, LANES)
    _per, groups = packing(rows // SUB + 2)
    small = pltpu.CompilerParams(vmem_limit_bytes=VMEM_BYTES)

    def call(kernel, ins, outs, scratch=(), to_hbm=0, **more):
        return pl.pallas_call(
            kernel,
            in_specs=[VM] * len(ins),
            out_specs=[pl.BlockSpec(memory_space=pltpu.HBM)] * to_hbm + [VM] * (len(outs) - to_hbm),
            out_shape=outs,
            scratch_shapes=scratch,
            compiler_params=small,
            **more,
        )(*ins)

    cost = lambda us: pl.CostEstimate(flops=0, bytes_accessed=int(us * 2e6), transcendentals=0)
    up, down = edge_rows(*args)
    even = is_even("row")
    near, far = exchange(jnp.where(even, down, up), jnp.where(even, up, down), "row")
    forcing, conduct = fields_of(*args[:3])
    prior = args[3]
    state = call(
        inner_first_kernel, (forcing, conduct, prior),
        [ext] * 5 + [ext4, ext, ext], cost_estimate=cost(1.5))
    packs = call(pack_columns_kernel, (*state[:3], near, far), [f32(3 * groups * SUB, LANES)] * 2)
    sides = exchange(*packs, "col")
    *state, sums = call(
        inner_rest_kernel, (packs[0], near, far, *state),
        [ext] * 5 + [ext4, ext, ext, f32(2 * len(PAIRS), SUB, LANES)],
        input_output_aliases={3 + k: k for k in range(8)}, cost_estimate=cost(4))
    f, c, p, v1, v2, w, faces, _center, row = call(
        margin_kernel, (*sides, sums, *state),
        [ext] * 5 + [ext4, ext, ext, everyones], input_output_aliases={3 + k: k for k in range(8)})
    vmem = lambda like: pltpu.VMEM(like.shape, jnp.float32)
    block = f32(rows, cols)
    value, u1, u2, row = call(
        density_kernel, (everyone(row), f, c, p, v1, v2, w, faces), [block, ext, ext, everyones],
        [vmem(ext), vmem(ext), vmem(block), pltpu.SemaphoreType.DMA], 1)
    density, ergodic = call(
        finish_kernel, (everyone(row), p, u1, u2), [block, f32(1, 1)])
    return value, density, ergodic[0, 0]


def solution(mesh):
    spec = P("row", "col")
    return jax.shard_map(body, mesh=mesh, in_specs=(spec,) * 4, out_specs=(spec, spec, P()), check_vma=False)
```

```python
import functools

import jax
import jax.numpy as jnp
from jax import lax
from jax.experimental import pallas as pl
from jax.experimental.pallas import tpu as pltpu
from jax.sharding import PartitionSpec as P

discount_rate = 0.05
diffusion = 0.25
SCALE = 0.0625
FACE = diffusion * 0.5 * SCALE
LANES = 128
SUB = 8
WIDE = 5
EDGE = 10
DEEP = 5
PAD = 2 * SUB
VMEM_BYTES = 16 * 2**20
VM = pl.BlockSpec(memory_space=pltpu.VMEM)
BOTH = ("row", "col")
CHAIN = 8


def two_sum(a, b):
    s = a + b
    t = s - a
    return s, (a - (s - t)) + (b - t)


def fast_sum(a, b):
    s = a + b
    return s, b - (s - a)


def halves(a):
    t = a * 4097.0
    hi = t - (t - a)
    return hi, a - hi


def two_prod(a, b):
    p = a * b
    ah, al = halves(a)
    bh, bl = halves(b)
    return p, ((ah * bh - p) + ah * bl + al * bh) + al * bl


def dmul(a, b):
    p, e = two_prod(a[0], b[0])
    return fast_sum(p, e + (a[0] * b[1] + a[1] * b[0]))


def dsub(a, b):
    s, e = two_sum(a[0], -b[0])
    return fast_sum(s, e + (a[1] - b[1]))


def ddiv(a, b):
    q = a[0] / b[0]
    r = dsub(a, dmul((q, jnp.zeros_like(q)), b))
    return fast_sum(q, r[0] / b[0])


def galerkin(dots):
    d00, d01, d02, d03, d11, d12, d13, d22, d23 = dots
    zero = jnp.zeros_like(d00[0])
    l1 = ddiv(d11, d01)
    l2 = ddiv(d12, d01)
    s11 = dsub(d12, dmul(l1, d02))
    s12 = dsub(d13, dmul(l1, d03))
    s21 = dsub(d22, dmul(l2, d02))
    s22 = dsub(d23, dmul(l2, d03))
    g0 = (d00[0] * SCALE, d00[1] * SCALE)
    g1 = dsub((d01[0] * SCALE, d01[1] * SCALE), dmul(l1, g0))
    g2 = dsub((d02[0] * SCALE, d02[1] * SCALE), dmul(l2, g0))
    l3 = ddiv(s21, s11)
    t22 = dsub(s22, dmul(l3, s12))
    g2 = dsub(g2, dmul(l3, g1))
    full1 = s11[0] > 1e-12 * d12[0]
    full2 = full1 & (t22[0] > 1e-12 * d23[0])
    c2 = jnp.where(full2, g2[0] / t22[0], zero)
    c1 = dsub(g1, dmul(s12, (c2, zero)))[0] / s11[0]
    c1 = jnp.where(full1, c1, zero)
    r0 = dsub(dsub(g0, dmul(d02, (c1, zero))), dmul(d03, (c2, zero)))
    return r0[0] / d01[0], c1, c2


PAIRS = ((0, 0), (0, 1), (0, 2), (0, 3), (1, 1), (1, 2), (1, 3), (2, 2), (2, 3))


def split_short(a):
    t = a * 65537.0
    hi = t - (t - a)
    return hi, a - hi


def dot_step(groups, sums):
    mains, rests = [None] * len(PAIRS), [None] * len(PAIRS)
    for vs in groups:
        parts = [split_short(v) for v in vs]
        for k, (i, j) in enumerate(PAIRS):
            m = parts[i][0] * parts[j][0]
            if i == j:
                r = parts[i][1] * (vs[i] + parts[i][0])
            else:
                r = parts[i][0] * parts[j][1] + parts[i][1] * vs[j]
            mains[k] = m if mains[k] is None else mains[k] + m
            rests[k] = r if rests[k] is None else rests[k] + r
    out = []
    for k, (main, rest) in enumerate(zip(mains, rests)):
        s, e = two_sum(sums[2 * k], main)
        out += [s, sums[2 * k + 1] + (e + rest)]
    return tuple(out)


def pack_sums(sums, extra=()):
    lane = lax.broadcasted_iota(jnp.int32, (1, LANES), 1)
    row = jnp.zeros((1, LANES), jnp.float32)
    total = lambda a: jnp.sum(jnp.sum(a, axis=0, keepdims=True), axis=1, keepdims=True)
    for k in range(len(PAIRS)):
        s, e = sums[2 * k], sums[2 * k + 1]
        peak = jnp.max(jnp.max(jnp.abs(s), axis=0, keepdims=True), axis=1, keepdims=True)
        lift = jnp.broadcast_to(peak * 2048.0, s.shape)
        main = (s + lift) - lift
        row = jnp.where(lane == k, total(main), row)
        row = jnp.where(lane == 64 + k, total((s - main) + e), row)
    for k, a in enumerate(extra):
        row = jnp.where(lane == len(PAIRS) + k, total(a), row)
    return row


def gathered_sums(ref, extra=0):
    rows = [(ref[d], None) for d in range(ref.shape[0])]
    while len(rows) > 1:
        merged = []
        for k in range(0, len(rows) - 1, 2):
            (a, ea), (b, eb) = rows[k], rows[k + 1]
            s, e = two_sum(a, b)
            e = e if ea is None else e + (ea + eb)
            merged.append((s, e))
        if len(rows) % 2:
            a, ea = rows[-1]
            merged.append((a, jnp.zeros_like(a) if ea is None else ea))
        rows = merged
    s, e = rows[0]
    lane = lax.broadcasted_iota(jnp.int32, s.shape, 1)
    pick = lambda a, k: jnp.sum(jnp.where(lane == k, a, 0.0), axis=1, keepdims=True)
    dots = []
    for k in range(len(PAIRS)):
        hi = pick(s, k)
        lo = pick(e, k) + pick(s, 64 + k)
        dots.append(fast_sum(hi, lo))
    return dots, [pick(s, len(PAIRS) + k) for k in range(extra)]


FIRST = EDGE + 2 * WIDE


def fields_of(rc, cx, cy):
    control_cost = 0.5 * (cx * cx + cy * cy)
    return rc + control_cost, 1.0 + control_cost


def edge_rows(rc, cx, cy, pd):
    rows, cols = rc.shape
    few = WIDE - 2
    gap = jnp.zeros((2 * SUB - 2 * WIDE - few, cols), jnp.float32)
    ends = [[x[:SUB] for x in (rc, cx, cy, pd)], [x[rows - SUB :] for x in (rc, cx, cy, pd)]]
    (f, c, p), (g, d, q) = lax.optimization_barrier([(*fields_of(*x[:3]), x[3]) for x in ends])
    up = jnp.concatenate([p[:few], f[:WIDE], c[:WIDE], gap])
    return up, jnp.concatenate([gap, d[SUB - WIDE :], g[SUB - WIDE :], q[SUB - few :]])


def neighbours_along(axis):
    i = lax.axis_index(axis)
    return i > 0, i < lax.axis_size(axis) - 1


def is_even(axis):
    return lax.rem(lax.axis_index(axis), 2) == 0


def even_share(n, most):
    return max(d for d in range(1, most + 1) if n % d == 0)


def lanes():
    return lax.broadcasted_iota(jnp.int32, (SUB, LANES), 1)


def tile_cols(j):
    return slice(j * LANES, (j + 1) * LANES)


def halo_tile(refs, field, j, south):
    at = ((3, 8, 0) if south else (5, 0, 8))[field]
    first, second = [ref[at : at + SUB, tile_cols(j)] for ref in refs]
    tile = jnp.where(is_even("row"), first, second) if south else jnp.where(is_even("row"), second, first)
    return jnp.where(neighbours_along("row")[int(south)], tile, 0.0)


def packing(tiles):
    per = LANES // (2 * WIDE)
    return per, -(-tiles // per)


def pack_columns_kernel(f_ref, c_ref, p_ref, near_ref, far_ref, first_ref, second_ref):
    tiles = row_tiles(f_ref)
    per, groups = packing(tiles)
    end = p_ref.shape[0] - 2
    lane = lanes()
    even = is_even("col")
    for field in range(3):

        def tile(j, t):
            if t == 0:
                return halo_tile((near_ref, far_ref), field, j, False)
            if t == tiles - 1:
                return halo_tile((near_ref, far_ref), field, j, True)
            return (f_ref, c_ref, p_ref)[field][j, (t + 1) * SUB : (t + 2) * SUB]

        for v in range(groups):
            west = jnp.zeros((SUB, LANES), jnp.float32)
            east = west
            for g in range(min(per, tiles - v * per)):
                at = 2 * WIDE * g
                a, b = tile(0, v * per + g), tile(end, v * per + g)
                west = jnp.where((lane >= at) & (lane < at + WIDE), pltpu.roll(a, at, 1), west)
                there = (lane >= at + WIDE) & (lane < at + 2 * WIDE)
                east = jnp.where(there, pltpu.roll(b, (at + 2 * WIDE) % LANES, 1), east)
            at = (field * groups + v) * SUB
            first_ref[at : at + SUB] = jnp.where(even, east, west)
            second_ref[at : at + SUB] = jnp.where(even, west, east)


def beside(ref, r, which):
    lane = lanes()
    n = len(which)
    here = [ref[j, pl.ds(r, SUB), :] for j in which]
    south = [ref[j, pl.ds(r + 1, SUB), :] for j in which]
    north = [ref[j, pl.ds(r - 1, SUB), :] for j in which]
    east = [pltpu.roll(a, LANES - 1, 1) for a in here]
    west = [pltpu.roll(a, 1, 1) for a in here]
    if n > 1:
        east, west = (
            [jnp.where(lane == LANES - 1, east[(k + 1) % n], east[k]) for k in range(n)],
            [jnp.where(lane == 0, west[k - 1], west[k]) for k in range(n)],
        )
    return [dict(zip(which, x)) for x in (here, south, north, east, west)]


def beside_all(ref, r, parts):
    found = [beside(ref, r, which) for which in parts]
    return [{j: x for part in found for j, x in part[k].items()} for k in range(5)]


def weighted_apply(center, w, cells):
    here, south, north, east, west = cells
    return center * here - ((w[0] * south + w[1] * north) + (w[2] * east + w[3] * west))


def apply_tiles(ref, w_ref, center_ref, r, parts):
    cells = beside_all(ref, r, parts)
    at = pl.ds(r, SUB)
    out = {}
    for j in cells[0]:
        w = [w_ref[k, j, at, :] for k in range(4)]
        out[j] = weighted_apply(center_ref[j, at, :], w, [c[j] for c in cells])
    return out, cells[0]


def first_vector(f_ref, c_ref, v1_ref, w_ref, faces_ref, center_ref, r, which):
    at = pl.ds(r, SUB)
    cond = beside(c_ref, r, which)
    cells = beside(f_ref, r, which)
    out = []
    for j in which:
        c = cond[0][j]
        inside = jnp.minimum(c, 1.0)
        face = inside * FACE
        w = [face * (c + cond[k][j]) for k in (1, 2, 3, 4)]
        faces = (w[0] + w[1]) + (w[2] + w[3])
        center = inside * (discount_rate * SCALE) + faces
        out += [(w_ref.at[k], j, at, w[k]) for k in range(4)]
        out.append((faces_ref, j, at, faces))
        out.append((center_ref, j, at, center))
        out.append((v1_ref, j, at, weighted_apply(center, w, [x[j] for x in cells])))
    return out


def clear_pads(refs, which):
    zero = jnp.zeros((SUB, LANES), jnp.float32)
    for ref in refs:
        rows = ref.shape[1]
        for j in which:
            ref[j, 0:SUB] = zero
            ref[j, rows - SUB : rows] = zero


def row_tiles(ref):
    return (ref.shape[1] - 2 * SUB) // SUB


def sweep(start, stop, step, unroll=2):
    def group(rows):
        stores = [store for r in rows for store in step(r)]
        for ref, j, at, value in stores:
            ref[j, at, :] = value

    def some(t, _):
        base = start + t * unroll
        group([pl.multiple_of(SUB + (base + u) * SUB, SUB) for u in range(unroll)])
        return 0

    whole = (stop - start) // unroll
    lax.fori_loop(0, whole, some, 0)
    rest = range(start + whole * unroll, stop)
    if len(rest):
        group([SUB + t * SUB for t in rest])


def second_vector(v1_ref, v2_ref, w_ref, center_ref, parts, unroll=34, start=0, stop=None):
    def step(r):
        out, _here = apply_tiles(v1_ref, w_ref, center_ref, r, parts)
        return [(v2_ref, j, pl.ds(r, SUB), x) for j, x in out.items()]

    sweep(start, row_tiles(v1_ref) if stop is None else stop, step, unroll)


def no_sums():
    return (jnp.zeros((SUB, LANES), jnp.float32),) * (2 * len(PAIRS))


def own_products(v0_ref, v1_ref, v2_ref, w_ref, center_ref, sums, most=8):
    own = list(range(v0_ref.shape[0] - 1))
    lane = lanes()
    unroll = even_share(row_tiles(v0_ref) - 2, most)

    def step(t, sums):
        groups = []
        for u in range(unroll):
            r = pl.multiple_of(PAD + (t * unroll + u) * SUB, SUB)
            out, here = apply_tiles(v2_ref, w_ref, center_ref, r, [own])
            at = pl.ds(r, SUB)
            for j in own:
                vs = [v0_ref[j, at, :], v1_ref[j, at, :], here[j]]
                if j == 0:
                    vs = [jnp.where(lane >= DEEP, v, 0.0) for v in vs]
                if j == own[-1]:
                    vs = [jnp.where(lane < LANES - DEEP, v, 0.0) for v in vs]
                groups.append((*vs, out[j]))
        for k in range(0, len(groups), CHAIN):
            sums = dot_step(groups[k : k + CHAIN], sums)
        return sums

    return lax.fori_loop(0, (row_tiles(v0_ref) - 2) // unroll, step, sums)


def margin_products(v0_ref, v1_ref, v2_ref, w_ref, center_ref, sums):
    margin = v0_ref.shape[0] - 1
    lane = lanes()
    span = FIRST + DEEP - (EDGE - DEEP)
    runs = (FIRST - EDGE + DEEP) // DEEP
    block = span + (runs - 1) * DEEP
    slots = [block * b + DEEP * k for b in range(LANES // block) for k in range(runs)]
    tiles = row_tiles(v0_ref) - 2
    groups = []
    for start in range(0, tiles, len(slots)):
        packed = None
        for t, slot in zip(range(start, tiles), slots):
            at = slice(PAD + t * SUB, PAD + (t + 1) * SUB)
            out, here = apply_tiles(v2_ref, w_ref, center_ref, PAD + t * SUB, [[margin]])
            vs = [v0_ref[margin, at], v1_ref[margin, at], here[margin], out[margin]]
            put = (slot - (EDGE - DEEP)) % LANES
            vs = [pltpu.roll(v, put, 1) if put else v for v in vs]
            low, high = slot, slot + span - DEEP
            mask = ((lane >= low) & (lane < low + DEEP)) | ((lane >= high) & (lane < high + DEEP))
            if packed is None:
                packed = [jnp.where(mask, v, 0.0) for v in vs]
            else:
                packed = [jnp.where(mask, v, x) for v, x in zip(vs, packed)]
        groups.append(tuple(packed))
    return dot_step(groups, sums)


def with_sides(tile, side, j, count):
    lane = lanes()
    if j == 0:
        tile = jnp.where(lane < DEEP, pltpu.roll(side, LANES - FIRST, 1), tile)
    if j == count - 1:
        tile = jnp.where(lane >= LANES - DEEP, pltpu.roll(side, LANES - EDGE, 1), tile)
    return tile


def repeat_sides(ref, t):
    count = ref.shape[0] - 1
    lane = lanes()
    at = slice((t + 1) * SUB, (t + 2) * SUB)
    last = pltpu.roll(ref[count - 1, at], EDGE, 1)
    first = pltpu.roll(ref[0, at], FIRST, 1)
    keep = (lane >= FIRST) & (lane < FIRST + EDGE)
    ref[count, at] = jnp.where(lane < EDGE, last, jnp.where(keep, first, 0.0))


def inner_first_kernel(f_in, c_in, p_in,
                       f_ref, c_ref, p_ref, v1_ref, v2_ref, w_ref, faces_ref, center_ref):
    own = list(range(f_ref.shape[0] - 1))
    rows = f_in.shape[0]
    tiles = row_tiles(f_ref)
    clear_pads((f_ref, c_ref, p_ref, v1_ref, v2_ref), own)
    for ref, source in ((f_ref, f_in), (c_ref, c_in), (p_ref, p_in)):
        for j in own:
            ref[j, PAD : PAD + rows] = source[:, tile_cols(j)]
        for t in range(1, tiles - 1):
            repeat_sides(ref, t)
    sweep(2, tiles - 2,
          lambda r: first_vector(f_ref, c_ref, v1_ref, w_ref, faces_ref, center_ref, r, own), 30)
    second_vector(v1_ref, v2_ref, w_ref, center_ref, [own], 28, 3, tiles - 3)


def inner_rest_kernel(after, near_ref, far_ref, f_in, c_in, p_in, v1_in, v2_in, w_in, faces_in, center_in,
                      f_ref, c_ref, p_ref, v1_ref, v2_ref, w_ref, faces_ref, center_ref, sums_ref):
    own = list(range(f_ref.shape[0] - 1))
    rows = f_ref.shape[1]
    tiles = row_tiles(f_ref)
    for field, ref in enumerate((f_ref, c_ref, p_ref)):
        for j in own:
            ref[j, SUB : 2 * SUB] = halo_tile((near_ref, far_ref), field, j, False)
            ref[j, rows - 2 * SUB : rows - SUB] = halo_tile((near_ref, far_ref), field, j, True)
        repeat_sides(ref, 0)
        repeat_sides(ref, tiles - 1)
    for start in (0, tiles - 2):
        sweep(start, start + 2,
              lambda r: first_vector(f_ref, c_ref, v1_ref, w_ref, faces_ref, center_ref, r, own))
    for start in (0, tiles - 3):
        second_vector(v1_ref, v2_ref, w_ref, center_ref, [own], 3, start, start + 3)
    sums = own_products(f_ref, v1_ref, v2_ref, w_ref, center_ref, no_sums())
    for k, a in enumerate(sums):
        sums_ref[k] = a


def margin_kernel(near_ref, far_ref, sums_in, f_in, c_in, p_in, v1_in, v2_in, w_in, faces_in, center_in,
                  f_ref, c_ref, p_ref, v1_ref, v2_ref, w_ref, faces_ref, center_ref, row_ref):
    count = f_ref.shape[0] - 1
    tiles = row_tiles(f_ref)
    per, groups = packing(tiles)
    lane = lanes()
    has_west, has_east = neighbours_along("col")
    even = is_even("col")
    from_east = lax.rem(lane, 2 * WIDE) < WIDE
    halo = (lane >= EDGE) & (lane < FIRST)
    clear_pads((f_ref, c_ref, p_ref, v1_ref, v2_ref), [count])
    for field, ref in enumerate((f_ref, c_ref, p_ref)):
        for v in range(groups):
            src = slice((field * groups + v) * SUB, (field * groups + v + 1) * SUB)
            near, far = near_ref[src], far_ref[src]
            east = jnp.where(has_east, jnp.where(even, near, far), 0.0)
            west = jnp.where(has_west, jnp.where(even, far, near), 0.0)
            both = jnp.where(from_east, east, west)
            for g in range(min(per, tiles - v * per)):
                t = v * per + g
                at = slice(SUB + t * SUB, 2 * SUB + t * SUB)
                ref[count, at] = jnp.where(halo, pltpu.roll(both, (EDGE - 2 * WIDE * g) % LANES, 1), ref[count, at])
    sweep(0, tiles, lambda r: first_vector(
        f_ref, c_ref, v1_ref, w_ref, faces_ref, center_ref, r, [count]), 34)
    second_vector(v1_ref, v2_ref, w_ref, center_ref, [[count]], 34)
    sums = tuple(sums_in[k] for k in range(2 * len(PAIRS)))
    sums = margin_products(f_ref, v1_ref, v2_ref, w_ref, center_ref, sums)
    row_ref[...] = jnp.broadcast_to(pack_sums(sums)[None], row_ref.shape)


def density_kernel(rows_ref, f_ref, c_ref, p_ref, v1_ref, v2_ref, w_ref, faces_ref,
                   value_out, u1_ref, u2_ref, row_ref, vx_ref, center_ref, value_ref, sem):
    dots, _unused = gathered_sums(rows_ref)
    c0, c1, c2 = [jnp.broadcast_to(c, (SUB, LANES)) for c in galerkin(dots)]
    which = list(range(f_ref.shape[0]))
    own = which[:-1]
    parts = [own, which[-1:]]
    tiles = row_tiles(f_ref)
    clear_pads((vx_ref, u1_ref, u2_ref), which)

    def value(r):
        at = pl.ds(r, SUB)
        return [
            (vx_ref, j, at, (c0 * f_ref[j, at, :] + c1 * v1_ref[j, at, :]) + c2 * v2_ref[j, at, :])
            for j in which
        ]

    sweep(0, tiles, value, 34)

    def first(r):
        at = pl.ds(r, SUB)
        val = beside_all(vx_ref, r, parts)
        cells = beside_all(p_ref, r, parts)
        out = []
        for j in which:
            inside = jnp.minimum(c_ref[j, at, :], 1.0)
            slope_row = 0.5 * (val[1][j] - val[2][j])
            slope_col = 0.5 * (val[3][j] - val[4][j])
            congestion = (slope_row * slope_row + slope_col * slope_col) * (0.5 / diffusion)
            zeroth = (discount_rate + congestion) * SCALE
            center = inside * zeroth + faces_ref[j, at, :]
            w = [w_ref[k, j, at, :] for k in range(4)]
            out.append((center_ref, j, at, center))
            out.append((u1_ref, j, at, weighted_apply(center, w, [x[j] for x in cells])))
        return out

    sweep(0, tiles, first, 34)

    unroll = even_share(tiles - 2, 32)

    def outer(t, sums):
        cost, weight = [list(x) for x in sums]
        for u in range(unroll):
            at = pl.ds(pl.multiple_of(PAD + (unroll * t + u) * SUB, SUB), SUB)
            to = pl.ds(pl.multiple_of((unroll * t + u) * SUB, SUB), SUB)
            for j in own:
                v = with_sides(vx_ref[j, at, :], vx_ref[len(own), at, :], j, len(own))
                p = p_ref[j, at, :]
                value_ref[to, tile_cols(j)] = v
                cost[j] = cost[j] + p * (f_ref[j, at, :] - discount_rate * v)
                weight[j] = weight[j] + p
        return tuple(cost), tuple(weight)

    zeros = (jnp.zeros((SUB, LANES), jnp.float32),) * len(own)
    extra = [sum(x) for x in lax.fori_loop(0, (tiles - 2) // unroll, outer, (zeros, zeros))]
    copy = pltpu.make_async_copy(value_ref, value_out, sem)
    copy.start()
    second_vector(u1_ref, u2_ref, w_ref, center_ref, parts)
    sums = own_products(p_ref, u1_ref, u2_ref, w_ref, center_ref, no_sums())
    sums = margin_products(p_ref, u1_ref, u2_ref, w_ref, center_ref, sums)
    row_ref[...] = jnp.broadcast_to(pack_sums(sums, extra)[None], row_ref.shape)
    copy.wait()


def finish_kernel(rows_ref, p_ref, u1_ref, u2_ref, density_ref, ergodic_ref):
    dots, (cost, weight) = gathered_sums(rows_ref, 2)
    ergodic_ref[...] = cost / weight
    c0, c1, c2 = [jnp.broadcast_to(c, (SUB, LANES)) for c in galerkin(dots)]
    count = p_ref.shape[0] - 1

    tiles = density_ref.shape[0] // SUB
    unroll = even_share(tiles, 32)

    def some(t, _):
        for u in range(unroll):
            at = pl.ds(pl.multiple_of(PAD + (unroll * t + u) * SUB, SUB), SUB)
            to = pl.ds(pl.multiple_of((unroll * t + u) * SUB, SUB), SUB)
            made = [(c0 * p_ref[j, at, :] + c1 * u1_ref[j, at, :]) + c2 * u2_ref[j, at, :] for j in range(count + 1)]
            for j in range(count):
                density_ref[to, tile_cols(j)] = with_sides(made[j], made[count], j, count)
        return 0

    lax.fori_loop(0, tiles // unroll, some, 0)


def f32(*shape):
    return jax.ShapeDtypeStruct(shape, jnp.float32)


def exchange(near, far, axis):
    n = lax.axis_size(axis)
    assert n % 2 == 0
    near = lax.ppermute(near, axis, [(i, i ^ 1) for i in range(n)])
    far = lax.ppermute(far, axis, [(i, (((i + 1) % n ^ 1) - 1) % n) for i in range(n)])
    return near, far


def everyone(row):
    return lax.all_to_all(row, BOTH, 0, 0, tiled=True)


def body(*args):
    rows, cols = args[0].shape
    devices = lax.axis_size("row") * lax.axis_size("col")
    count = cols // LANES
    ext = f32(count + 1, rows + 2 * PAD, LANES)
    ext4 = f32(4, *ext.shape)
    everyones = f32(devices, 1, LANES)
    _per, groups = packing(rows // SUB + 2)
    small = pltpu.CompilerParams(vmem_limit_bytes=VMEM_BYTES)

    def call(kernel, ins, outs, scratch=(), to_hbm=0, **more):
        return pl.pallas_call(
            kernel,
            in_specs=[VM] * len(ins),
            out_specs=[pl.BlockSpec(memory_space=pltpu.HBM)] * to_hbm + [VM] * (len(outs) - to_hbm),
            out_shape=outs,
            scratch_shapes=scratch,
            compiler_params=small,
            **more,
        )(*ins)

    cost = lambda us: pl.CostEstimate(flops=0, bytes_accessed=int(us * 2e6), transcendentals=0)
    up, down = edge_rows(*args)
    even = is_even("row")
    near, far = exchange(jnp.where(even, down, up), jnp.where(even, up, down), "row")
    forcing, conduct = fields_of(*args[:3])
    prior = args[3]
    state = call(
        inner_first_kernel, (forcing, conduct, prior),
        [ext] * 5 + [ext4, ext, ext], cost_estimate=cost(1.5))
    packs = call(pack_columns_kernel, (*state[:3], near, far), [f32(3 * groups * SUB, LANES)] * 2)
    sides = exchange(*packs, "col")
    *state, sums = call(
        inner_rest_kernel, (packs[0], near, far, *state),
        [ext] * 5 + [ext4, ext, ext, f32(2 * len(PAIRS), SUB, LANES)],
        input_output_aliases={3 + k: k for k in range(8)}, cost_estimate=cost(4))
    f, c, p, v1, v2, w, faces, _center, row = call(
        margin_kernel, (*sides, sums, *state),
        [ext] * 5 + [ext4, ext, ext, everyones], input_output_aliases={3 + k: k for k in range(8)})
    vmem = lambda like: pltpu.VMEM(like.shape, jnp.float32)
    block = f32(rows, cols)
    value, u1, u2, row = call(
        density_kernel, (everyone(row), f, c, p, v1, v2, w, faces), [block, ext, ext, everyones],
        [vmem(ext), vmem(ext), vmem(block), pltpu.SemaphoreType.DMA], 1)
    density, ergodic = call(
        finish_kernel, (everyone(row), p, u1, u2), [block, f32(1, 1)])
    return value, density, ergodic[0, 0]


def solution(mesh):
    spec = P("row", "col")
    return jax.shard_map(body, mesh=mesh, in_specs=(spec,) * 4, out_specs=(spec, spec, P()), check_vma=False)
```

```python
import functools

import jax
import jax.numpy as jnp
from jax import lax
from jax.experimental import pallas as pl
from jax.experimental.pallas import tpu as pltpu
from jax.sharding import PartitionSpec as P

discount_rate = 0.05
diffusion = 0.25
SCALE = 0.0625
FACE = diffusion * 0.5 * SCALE
LANES = 128
SUB = 8
WIDE = 5
EDGE = 10
DEEP = 5
PAD = 2 * SUB
VMEM_BYTES = 16 * 2**20
VM = pl.BlockSpec(memory_space=pltpu.VMEM)
BOTH = ("row", "col")
CHAIN = 8


def two_sum(a, b):
    s = a + b
    t = s - a
    return s, (a - (s - t)) + (b - t)


def fast_sum(a, b):
    s = a + b
    return s, b - (s - a)


def halves(a):
    t = a * 4097.0
    hi = t - (t - a)
    return hi, a - hi


def two_prod(a, b):
    p = a * b
    ah, al = halves(a)
    bh, bl = halves(b)
    return p, ((ah * bh - p) + ah * bl + al * bh) + al * bl


def dmul(a, b):
    p, e = two_prod(a[0], b[0])
    return fast_sum(p, e + (a[0] * b[1] + a[1] * b[0]))


def dsub(a, b):
    s, e = two_sum(a[0], -b[0])
    return fast_sum(s, e + (a[1] - b[1]))


def ddiv(a, b):
    q = a[0] / b[0]
    r = dsub(a, dmul((q, jnp.zeros_like(q)), b))
    return fast_sum(q, r[0] / b[0])


def galerkin(dots):
    d00, d01, d02, d03, d11, d12, d13, d22, d23 = dots
    zero = jnp.zeros_like(d00[0])
    l1 = ddiv(d11, d01)
    l2 = ddiv(d12, d01)
    s11 = dsub(d12, dmul(l1, d02))
    s12 = dsub(d13, dmul(l1, d03))
    s21 = dsub(d22, dmul(l2, d02))
    s22 = dsub(d23, dmul(l2, d03))
    g0 = (d00[0] * SCALE, d00[1] * SCALE)
    g1 = dsub((d01[0] * SCALE, d01[1] * SCALE), dmul(l1, g0))
    g2 = dsub((d02[0] * SCALE, d02[1] * SCALE), dmul(l2, g0))
    l3 = ddiv(s21, s11)
    t22 = dsub(s22, dmul(l3, s12))
    g2 = dsub(g2, dmul(l3, g1))
    full1 = s11[0] > 1e-12 * d12[0]
    full2 = full1 & (t22[0] > 1e-12 * d23[0])
    c2 = jnp.where(full2, g2[0] / t22[0], zero)
    c1 = dsub(g1, dmul(s12, (c2, zero)))[0] / s11[0]
    c1 = jnp.where(full1, c1, zero)
    r0 = dsub(dsub(g0, dmul(d02, (c1, zero))), dmul(d03, (c2, zero)))
    return r0[0] / d01[0], c1, c2


PAIRS = ((0, 0), (0, 1), (0, 2), (0, 3), (1, 1), (1, 2), (1, 3), (2, 2), (2, 3))


def split_short(a):
    t = a * 65537.0
    hi = t - (t - a)
    return hi, a - hi


def dot_step(groups, sums):
    mains, rests = [None] * len(PAIRS), [None] * len(PAIRS)
    for vs in groups:
        parts = [split_short(v) for v in vs]
        for k, (i, j) in enumerate(PAIRS):
            m = parts[i][0] * parts[j][0]
            if i == j:
                r = parts[i][1] * (vs[i] + parts[i][0])
            else:
                r = parts[i][0] * parts[j][1] + parts[i][1] * vs[j]
            mains[k] = m if mains[k] is None else mains[k] + m
            rests[k] = r if rests[k] is None else rests[k] + r
    out = []
    for k, (main, rest) in enumerate(zip(mains, rests)):
        s, e = two_sum(sums[2 * k], main)
        out += [s, sums[2 * k + 1] + (e + rest)]
    return tuple(out)


def pack_sums(sums, extra=()):
    lane = lax.broadcasted_iota(jnp.int32, (1, LANES), 1)
    row = jnp.zeros((1, LANES), jnp.float32)
    total = lambda a: jnp.sum(jnp.sum(a, axis=0, keepdims=True), axis=1, keepdims=True)
    for k in range(len(PAIRS)):
        s, e = sums[2 * k], sums[2 * k + 1]
        peak = jnp.max(jnp.max(jnp.abs(s), axis=0, keepdims=True), axis=1, keepdims=True)
        lift = jnp.broadcast_to(peak * 2048.0, s.shape)
        main = (s + lift) - lift
        row = jnp.where(lane == k, total(main), row)
        row = jnp.where(lane == 64 + k, total((s - main) + e), row)
    for k, a in enumerate(extra):
        row = jnp.where(lane == len(PAIRS) + k, total(a), row)
    return row


def gathered_sums(ref, extra=0):
    rows = [(ref[d], None) for d in range(ref.shape[0])]
    while len(rows) > 1:
        merged = []
        for k in range(0, len(rows) - 1, 2):
            (a, ea), (b, eb) = rows[k], rows[k + 1]
            s, e = two_sum(a, b)
            e = e if ea is None else e + (ea + eb)
            merged.append((s, e))
        if len(rows) % 2:
            a, ea = rows[-1]
            merged.append((a, jnp.zeros_like(a) if ea is None else ea))
        rows = merged
    s, e = rows[0]
    lane = lax.broadcasted_iota(jnp.int32, s.shape, 1)
    pick = lambda a, k: jnp.sum(jnp.where(lane == k, a, 0.0), axis=1, keepdims=True)
    dots = []
    for k in range(len(PAIRS)):
        hi = pick(s, k)
        lo = pick(e, k) + pick(s, 64 + k)
        dots.append(fast_sum(hi, lo))
    return dots, [pick(s, len(PAIRS) + k) for k in range(extra)]


FIRST = EDGE + 2 * WIDE


def fields_of(rc, cx, cy):
    control_cost = 0.5 * (cx * cx + cy * cy)
    return rc + control_cost, 1.0 + control_cost


def edge_rows(rc, cx, cy, pd):
    rows, cols = rc.shape
    few = WIDE - 2
    gap = jnp.zeros((2 * SUB - 2 * WIDE - few, cols), jnp.float32)
    ends = [[x[:SUB] for x in (rc, cx, cy, pd)], [x[rows - SUB :] for x in (rc, cx, cy, pd)]]
    (f, c, p), (g, d, q) = lax.optimization_barrier([(*fields_of(*x[:3]), x[3]) for x in ends])
    up = jnp.concatenate([p[:few], f[:WIDE], c[:WIDE], gap])
    return up, jnp.concatenate([gap, d[SUB - WIDE :], g[SUB - WIDE :], q[SUB - few :]])


def neighbours_along(axis):
    i = lax.axis_index(axis)
    return i > 0, i < lax.axis_size(axis) - 1


def is_even(axis):
    return lax.rem(lax.axis_index(axis), 2) == 0


def even_share(n, most):
    return max(d for d in range(1, most + 1) if n % d == 0)


def lanes():
    return lax.broadcasted_iota(jnp.int32, (SUB, LANES), 1)


def tile_cols(j):
    return slice(j * LANES, (j + 1) * LANES)


def halo_tile(refs, field, j, south):
    at = ((3, 8, 0) if south else (5, 0, 8))[field]
    first, second = [ref[at : at + SUB, tile_cols(j)] for ref in refs]
    tile = jnp.where(is_even("row"), first, second) if south else jnp.where(is_even("row"), second, first)
    return jnp.where(neighbours_along("row")[int(south)], tile, 0.0)


def packing(tiles):
    per = LANES // (2 * WIDE)
    return per, -(-tiles // per)


def pack_columns_kernel(f_ref, c_ref, p_ref, near_ref, far_ref, first_ref, second_ref):
    tiles = row_tiles(f_ref)
    per, groups = packing(tiles)
    end = p_ref.shape[0] - 2
    lane = lanes()
    even = is_even("col")
    for field in range(3):

        def tile(j, t):
            if t == 0:
                return halo_tile((near_ref, far_ref), field, j, False)
            if t == tiles - 1:
                return halo_tile((near_ref, far_ref), field, j, True)
            return (f_ref, c_ref, p_ref)[field][j, (t + 1) * SUB : (t + 2) * SUB]

        for v in range(groups):
            west = jnp.zeros((SUB, LANES), jnp.float32)
            east = west
            for g in range(min(per, tiles - v * per)):
                at = 2 * WIDE * g
                a, b = tile(0, v * per + g), tile(end, v * per + g)
                west = jnp.where((lane >= at) & (lane < at + WIDE), pltpu.roll(a, at, 1), west)
                there = (lane >= at + WIDE) & (lane < at + 2 * WIDE)
                east = jnp.where(there, pltpu.roll(b, (at + 2 * WIDE) % LANES, 1), east)
            at = (field * groups + v) * SUB
            first_ref[at : at + SUB] = jnp.where(even, east, west)
            second_ref[at : at + SUB] = jnp.where(even, west, east)


def beside(ref, r, which):
    lane = lanes()
    n = len(which)
    here = [ref[j, pl.ds(r, SUB), :] for j in which]
    south = [ref[j, pl.ds(r + 1, SUB), :] for j in which]
    north = [ref[j, pl.ds(r - 1, SUB), :] for j in which]
    east = [pltpu.roll(a, LANES - 1, 1) for a in here]
    west = [pltpu.roll(a, 1, 1) for a in here]
    if n > 1:
        east, west = (
            [jnp.where(lane == LANES - 1, east[(k + 1) % n], east[k]) for k in range(n)],
            [jnp.where(lane == 0, west[k - 1], west[k]) for k in range(n)],
        )
    return [dict(zip(which, x)) for x in (here, south, north, east, west)]


def beside_all(ref, r, parts):
    found = [beside(ref, r, which) for which in parts]
    return [{j: x for part in found for j, x in part[k].items()} for k in range(5)]


def weighted_apply(center, w, cells):
    here, south, north, east, west = cells
    return center * here - ((w[0] * south + w[1] * north) + (w[2] * east + w[3] * west))


def apply_tiles(ref, w_ref, center_ref, r, parts):
    cells = beside_all(ref, r, parts)
    at = pl.ds(r, SUB)
    out = {}
    for j in cells[0]:
        w = [w_ref[k, j, at, :] for k in range(4)]
        out[j] = weighted_apply(center_ref[j, at, :], w, [c[j] for c in cells])
    return out, cells[0]


def first_vector(f_ref, c_ref, v1_ref, w_ref, faces_ref, center_ref, r, which):
    at = pl.ds(r, SUB)
    cond = beside(c_ref, r, which)
    cells = beside(f_ref, r, which)
    out = []
    for j in which:
        c = cond[0][j]
        inside = jnp.minimum(c, 1.0)
        face = inside * FACE
        w = [face * (c + cond[k][j]) for k in (1, 2, 3, 4)]
        faces = (w[0] + w[1]) + (w[2] + w[3])
        center = inside * (discount_rate * SCALE) + faces
        out += [(w_ref.at[k], j, at, w[k]) for k in range(4)]
        out.append((faces_ref, j, at, faces))
        out.append((center_ref, j, at, center))
        out.append((v1_ref, j, at, weighted_apply(center, w, [x[j] for x in cells])))
    return out


def clear_pads(refs, which):
    zero = jnp.zeros((SUB, LANES), jnp.float32)
    for ref in refs:
        rows = ref.shape[1]
        for j in which:
            ref[j, 0:SUB] = zero
            ref[j, rows - SUB : rows] = zero


def row_tiles(ref):
    return (ref.shape[1] - 2 * SUB) // SUB


def sweep(start, stop, step, unroll=2):
    def group(rows):
        stores = [store for r in rows for store in step(r)]
        for ref, j, at, value in stores:
            ref[j, at, :] = value

    def some(t, _):
        base = start + t * unroll
        group([pl.multiple_of(SUB + (base + u) * SUB, SUB) for u in range(unroll)])
        return 0

    whole = (stop - start) // unroll
    lax.fori_loop(0, whole, some, 0)
    rest = range(start + whole * unroll, stop)
    if len(rest):
        group([SUB + t * SUB for t in rest])


def second_vector(v1_ref, v2_ref, w_ref, center_ref, parts, unroll=34, start=0, stop=None):
    def step(r):
        out, _here = apply_tiles(v1_ref, w_ref, center_ref, r, parts)
        return [(v2_ref, j, pl.ds(r, SUB), x) for j, x in out.items()]

    sweep(start, row_tiles(v1_ref) if stop is None else stop, step, unroll)


def no_sums():
    return (jnp.zeros((SUB, LANES), jnp.float32),) * (2 * len(PAIRS))


def own_products(v0_ref, v1_ref, v2_ref, w_ref, center_ref, sums, most=16):
    own = list(range(v0_ref.shape[0] - 1))
    lane = lanes()
    unroll = even_share(row_tiles(v0_ref) - 2, most)

    def step(t, sums):
        groups = []
        for u in range(unroll):
            r = pl.multiple_of(PAD + (t * unroll + u) * SUB, SUB)
            out, here = apply_tiles(v2_ref, w_ref, center_ref, r, [own])
            at = pl.ds(r, SUB)
            for j in own:
                vs = [v0_ref[j, at, :], v1_ref[j, at, :], here[j]]
                if j == 0:
                    vs = [jnp.where(lane >= DEEP, v, 0.0) for v in vs]
                if j == own[-1]:
                    vs = [jnp.where(lane < LANES - DEEP, v, 0.0) for v in vs]
                groups.append((*vs, out[j]))
        for k in range(0, len(groups), CHAIN):
            sums = dot_step(groups[k : k + CHAIN], sums)
        return sums

    return lax.fori_loop(0, (row_tiles(v0_ref) - 2) // unroll, step, sums)


def margin_products(v0_ref, v1_ref, v2_ref, w_ref, center_ref, sums):
    margin = v0_ref.shape[0] - 1
    lane = lanes()
    span = FIRST + DEEP - (EDGE - DEEP)
    runs = (FIRST - EDGE + DEEP) // DEEP
    block = span + (runs - 1) * DEEP
    slots = [block * b + DEEP * k for b in range(LANES // block) for k in range(runs)]
    tiles = row_tiles(v0_ref) - 2
    groups = []
    for start in range(0, tiles, len(slots)):
        packed = None
        for t, slot in zip(range(start, tiles), slots):
            at = slice(PAD + t * SUB, PAD + (t + 1) * SUB)
            out, here = apply_tiles(v2_ref, w_ref, center_ref, PAD + t * SUB, [[margin]])
            vs = [v0_ref[margin, at], v1_ref[margin, at], here[margin], out[margin]]
            put = (slot - (EDGE - DEEP)) % LANES
            vs = [pltpu.roll(v, put, 1) if put else v for v in vs]
            low, high = slot, slot + span - DEEP
            mask = ((lane >= low) & (lane < low + DEEP)) | ((lane >= high) & (lane < high + DEEP))
            if packed is None:
                packed = [jnp.where(mask, v, 0.0) for v in vs]
            else:
                packed = [jnp.where(mask, v, x) for v, x in zip(vs, packed)]
        groups.append(tuple(packed))
    return dot_step(groups, sums)


def with_sides(tile, side, j, count):
    lane = lanes()
    if j == 0:
        tile = jnp.where(lane < DEEP, pltpu.roll(side, LANES - FIRST, 1), tile)
    if j == count - 1:
        tile = jnp.where(lane >= LANES - DEEP, pltpu.roll(side, LANES - EDGE, 1), tile)
    return tile


def repeat_sides(ref, t):
    count = ref.shape[0] - 1
    lane = lanes()
    at = slice((t + 1) * SUB, (t + 2) * SUB)
    last = pltpu.roll(ref[count - 1, at], EDGE, 1)
    first = pltpu.roll(ref[0, at], FIRST, 1)
    keep = (lane >= FIRST) & (lane < FIRST + EDGE)
    ref[count, at] = jnp.where(lane < EDGE, last, jnp.where(keep, first, 0.0))


def inner_first_kernel(f_in, c_in, p_in,
                       f_ref, c_ref, p_ref, v1_ref, v2_ref, w_ref, faces_ref, center_ref):
    own = list(range(f_ref.shape[0] - 1))
    rows = f_in.shape[0]
    tiles = row_tiles(f_ref)
    clear_pads((f_ref, c_ref, p_ref, v1_ref, v2_ref), own)
    for ref, source in ((f_ref, f_in), (c_ref, c_in), (p_ref, p_in)):
        for j in own:
            ref[j, PAD : PAD + rows] = source[:, tile_cols(j)]
        for t in range(1, tiles - 1):
            repeat_sides(ref, t)
    sweep(2, tiles - 2,
          lambda r: first_vector(f_ref, c_ref, v1_ref, w_ref, faces_ref, center_ref, r, own), 15)
    second_vector(v1_ref, v2_ref, w_ref, center_ref, [own], 14, 3, tiles - 3)


def inner_rest_kernel(after, near_ref, far_ref, f_in, c_in, p_in, v1_in, v2_in, w_in, faces_in, center_in,
                      f_ref, c_ref, p_ref, v1_ref, v2_ref, w_ref, faces_ref, center_ref, sums_ref):
    own = list(range(f_ref.shape[0] - 1))
    rows = f_ref.shape[1]
    tiles = row_tiles(f_ref)
    for field, ref in enumerate((f_ref, c_ref, p_ref)):
        for j in own:
            ref[j, SUB : 2 * SUB] = halo_tile((near_ref, far_ref), field, j, False)
            ref[j, rows - 2 * SUB : rows - SUB] = halo_tile((near_ref, far_ref), field, j, True)
        repeat_sides(ref, 0)
        repeat_sides(ref, tiles - 1)
    for start in (0, tiles - 2):
        sweep(start, start + 2,
              lambda r: first_vector(f_ref, c_ref, v1_ref, w_ref, faces_ref, center_ref, r, own))
    for start in (0, tiles - 3):
        second_vector(v1_ref, v2_ref, w_ref, center_ref, [own], 3, start, start + 3)
    sums = own_products(f_ref, v1_ref, v2_ref, w_ref, center_ref, no_sums())
    for k, a in enumerate(sums):
        sums_ref[k] = a


def margin_kernel(near_ref, far_ref, sums_in, f_in, c_in, p_in, v1_in, v2_in, w_in, faces_in, center_in,
                  f_ref, c_ref, p_ref, v1_ref, v2_ref, w_ref, faces_ref, center_ref, row_ref):
    count = f_ref.shape[0] - 1
    tiles = row_tiles(f_ref)
    per, groups = packing(tiles)
    lane = lanes()
    has_west, has_east = neighbours_along("col")
    even = is_even("col")
    from_east = lax.rem(lane, 2 * WIDE) < WIDE
    halo = (lane >= EDGE) & (lane < FIRST)
    clear_pads((f_ref, c_ref, p_ref, v1_ref, v2_ref), [count])
    for field, ref in enumerate((f_ref, c_ref, p_ref)):
        for v in range(groups):
            src = slice((field * groups + v) * SUB, (field * groups + v + 1) * SUB)
            near, far = near_ref[src], far_ref[src]
            east = jnp.where(has_east, jnp.where(even, near, far), 0.0)
            west = jnp.where(has_west, jnp.where(even, far, near), 0.0)
            both = jnp.where(from_east, east, west)
            for g in range(min(per, tiles - v * per)):
                t = v * per + g
                at = slice(SUB + t * SUB, 2 * SUB + t * SUB)
                ref[count, at] = jnp.where(halo, pltpu.roll(both, (EDGE - 2 * WIDE * g) % LANES, 1), ref[count, at])
    sweep(0, tiles, lambda r: first_vector(
        f_ref, c_ref, v1_ref, w_ref, faces_ref, center_ref, r, [count]), 34)
    second_vector(v1_ref, v2_ref, w_ref, center_ref, [[count]], 34)
    sums = tuple(sums_in[k] for k in range(2 * len(PAIRS)))
    sums = margin_products(f_ref, v1_ref, v2_ref, w_ref, center_ref, sums)
    row_ref[...] = jnp.broadcast_to(pack_sums(sums)[None], row_ref.shape)


def density_kernel(rows_ref, f_ref, c_ref, p_ref, v1_ref, v2_ref, w_ref, faces_ref,
                   value_out, u1_ref, u2_ref, row_ref, vx_ref, center_ref, value_ref, sem):
    dots, _unused = gathered_sums(rows_ref)
    c0, c1, c2 = [jnp.broadcast_to(c, (SUB, LANES)) for c in galerkin(dots)]
    which = list(range(f_ref.shape[0]))
    own = which[:-1]
    parts = [own, which[-1:]]
    tiles = row_tiles(f_ref)
    clear_pads((vx_ref, u1_ref, u2_ref), which)

    def value(r):
        at = pl.ds(r, SUB)
        return [
            (vx_ref, j, at, (c0 * f_ref[j, at, :] + c1 * v1_ref[j, at, :]) + c2 * v2_ref[j, at, :])
            for j in which
        ]

    sweep(0, tiles, value, 34)

    def first(r):
        at = pl.ds(r, SUB)
        val = beside_all(vx_ref, r, parts)
        cells = beside_all(p_ref, r, parts)
        out = []
        for j in which:
            inside = jnp.minimum(c_ref[j, at, :], 1.0)
            slope_row = 0.5 * (val[1][j] - val[2][j])
            slope_col = 0.5 * (val[3][j] - val[4][j])
            congestion = (slope_row * slope_row + slope_col * slope_col) * (0.5 / diffusion)
            zeroth = (discount_rate + congestion) * SCALE
            center = inside * zeroth + faces_ref[j, at, :]
            w = [w_ref[k, j, at, :] for k in range(4)]
            out.append((center_ref, j, at, center))
            out.append((u1_ref, j, at, weighted_apply(center, w, [x[j] for x in cells])))
        return out

    sweep(0, tiles, first, 34)

    unroll = even_share(tiles - 2, 32)

    def outer(t, sums):
        cost, weight = [list(x) for x in sums]
        for u in range(unroll):
            at = pl.ds(pl.multiple_of(PAD + (unroll * t + u) * SUB, SUB), SUB)
            to = pl.ds(pl.multiple_of((unroll * t + u) * SUB, SUB), SUB)
            for j in own:
                v = with_sides(vx_ref[j, at, :], vx_ref[len(own), at, :], j, len(own))
                p = p_ref[j, at, :]
                value_ref[to, tile_cols(j)] = v
                cost[j] = cost[j] + p * (f_ref[j, at, :] - discount_rate * v)
                weight[j] = weight[j] + p
        return tuple(cost), tuple(weight)

    zeros = (jnp.zeros((SUB, LANES), jnp.float32),) * len(own)
    extra = [sum(x) for x in lax.fori_loop(0, (tiles - 2) // unroll, outer, (zeros, zeros))]
    copy = pltpu.make_async_copy(value_ref, value_out, sem)
    copy.start()
    second_vector(u1_ref, u2_ref, w_ref, center_ref, parts)
    sums = own_products(p_ref, u1_ref, u2_ref, w_ref, center_ref, no_sums())
    sums = margin_products(p_ref, u1_ref, u2_ref, w_ref, center_ref, sums)
    row_ref[...] = jnp.broadcast_to(pack_sums(sums, extra)[None], row_ref.shape)
    copy.wait()


def finish_kernel(rows_ref, p_ref, u1_ref, u2_ref, density_ref, ergodic_ref):
    dots, (cost, weight) = gathered_sums(rows_ref, 2)
    ergodic_ref[...] = cost / weight
    c0, c1, c2 = [jnp.broadcast_to(c, (SUB, LANES)) for c in galerkin(dots)]
    count = p_ref.shape[0] - 1

    tiles = density_ref.shape[0] // SUB
    unroll = even_share(tiles, 32)

    def some(t, _):
        for u in range(unroll):
            at = pl.ds(pl.multiple_of(PAD + (unroll * t + u) * SUB, SUB), SUB)
            to = pl.ds(pl.multiple_of((unroll * t + u) * SUB, SUB), SUB)
            made = [(c0 * p_ref[j, at, :] + c1 * u1_ref[j, at, :]) + c2 * u2_ref[j, at, :] for j in range(count + 1)]
            for j in range(count):
                density_ref[to, tile_cols(j)] = with_sides(made[j], made[count], j, count)
        return 0

    lax.fori_loop(0, tiles // unroll, some, 0)


def f32(*shape):
    return jax.ShapeDtypeStruct(shape, jnp.float32)


def exchange(near, far, axis):
    n = lax.axis_size(axis)
    assert n % 2 == 0
    near = lax.ppermute(near, axis, [(i, i ^ 1) for i in range(n)])
    far = lax.ppermute(far, axis, [(i, (((i + 1) % n ^ 1) - 1) % n) for i in range(n)])
    return near, far


def everyone(row):
    return lax.all_to_all(row, BOTH, 0, 0, tiled=True)


def body(*args):
    rows, cols = args[0].shape
    devices = lax.axis_size("row") * lax.axis_size("col")
    count = cols // LANES
    ext = f32(count + 1, rows + 2 * PAD, LANES)
    ext4 = f32(4, *ext.shape)
    everyones = f32(devices, 1, LANES)
    _per, groups = packing(rows // SUB + 2)
    small = pltpu.CompilerParams(vmem_limit_bytes=VMEM_BYTES)

    def call(kernel, ins, outs, scratch=(), to_hbm=0, **more):
        return pl.pallas_call(
            kernel,
            in_specs=[VM] * len(ins),
            out_specs=[pl.BlockSpec(memory_space=pltpu.HBM)] * to_hbm + [VM] * (len(outs) - to_hbm),
            out_shape=outs,
            scratch_shapes=scratch,
            compiler_params=small,
            **more,
        )(*ins)

    cost = lambda us: pl.CostEstimate(flops=0, bytes_accessed=int(us * 2e6), transcendentals=0)
    up, down = edge_rows(*args)
    even = is_even("row")
    near, far = exchange(jnp.where(even, down, up), jnp.where(even, up, down), "row")
    forcing, conduct = fields_of(*args[:3])
    prior = args[3]
    state = call(
        inner_first_kernel, (forcing, conduct, prior),
        [ext] * 5 + [ext4, ext, ext], cost_estimate=cost(1.5))
    packs = call(pack_columns_kernel, (*state[:3], near, far), [f32(3 * groups * SUB, LANES)] * 2)
    sides = exchange(*packs, "col")
    *state, sums = call(
        inner_rest_kernel, (packs[0], near, far, *state),
        [ext] * 5 + [ext4, ext, ext, f32(2 * len(PAIRS), SUB, LANES)],
        input_output_aliases={3 + k: k for k in range(8)}, cost_estimate=cost(4))
    f, c, p, v1, v2, w, faces, _center, row = call(
        margin_kernel, (*sides, sums, *state),
        [ext] * 5 + [ext4, ext, ext, everyones], input_output_aliases={3 + k: k for k in range(8)})
    vmem = lambda like: pltpu.VMEM(like.shape, jnp.float32)
    block = f32(rows, cols)
    value, u1, u2, row = call(
        density_kernel, (everyone(row), f, c, p, v1, v2, w, faces), [block, ext, ext, everyones],
        [vmem(ext), vmem(ext), vmem(block), pltpu.SemaphoreType.DMA], 1)
    density, ergodic = call(
        finish_kernel, (everyone(row), p, u1, u2), [block, f32(1, 1)])
    return value, density, ergodic[0, 0]


def solution(mesh):
    spec = P("row", "col")
    return jax.shard_map(body, mesh=mesh, in_specs=(spec,) * 4, out_specs=(spec, spec, P()), check_vma=False)
```
